32 devices in a mesh: slab: 4 (over y, x), box: 8 (over z, core).
Axes of the slice: x: 2, y: 2, z: 4, core: 2. Of those that a mesh axis runs over, the one named last changes fastest.
Arguments:
- sources: bfloat16 [4, 8, 512, 4096], P('slab', 'box'), may hold values from -6 to 6
- leaf_ops: bfloat16 [4, 8, 256, 4096], P('slab', 'box'), may hold values from -0.09375 to 0.09375
- edge_slot: int32 [4, 8, 256], P('slab', 'box'), may hold values from 0 to 255, each once within a row
- merge_ops: float32 [4, 8, 256, 256], P('slab', 'box'), may hold values from -0.25 to 0.25
- lift_ops: float32 [4, 8, 512, 256], P('slab', 'box'), may hold values from -0.375 to 0.375
- coupling: float32 [4, 512, 512], P('slab', 'box'), may hold values from -0.125 to 0.125
- inverse: float32 [4, 512, 512], P('slab', 'box'), may hold values from -0.25 to 0.25
- boundary: float32 [512, 512], P(None, 'box'), may hold values from -6 to 6
Outputs:
- interface_solution: float32 [4, 512, 512], P('slab', None, 'box')
The draws below stay inside these ranges and needn't reach their ends.
Inputs may be any that keep to these rules, and one draw needn't show every extreme that they name: Each row edge_slot[s, b] holds every number from 0 to 255 once.
All inputs are finite; a program needn't handle non-finite values.
Results may differ from the reference program's by a relative error of at most 0.0003.
Values sent between devices are 32-bit elements; how exact they have to be, the bound alone decides.
A program may use at most 64 MiB of HBM per device.

```python
import jax
import jax.numpy as jnp
from jax import lax

E = 256
P_SIZE = 4096
NI = 512
R = 512
SLABS = 4
BOXES = 8
LEVELS = 3


def level_of(key, shape, shards, smallest, top_value):
    factor_of, own = 1.0, jax.random.fold_in(key, 6)
    for dim, parts in shards:
        steps = jnp.exp(jax.random.uniform(jax.random.fold_in(own, dim), (parts,), jnp.float32, smallest / len(shards), top_value / len(shards)))
        factor_of = factor_of * jnp.repeat(steps, shape[dim] // parts).reshape([-1 if axis == dim else 1 for axis in range(len(shape))])
    return factor_of


def centred(own_key, dims, width, reach, shards=(), held_as=jnp.bfloat16):
    factor_of = level_of(own_key, dims, shards, -0.22, 0.18) if shards else 1.0
    result = jax.random.normal(own_key, dims, jnp.float32) * width * factor_of
    return jnp.minimum(jnp.maximum(result, -reach), reach).astype(held_as)


def setup_inputs(seed: int = 0) -> dict:
    key_list = jax.random.split(jax.random.key(seed), 9)
    return {
        "sources": centred(key_list[0], (SLABS, BOXES, R, P_SIZE), 1.0, 6.0, ((0, 4), (1, 8))),
        "leaf_ops": centred(key_list[1], (SLABS, BOXES, E, P_SIZE), P_SIZE ** -0.5, 0.09375, ((0, 4), (1, 8))),
        "edge_slot": jax.vmap(lambda own: jax.random.permutation(own, E))(jax.random.split(key_list[2], SLABS * BOXES)).reshape((SLABS, BOXES, E)).astype(jnp.int32),
        "merge_ops": centred(key_list[3], (SLABS, BOXES, E, E), (2 * E) ** -0.5, 0.25, ((0, 4), (1, 8)), jnp.float32),
        "lift_ops": centred(key_list[4], (SLABS, BOXES, NI, E), E ** -0.5, 0.375, ((0, 4), (1, 8)), jnp.float32),
        "coupling": centred(key_list[5], (SLABS, NI, NI), (4 * NI) ** -0.5, 0.125, ((0, 4), (1, 8)), jnp.float32),
        "inverse": centred(key_list[6], (SLABS, NI, NI), NI ** -0.5, 0.25, ((0, 4), (1, 8)), jnp.float32),
        "boundary": centred(key_list[7], (R, NI), 1.0, 6.0, ((1, 8),), jnp.float32),
    }


highest = lax.Precision.HIGHEST


def reorder(box_flux, slot_row):
    return jnp.take(box_flux, slot_row, axis=1)


def reference(sources, leaf_ops, edge_slot, merge_ops, lift_ops, coupling, inverse, boundary):
    previous = boundary
    outputs = []
    box_ids = jnp.arange(BOXES, dtype=jnp.int32)
    for slab_index in range(SLABS):
        box_flux = jnp.einsum("brp,bep->bre", sources[slab_index].astype(jnp.float32), leaf_ops[slab_index].astype(jnp.float32), precision=highest)
        current = jax.vmap(reorder)(box_flux, edge_slot[slab_index])
        for tree_level in range(LEVELS):
            bit_number = LEVELS - 1 - tree_level
            merged = jnp.einsum("bre,bfe->brf", current, merge_ops[slab_index], precision=highest)
            partner = jnp.bitwise_xor(box_ids, jnp.int32(2 ** bit_number))
            summed = merged + merged[partner]
            half_rows = summed.shape[1] // 2
            upper_half = jnp.bitwise_and(jnp.right_shift(box_ids, bit_number), 1)
            current = jnp.where((upper_half == 1)[:, None, None], summed[:, half_rows:], summed[:, :half_rows])
        lifted = jnp.einsum("bre,bie->bri", current, lift_ops[slab_index], precision=highest)
        slab_load = lifted.reshape(R, NI)
        corrected = slab_load - jnp.dot(previous, coupling[slab_index].T, precision=highest, preferred_element_type=jnp.float32)
        previous = jnp.dot(corrected, inverse[slab_index].T, precision=highest, preferred_element_type=jnp.float32)
        outputs.append(previous)
    return jnp.stack(outputs)
```

```python
import functools

import jax
import jax.numpy as jnp
from jax import lax
from jax.experimental import pallas as pl
from jax.experimental.pallas import tpu as pltpu
from jax.sharding import PartitionSpec as P

MESH = pl.DeviceIdType.MESH
contract_last = (((1,), (1,)), ((), ()))
DEPTH_CHUNKS = 2
CHAIN_CHUNKS = 4


def dot_t(a, b):
    return lax.dot_general(a, b, contract_last, preferred_element_type=jnp.float32)


def st_fold(rows):
    return max(1, 128 // rows)


def halves(x):
    hi = x.astype(jnp.bfloat16)
    return hi, (x - hi.astype(jnp.float32)).astype(jnp.bfloat16)


def dot3(x, w_hi, w_lo):
    hi, lo = halves(x)
    return dot_t(hi, w_hi) + (dot_t(hi, w_lo) + dot_t(lo, w_hi))


def kernel(
    n, n_slab, split_ahead,
    src, leaf, slot_in, merge, lift, coup, inv, bnd_in, out,
    sv, lv, mv, ltv, slot, bnd, full, split, lift_split, lsend, lrecv,
    bst, br, bv, pv, st, cz, ob, rb,
    loc, lev_s, lev_r, g_s, g_r, p_s, p_r, ch_s, ch_r, o_s, o_r, b_s, b_r,
):
    me, slab = lax.axis_index("box"), lax.axis_index("slab")
    chips = n // 2
    chip = me // 2
    core = me - 2 * chip
    mate = me + 1 - 2 * core
    rows, points = pv.shape
    width = points // n
    total, edges = lsend.shape
    depth = lv.shape[1]
    kd = depth // DEPTH_CHUNKS
    levels = n.bit_length() - 1
    is_first = slab == 0
    fold = st_fold(rows)
    part = width // fold

    def peer(level):
        mask = 2 ** (levels - 1 - level)
        return me + mask - 2 * mask * lax.rem(me // mask, 2)

    def block_of(position):
        block = 0
        for q in range(levels):
            bit = lax.rem(me // 2**q, 2)
            block = block + 2**q * (bit if (position >> q) & 1 else 1 - bit)
        return block

    def read(k, pairs):
        copies = [pltpu.make_async_copy(a, b, loc.at[k]) for a, b in pairs]
        for c in copies:
            c.start()

    def rows_of(who):
        return pl.ds(pl.multiple_of(who * rows, rows), rows)

    def shard_at(i, owner):
        return full.at[i, pl.ds(pl.multiple_of(owner * width, width), width), :]

    def src_part(which, k):
        return sv.at[pl.ds(which * total // 2, total // 2), pl.ds(k * kd, kd)]

    def leaf_part(k):
        return lv.at[:, pl.ds(k * kd, kd)]

    SLOT, MERGE, LIFT, OWN, BND, SRC = 0, 1, 2, 3, 5, 6
    LEAF = SRC + 2 * DEPTH_CHUNKS
    arrays = {SLOT: slot, MERGE: mv, LIFT: ltv, OWN: shard_at(0, me), OWN + 1: shard_at(1, me), BND: bnd}
    for k in range(DEPTH_CHUNKS):
        arrays[LEAF + k] = leaf_part(k)
        for which in range(2):
            arrays[SRC + which * DEPTH_CHUNKS + k] = src_part(which, k)

    def read_done(k):
        pltpu.make_async_copy(arrays[k], arrays[k], loc.at[k]).wait()

    barrier = pltpu.get_barrier_semaphore()
    for d in range(1, n):
        pl.semaphore_signal(
            barrier, inc=1, device_id={"box": lax.rem(me + d, n)}, device_id_type=MESH
        )
    for d in (1, n_slab - 1):
        pl.semaphore_signal(
            barrier, inc=1, device_id={"slab": lax.rem(slab + d, n_slab)}, device_id_type=MESH
        )

    pl.when(is_first)(lambda: read(BND, [(bnd_in, bnd)]))
    read(SLOT, [(slot_in, slot)])
    read(MERGE, [(merge, mv)])
    for which in range(2):
        for k in range(DEPTH_CHUNKS):
            cols = pl.ds(k * kd, kd)
            if which == 0:
                read(LEAF + k, [(leaf.at[:, cols], lv.at[:, cols])])
            read(SRC + which * DEPTH_CHUNKS + k, [
                (src.at[rows_of(block_of(p)), cols], sv.at[pl.ds(p * rows, rows), cols])
                for p in range(which * n // 2, (which + 1) * n // 2)
            ])
    read(LIFT, [(lift, ltv)])
    for i, m in enumerate((coup, inv)):
        read(OWN + i, [(m, shard_at(i, me))])

    pl.semaphore_wait(barrier, n + 1)

    def remote(a, b, s, r, to, axis="box"):
        return pltpu.make_async_remote_copy(
            src_ref=a, dst_ref=b, send_sem=s, recv_sem=r,
            device_id={axis: to}, device_id_type=MESH,
        )

    def line(direction, t, i):
        step = 1 if direction == 0 else -1
        owner = me - 2 * step * t
        ok_chip = chip - step * t
        to_chip = chip + step
        a = (coup, inv)[i] if t == 0 else shard_at(i, owner)
        ok = (ok_chip >= 0) & (ok_chip < chips) & (to_chip >= 0) & (to_chip < chips)
        return ok, remote(
            a, shard_at(i, owner), g_s.at[i, ok_chip + direction], g_r.at[i, ok_chip], me + 2 * step
        )

    def arrival(direction, t, i):
        step = 1 if direction == 0 else -1
        ref = shard_at(i, me - 2 * step * (t + 1))
        return remote(
            ref, ref, g_s.at[i, chip], g_r.at[i, chip - step * (t + 1)], me - 2 * step
        )

    def came(direction, t):
        owner_chip = chip - (t + 1 if direction == 0 else -t - 1)
        return (owner_chip >= 0) & (owner_chip < chips)

    def share(direction, t, i):
        step = 1 if direction == 0 else -1
        owner = me - 2 * step * (t + 1)
        a = (coup, inv)[i] if t < 0 else shard_at(i, owner)
        return remote(a, shard_at(i, owner), p_s.at[i], p_r.at[i], mate)

    def half_of(i):
        return full.at[i, pl.ds(0, points // 2), :]

    def all_shares(i):
        return remote(half_of(i), half_of(i), p_s.at[i], p_r.at[i], mate)

    def launch(t, i):
        if t == 0:
            share(0, -1, i).start()
        for direction in range(2):
            ok, copy = line(direction, t, i)
            pl.when(ok)(copy.start)

    def take(t, i):
        for direction in range(2):
            pl.when(came(direction, t))(arrival(direction, t, i).wait_recv)
        if t + 1 < chips - 1:
            launch(t + 1, i)
        for direction in range(2):
            pl.when(came(direction, t))(share(direction, t, i).start)

    def all_here(i):
        all_shares(i).wait_recv()

    def all_sent(i):
        all_shares(i).wait_send()
        for t in range(chips - 1):
            for direction in range(2):
                ok, copy = line(direction, t, i)
                pl.when(ok)(copy.wait_send)

    def edge_block(d):
        to = lax.rem(me + d, n)
        return remote(bst.at[to], br.at[me], b_s.at[0], b_r.at[0], to)

    own_edge = pltpu.make_async_copy(bst.at[me], br.at[me], b_s.at[1])
    edge_rest = remote(bst.at[pl.ds(0, n - 1)], br.at[pl.ds(0, n - 1)], b_s.at[0], b_r.at[0], mate)

    launch(0, 1)
    launch(0, 0)

    @pl.when(is_first)
    def _():
        read_done(BND)
        for j in range(n):
            for q in range(fold):
                bst[j, :, q * rows : (q + 1) * rows] = bnd[
                    q * part : (q + 1) * part, j * rows : (j + 1) * rows
                ]
        own_edge.start()
        for d in range(1, n):
            edge_block(d).start()

    read_done(MERGE)
    read_done(SLOT)
    m_hi, m_lo = halves(mv[...])
    place = (
        lax.broadcasted_iota(jnp.int32, (edges, edges), 0) == slot[...]
    ).astype(jnp.float32).astype(jnp.bfloat16)
    first = (dot_t(m_hi, place).astype(jnp.bfloat16), dot_t(m_lo, place).astype(jnp.bfloat16))

    def flux(which):
        acc = None
        for k in range(DEPTH_CHUNKS):
            if which == 0:
                read_done(LEAF + k)
            read_done(SRC + which * DEPTH_CHUNKS + k)
            cols = slice(k * kd, (k + 1) * kd)
            part = dot_t(sv[which * total // 2 : (which + 1) * total // 2, cols], lv[:, cols])
            acc = part if acc is None else acc + part
        return acc

    offset = 0
    place_of = []
    for level in range(levels):
        half = total >> (level + 1)
        pieces = 2 if level < levels - 1 else 1
        place_of.append((offset, half // pieces, pieces))
        offset += half

    def give(level, y):
        start, size, pieces = place_of[level]
        lsend[start : start + size * pieces, :] = y
        copies = []
        for c in range(pieces):
            at = pl.ds(start + c * size, size)
            copy = remote(
                lsend.at[at, :], lrecv.at[at, :], lev_s.at[0], lev_r.at[level, c], peer(level)
            )
            copy.start()
            copies.append(copy)
        return copies

    def got(level, c):
        start, size, _ = place_of[level]
        return lrecv[start + c * size : start + (c + 1) * size, :]

    copies = give(0, dot3(flux(0), *first))
    keep = dot3(flux(1), *first)
    read_done(LIFT)
    lift_split[0], lift_split[1] = halves(ltv[...])
    for i in range(2):
        read_done(OWN + i)

    taken = 0
    for level in range(levels):
        size = place_of[level][1]
        if taken < chips - 1:
            take(taken, 1)
            take(taken, 0)
            taken += 1
        copies[0].wait_recv()
        x = keep[:size] + got(level, 0)
        if level < levels - 1:
            later = give(level + 1, dot3(x, m_hi, m_lo))
            copies[1].wait_recv()
            keep = dot3(keep[size:] + got(level, 1), m_hi, m_lo)
            copies = later
    load = dot3(x, lift_split[0], lift_split[1])

    for t in range(taken, chips - 1):
        take(t, 1)
        take(t, 0)

    block = min(points, 256)

    def prepare(i):
        if split_ahead:
            for r in range(0, points, block):
                hi, lo = halves(full[i, r : r + block, :])
                split[2 * i, r : r + block, :] = hi
                split[2 * i + 1, r : r + block, :] = lo

    all_here(1)
    prepare(1)

    all_here(0)
    prepare(0)

    def rows_at(i, r):
        if split_ahead:
            return split[2 * i, r : r + block, :], split[2 * i + 1, r : r + block, :]
        return halves(full[i, r : r + block, :])

    def times(x, i):
        if split_ahead:
            return dot3(x, split[2 * i], split[2 * i + 1])
        return jnp.concatenate(
            [dot3(x, *rows_at(i, r)) for r in range(0, points, block)], axis=1
        )

    @pl.when(is_first)
    def _():
        own_edge.wait()
        edge_rest.wait_recv()
        for j in range(n):
            for q in range(fold):
                at = j * width + q * part
                bv[at : at + part, :] = br[j, :, q * rows : (q + 1) * rows]
        pv[...] = bv[...].T

    chunks = max(1, min(CHAIN_CHUNKS, rows // 16))
    size = rows // chunks

    def hop(c):
        at = pl.ds(c * size, size)
        return remote(
            st.at[at, :], pv.at[at, :], ch_s.at[0], ch_r.at[c],
            lax.rem(slab + 1, n_slab), "slab",
        )

    all_hops = remote(st, pv, ch_s.at[0], ch_r.at[0], lax.rem(slab + 1, n_slab), "slab")
    for c in range(chunks):
        at = slice(c * size, (c + 1) * size)
        pl.when(slab > 0)(hop(c).wait_recv)
        cz[at, :] = load[at] - times(pv[at, :], 0)

        @pl.when(slab < n_slab - 1)
        def _():
            st[at, :] = times(cz[at, :], 1)
            hop(c).start()

    c_hi, c_lo = halves(cz[...])
    for r in range(0, points, block):
        w_hi, w_lo = rows_at(1, r)
        turned = dot_t(w_hi, c_hi) + (dot_t(w_hi, c_lo) + dot_t(w_lo, c_hi))
        for j in range(block // width):
            for q in range(fold):
                at = j * width + q * part
                ob[r // width + j, :, q * rows : (q + 1) * rows] = turned[at : at + part]

    own = pltpu.make_async_copy(ob.at[me], rb.at[me], o_s.at[1])
    own.start()
    for d in range(1, n):
        to = lax.rem(me + d, n)
        remote(ob.at[to], rb.at[me], o_s.at[0], o_r.at[0], to).start()

    exchanged = lsend.at[pl.ds(0, offset), :]
    remote(exchanged, exchanged, lev_s.at[0], lev_r.at[0, 0], mate).wait_send()
    all_sent(1)
    all_sent(0)
    pl.when(is_first)(edge_rest.wait_send)
    pl.when(slab < n_slab - 1)(all_hops.wait_send)
    own.wait()
    rest = remote(ob.at[pl.ds(0, n - 1)], rb.at[pl.ds(0, n - 1)], o_s.at[0], o_r.at[0], mate)
    rest.wait_recv()
    for j in range(n):
        for q in range(fold):
            out[q * part : (q + 1) * part, j * rows : (j + 1) * rows] = rb[
                j, :, q * rows : (q + 1) * rows
            ]
    rest.wait_send()


def on_device(sources, leaf_ops, edge_slot, merge_ops, lift_ops, coupling, inverse, boundary):
    n, n_slab = lax.axis_size("box"), lax.axis_size("slab")
    total, depth = sources.shape[2:]
    edges = leaf_ops.shape[2]
    points = lift_ops.shape[2]
    rows, width = total // n, points // n
    chips, levels = n // 2, n.bit_length() - 1
    split_ahead = points * points <= 2**20
    f32, bf16 = jnp.float32, jnp.bfloat16
    hbm = pl.BlockSpec(memory_space=pl.ANY)
    dma = lambda *s: pltpu.SemaphoreType.DMA(s)
    vmem = pl.BlockSpec(memory_space=pltpu.VMEM)
    fold = st_fold(rows)
    result = pl.pallas_call(
        functools.partial(kernel, n, n_slab, split_ahead),
        out_shape=pltpu.VMEM((width, total), f32),
        in_specs=[hbm] * 8,
        out_specs=vmem,
        scratch_shapes=[
            pltpu.VMEM((total, depth), bf16),
            pltpu.VMEM((edges, depth), bf16),
            pltpu.VMEM((edges, edges), f32),
            pltpu.VMEM((points, edges), f32),
            pltpu.VMEM((1, edges), jnp.int32),
            pltpu.VMEM((width, total), f32),
            pltpu.VMEM((2, points, points), f32),
            pltpu.VMEM((4, points, points) if split_ahead else (4, 16, 128), bf16),
            pltpu.VMEM((2, points, edges), bf16),
            pltpu.VMEM((total, edges), f32),
            pltpu.VMEM((total, edges), f32),
            pltpu.VMEM((n, width // fold, rows * fold), f32),
            pltpu.VMEM((n, width // fold, rows * fold), f32),
            pltpu.VMEM((points, rows), f32),
            pltpu.VMEM((rows, points), f32),
            pltpu.VMEM((rows, points), f32),
            pltpu.VMEM((rows, points), f32),
            pltpu.VMEM((n, width // fold, rows * fold), f32),
            pltpu.VMEM((n, width // fold, rows * fold), f32),
            dma(3 * DEPTH_CHUNKS + 6),
            dma(1), dma(levels, 2),
            dma(2, chips + 1), dma(2, chips),
            dma(2), dma(2),
            dma(1), dma(CHAIN_CHUNKS),
            dma(2), dma(1), dma(2), dma(1),
        ],
        compiler_params=pltpu.CompilerParams(collective_id=0, has_side_effects=True),
        name="slab_solve",
    )(
        sources[0, 0], leaf_ops[0, 0], edge_slot[0], merge_ops[0, 0], lift_ops[0, 0],
        coupling[0], inverse[0], boundary.T,
    )
    return result.T[None]


def solution(mesh):
    return jax.shard_map(
        on_device,
        mesh=mesh,
        in_specs=(
            P("slab", "box", None, None),
            P("slab", "box", None, None),
            P("slab", "box", None),
            P("slab", "box", None, None),
            P("slab", "box", None, None),
            P("slab", "box", None),
            P("slab", "box", None),
            P(None, "box"),
        ),
        out_specs=P("slab", None, "box"),
        check_vma=False,
    )
```

```python
import functools

import jax
import jax.numpy as jnp
from jax import lax
from jax.experimental import pallas as pl
from jax.experimental.pallas import tpu as pltpu
from jax.sharding import PartitionSpec as P

MESH = pl.DeviceIdType.MESH
contract_last = (((1,), (1,)), ((), ()))
DEPTH_CHUNKS = 2
CHAIN_CHUNKS = 4
HELPERS = 2
COUP, INV, LENT = 0, 1, 2


def dot_t(a, b):
    return lax.dot_general(a, b, contract_last, preferred_element_type=jnp.float32)


def st_fold(rows):
    return max(1, 128 // rows)


def halves(x):
    hi = x.astype(jnp.bfloat16)
    return hi, (x - hi.astype(jnp.float32)).astype(jnp.bfloat16)


def product3(a_hi, a_lo, b_hi, b_lo):
    mm = functools.partial(jnp.dot, preferred_element_type=jnp.float32)
    return mm(a_hi, b_hi) + (mm(a_hi, b_lo) + mm(a_lo, b_hi))


def dot3(x, w_hi, w_lo):
    hi, lo = halves(x)
    return dot_t(hi, w_hi) + (dot_t(hi, w_lo) + dot_t(lo, w_hi))


def kernel(
    n, n_slab, split_ahead,
    src, leaf, slot_in, merge, lift, coup, inv, bnd_in, out,
    sv, lv, mv, ltv, slot, bnd, full, lent, split, lift_split, lsend, lrecv,
    bst, br, bv, dst, dv, pv, st, cz, ob, rb,
    loc, lev_s, lev_r, g_s, g_r, p_s, p_r, ch_s, ch_r, o_s, o_r, b_s, b_r, x_s, x_r,
):
    me, slab = lax.axis_index("box"), lax.axis_index("slab")
    chips = n // 2
    chip = me // 2
    core = me - 2 * chip
    mate = me + 1 - 2 * core
    rows, points = pv.shape
    width = points // n
    total, edges = lsend.shape
    depth = lv.shape[1]
    kd = depth // DEPTH_CHUNKS
    levels = n.bit_length() - 1
    block = min(points, 256)
    depth_lent = lent.shape[1]
    helpers = points // depth_lent
    helping = n // helpers
    helper0 = n_slab - helpers
    is_helper = slab >= helper0
    is_sender = is_helper & (me // helping == slab - helper0)
    is_first = slab == 0
    is_later = slab > 0
    fold = st_fold(rows)
    part = width // fold

    def flip(mask):
        to = me
        for q in range(levels):
            if (mask >> q) & 1:
                to = to + 2**q - 2 ** (q + 1) * lax.rem(me // 2**q, 2)
        return to

    def peer(level):
        mask = 2 ** (levels - 1 - level)
        return me + mask - 2 * mask * lax.rem(me // mask, 2)

    def block_of(position):
        block = 0
        for q in range(levels):
            bit = lax.rem(me // 2**q, 2)
            block = block + 2**q * (bit if (position >> q) & 1 else 1 - bit)
        return block

    def read(k, pairs):
        copies = [pltpu.make_async_copy(a, b, loc.at[k]) for a, b in pairs]
        for c in copies:
            c.start()

    def rows_of(who):
        return pl.ds(pl.multiple_of(who * rows, rows), rows)

    def points_at(i, at):
        return lent.at[at, :] if i == LENT else full.at[i, at, :]

    def shard_at(i, owner):
        return points_at(i, pl.ds(pl.multiple_of(owner * width, width), width))

    def own_shard(i):
        return shard_at(LENT, me) if i == LENT else (coup, inv)[i]

    def src_part(which, k):
        return sv.at[pl.ds(which * total // 2, total // 2), pl.ds(k * kd, kd)]

    def leaf_part(k):
        return lv.at[:, pl.ds(k * kd, kd)]

    SLOT, MERGE, LIFT, OWN, BND, SRC = 0, 1, 2, 3, 5, 6
    LEAF = SRC + 2 * DEPTH_CHUNKS
    arrays = {SLOT: slot, MERGE: mv, LIFT: ltv, OWN: shard_at(0, me), OWN + 1: shard_at(1, me), BND: bnd}
    for k in range(DEPTH_CHUNKS):
        arrays[LEAF + k] = leaf_part(k)
        for which in range(2):
            arrays[SRC + which * DEPTH_CHUNKS + k] = src_part(which, k)

    def read_done(k):
        pltpu.make_async_copy(arrays[k], arrays[k], loc.at[k]).wait()

    barrier = pltpu.get_barrier_semaphore()
    for d in range(1, n):
        pl.semaphore_signal(
            barrier, inc=1, device_id={"box": lax.rem(me + d, n)}, device_id_type=MESH
        )
    for d in range(1, n_slab):
        pl.semaphore_signal(
            barrier, inc=1, device_id={"slab": lax.rem(slab + d, n_slab)}, device_id_type=MESH
        )

    pl.when(is_sender)(lambda: read(BND, [(bnd_in, bnd)]))
    read(SLOT, [(slot_in, slot)])
    read(MERGE, [(merge, mv)])
    for which in range(2):
        for k in range(DEPTH_CHUNKS):
            cols = pl.ds(k * kd, kd)
            if which == 0:
                read(LEAF + k, [(leaf.at[:, cols], lv.at[:, cols])])
            read(SRC + which * DEPTH_CHUNKS + k, [
                (src.at[rows_of(block_of(p)), cols], sv.at[pl.ds(p * rows, rows), cols])
                for p in range(which * n // 2, (which + 1) * n // 2)
            ])
    read(LIFT, [(lift, ltv)])
    for i, m in enumerate((coup, inv)):
        read(OWN + i, [(m, shard_at(i, me))])

    pl.semaphore_wait(barrier, n + n_slab - 2)

    def remote(a, b, s, r, to, axis="box"):
        return pltpu.make_async_remote_copy(
            src_ref=a, dst_ref=b, send_sem=s, recv_sem=r,
            device_id={axis: to}, device_id_type=MESH,
        )

    def line(direction, t, i):
        step = 1 if direction == 0 else -1
        owner = me - 2 * step * t
        ok_chip = chip - step * t
        to_chip = chip + step
        a = own_shard(i) if t == 0 else shard_at(i, owner)
        ok = (ok_chip >= 0) & (ok_chip < chips) & (to_chip >= 0) & (to_chip < chips)
        return ok, remote(
            a, shard_at(i, owner), g_s.at[i, ok_chip + direction], g_r.at[i, ok_chip], me + 2 * step
        )

    def arrival(direction, t, i):
        step = 1 if direction == 0 else -1
        ref = shard_at(i, me - 2 * step * (t + 1))
        return remote(
            ref, ref, g_s.at[i, chip], g_r.at[i, chip - step * (t + 1)], me - 2 * step
        )

    def came(direction, t):
        owner_chip = chip - (t + 1 if direction == 0 else -t - 1)
        return (owner_chip >= 0) & (owner_chip < chips)

    def share(direction, t, i):
        step = 1 if direction == 0 else -1
        owner = me - 2 * step * (t + 1)
        a = own_shard(i) if t < 0 else shard_at(i, owner)
        return remote(a, shard_at(i, owner), p_s.at[i], p_r.at[i], mate)

    def all_shares(i):
        half = points_at(i, pl.ds(0, points // 2))
        return remote(half, half, p_s.at[i], p_r.at[i], mate)

    def launch(t, i):
        if t == 0:
            share(0, -1, i).start()
        for direction in range(2):
            ok, copy = line(direction, t, i)
            pl.when(ok)(copy.start)

    def take(t, i):
        for direction in range(2):
            pl.when(came(direction, t))(arrival(direction, t, i).wait_recv)
        if t + 1 < chips - 1:
            launch(t + 1, i)
        for direction in range(2):
            pl.when(came(direction, t))(share(direction, t, i).start)

    def all_here(i):
        all_shares(i).wait_recv()

    def all_sent(i):
        all_shares(i).wait_send()
        for t in range(chips - 1):
            for direction in range(2):
                ok, copy = line(direction, t, i)
                pl.when(ok)(copy.wait_send)

    def lend(h):
        return remote(
            coup.at[:, h * depth_lent : (h + 1) * depth_lent], shard_at(LENT, me),
            x_s.at[0], x_r.at[0], helper0 + h, "slab",
        )

    def lend_all():
        return remote(coup, shard_at(COUP, me), x_s.at[0], x_r.at[0], helper0, "slab")

    def answer(h):
        return remote(dst, dv.at[h], x_s.at[1], x_r.at[1 + h], 0, "slab")

    edge_at = lax.rem(me, helping)

    def edge_block(d):
        to = lax.rem(me + d, n)
        return remote(bst.at[to], br.at[edge_at], b_s.at[0], b_r.at[0], to)

    own_edge = pltpu.make_async_copy(bst.at[me], br.at[edge_at], b_s.at[1])

    def edge_blocks(count):
        blocks = bst.at[pl.ds(0, count)]
        return remote(blocks, blocks, b_s.at[0], b_r.at[0], mate)

    @pl.when(is_first)
    def _():
        for h in range(helpers):
            lend(h).start()

    launch(0, INV)
    pl.when(is_later & ~is_helper)(lambda: launch(0, COUP))

    @pl.when(is_sender)
    def _():
        read_done(BND)
        for j in range(n):
            for q in range(fold):
                bst[j, :, q * rows : (q + 1) * rows] = bnd[
                    q * part : (q + 1) * part, j * rows : (j + 1) * rows
                ]
        own_edge.start()
        for d in range(1, n):
            edge_block(d).start()

    read_done(MERGE)
    read_done(SLOT)
    m_hi, m_lo = halves(mv[...])
    place = (
        lax.broadcasted_iota(jnp.int32, (edges, edges), 0) == slot[...]
    ).astype(jnp.float32).astype(jnp.bfloat16)
    first = (dot_t(m_hi, place).astype(jnp.bfloat16), dot_t(m_lo, place).astype(jnp.bfloat16))

    def flux(which):
        acc = None
        for k in range(DEPTH_CHUNKS):
            if which == 0:
                read_done(LEAF + k)
            read_done(SRC + which * DEPTH_CHUNKS + k)
            cols = slice(k * kd, (k + 1) * kd)
            part = dot_t(sv[which * total // 2 : (which + 1) * total // 2, cols], lv[:, cols])
            acc = part if acc is None else acc + part
        return acc

    offset = 0
    place_of = []
    for level in range(levels):
        half = total >> (level + 1)
        pieces = 2 if level < levels - 1 else 1
        place_of.append((offset, half // pieces, pieces))
        offset += half

    def give(level, y):
        start, size, pieces = place_of[level]
        lsend[start : start + size * pieces, :] = y
        copies = []
        for c in range(pieces):
            at = pl.ds(start + c * size, size)
            copy = remote(
                lsend.at[at, :], lrecv.at[at, :], lev_s.at[0], lev_r.at[level, c], peer(level)
            )
            copy.start()
            copies.append(copy)
        return copies

    def got(level, c):
        start, size, _ = place_of[level]
        return lrecv[start + c * size : start + (c + 1) * size, :]

    copies = give(0, dot3(flux(0), *first))
    keep = dot3(flux(1), *first)
    read_done(LIFT)
    lift_split[0], lift_split[1] = halves(ltv[...])
    for i in range(2):
        read_done(OWN + i)

    @pl.when(is_helper)
    def _():
        lend(0).wait_recv()
        launch(0, LENT)
        for t in range(chips - 1):
            take(t, LENT)
        launch(0, COUP)

        @pl.when(is_sender)
        def _():
            own_edge.wait()
            edge_blocks(helping - 1).wait_recv()

        @pl.when(~is_sender)
        def _():
            edge_blocks(helping).wait_recv()

        for j in range(helping):
            for q in range(fold):
                at = j * width + q * part
                bv[at : at + part, :] = br[j, :, q * rows : (q + 1) * rows]
        edge = bv[...].T
        all_shares(LENT).wait_recv()
        for r in range(0, points, block):
            dst[:, r : r + block] = dot3(edge, *halves(lent[r : r + block, :]))
        answer(slab - helper0).start()

    taken = 0
    for level in range(levels):
        size = place_of[level][1]
        if taken < chips - 1:
            take(taken, INV)
            pl.when(is_later & ~is_helper)(lambda: take(taken, COUP))
            if taken > 0:
                pl.when(is_helper)(lambda: take(taken - 1, COUP))
            taken += 1
        copies[0].wait_recv()
        x = keep[:size] + got(level, 0)
        if level < levels - 1:
            later = give(level + 1, dot3(x, m_hi, m_lo))
            copies[1].wait_recv()
            keep = dot3(keep[size:] + got(level, 1), m_hi, m_lo)
            copies = later
    load = dot3(x, lift_split[0], lift_split[1])

    for t in range(taken, chips - 1):
        take(t, INV)
        pl.when(is_later & ~is_helper)(lambda: take(t, COUP))
        pl.when(is_helper)(lambda: take(t - 1, COUP))
    pl.when(is_helper)(lambda: take(chips - 2, COUP))

    def prepare(i):
        for r in range(0, points, block):
            hi, lo = halves(full[i, r : r + block, :])
            split[2 * i, r : r + block, :] = hi
            split[2 * i + 1, r : r + block, :] = lo

    def times(x, i):
        if split_ahead:
            return dot3(x, split[2 * i], split[2 * i + 1])
        return jnp.concatenate(
            [dot3(x, *halves(full[i, r : r + block, :])) for r in range(0, points, block)], axis=1
        )

    all_shares(INV).wait_recv()
    if split_ahead:
        prepare(INV)

    @pl.when(is_first)
    def _():
        rest = load
        for h in range(helpers):
            answer(h).wait_recv()
            rest = rest - dv[h]
        cz[...] = rest

    @pl.when(is_later)
    def _():
        cz[...] = times(load, INV) if split_ahead else load
        all_shares(COUP).wait_recv()
        if split_ahead:
            prepare(COUP)
            for r in range(0, points, block):
                at = slice(r, r + block)
                joint = product3(
                    split[2 * INV, at, :], split[2 * INV + 1, at, :],
                    split[2 * COUP], split[2 * COUP + 1],
                )
                split[4, at, :], split[5, at, :] = halves(joint)

    chunks = max(1, min(CHAIN_CHUNKS, rows // 16))
    size = rows // chunks

    def hop(c):
        at = pl.ds(c * size, size)
        return remote(
            st.at[at, :], pv.at[at, :], ch_s.at[0], ch_r.at[c],
            lax.rem(slab + 1, n_slab), "slab",
        )

    all_hops = remote(st, pv, ch_s.at[0], ch_r.at[0], lax.rem(slab + 1, n_slab), "slab")
    for c in range(chunks):
        at = slice(c * size, (c + 1) * size)

        @pl.when(is_first)
        def _():
            st[at, :] = times(cz[at, :], INV)

        @pl.when(is_later)
        def _():
            hop(c).wait_recv()
            if split_ahead:
                st[at, :] = cz[at, :] - times(pv[at, :], 2)
            else:
                st[at, :] = times(cz[at, :] - times(pv[at, :], COUP), INV)

        pl.when(slab < n_slab - 1)(hop(c).start)

    turned = st[...].T
    for j in range(n):
        for q in range(fold):
            at = j * width + q * part
            ob[j, :, q * rows : (q + 1) * rows] = turned[at : at + part]
    own = pltpu.make_async_copy(ob.at[me], rb.at[me], o_s.at[1])
    for mask in [m ^ 1 for m in range(n - 1, 1, -1)] + [1]:
        to = flip(mask)
        remote(ob.at[to], rb.at[me], o_s.at[0], o_r.at[0], to).start()
    own.start()

    exchanged = lsend.at[pl.ds(0, offset), :]
    remote(exchanged, exchanged, lev_s.at[0], lev_r.at[0, 0], mate).wait_send()
    all_sent(INV)
    pl.when(is_later)(lambda: all_sent(COUP))
    pl.when(is_first)(lambda: lend_all().wait_send())

    @pl.when(is_helper)
    def _():
        all_sent(LENT)
        answer(0).wait_send()

    pl.when(is_sender)(lambda: edge_blocks(n - 1).wait_send())
    pl.when(slab < n_slab - 1)(all_hops.wait_send)
    own.wait()
    rest = remote(ob.at[pl.ds(0, n - 1)], rb.at[pl.ds(0, n - 1)], o_s.at[0], o_r.at[0], mate)
    rest.wait_recv()
    for j in range(n):
        for q in range(fold):
            out[q * part : (q + 1) * part, j * rows : (j + 1) * rows] = rb[
                j, :, q * rows : (q + 1) * rows
            ]
    rest.wait_send()


def on_device(sources, leaf_ops, edge_slot, merge_ops, lift_ops, coupling, inverse, boundary):
    n, n_slab = lax.axis_size("box"), lax.axis_size("slab")
    total, depth = sources.shape[2:]
    edges = leaf_ops.shape[2]
    points = lift_ops.shape[2]
    rows, width = total // n, points // n
    chips, levels = n // 2, n.bit_length() - 1
    split_ahead = points * points <= 2**20
    f32, bf16 = jnp.float32, jnp.bfloat16
    hbm = pl.BlockSpec(memory_space=pl.ANY)
    dma = lambda *s: pltpu.SemaphoreType.DMA(s)
    vmem = pl.BlockSpec(memory_space=pltpu.VMEM)
    fold = st_fold(rows)
    helpers = min(HELPERS, n_slab - 1)
    result = pl.pallas_call(
        functools.partial(kernel, n, n_slab, split_ahead),
        out_shape=pltpu.VMEM((width, total), f32),
        in_specs=[hbm] * 8,
        out_specs=vmem,
        scratch_shapes=[
            pltpu.VMEM((total, depth), bf16),
            pltpu.VMEM((edges, depth), bf16),
            pltpu.VMEM((edges, edges), f32),
            pltpu.VMEM((points, edges), f32),
            pltpu.VMEM((1, edges), jnp.int32),
            pltpu.VMEM((width, total), f32),
            pltpu.VMEM((2, points, points), f32),
            pltpu.VMEM((points, points // helpers), f32),
            pltpu.VMEM((6, points, points) if split_ahead else (6, 16, 128), bf16),
            pltpu.VMEM((2, points, edges), bf16),
            pltpu.VMEM((total, edges), f32),
            pltpu.VMEM((total, edges), f32),
            pltpu.VMEM((n, width // fold, rows * fold), f32),
            pltpu.VMEM((n // helpers, width // fold, rows * fold), f32),
            pltpu.VMEM((points // helpers, rows), f32),
            pltpu.VMEM((rows, points), f32),
            pltpu.VMEM((helpers, rows, points), f32),
            pltpu.VMEM((rows, points), f32),
            pltpu.VMEM((rows, points), f32),
            pltpu.VMEM((rows, points), f32),
            pltpu.VMEM((n, width // fold, rows * fold), f32),
            pltpu.VMEM((n, width // fold, rows * fold), f32),
            dma(3 * DEPTH_CHUNKS + 6),
            dma(1), dma(levels, 2),
            dma(3, chips + 1), dma(3, chips),
            dma(3), dma(3),
            dma(1), dma(CHAIN_CHUNKS),
            dma(2), dma(1), dma(2), dma(1), dma(2), dma(1 + helpers),
        ],
        compiler_params=pltpu.CompilerParams(collective_id=0, has_side_effects=True),
        name="slab_solve",
    )(
        sources[0, 0], leaf_ops[0, 0], edge_slot[0], merge_ops[0, 0], lift_ops[0, 0],
        coupling[0], inverse[0], boundary.T,
    )
    return result.T[None]


def solution(mesh):
    return jax.shard_map(
        on_device,
        mesh=mesh,
        in_specs=(
            P("slab", "box", None, None),
            P("slab", "box", None, None),
            P("slab", "box", None),
            P("slab", "box", None, None),
            P("slab", "box", None, None),
            P("slab", "box", None),
            P("slab", "box", None),
            P(None, "box"),
        ),
        out_specs=P("slab", None, "box"),
        check_vma=False,
    )
```

```python
import functools

import jax
import jax.numpy as jnp
from jax import lax
from jax.experimental import pallas as pl
from jax.experimental.pallas import tpu as pltpu
from jax.sharding import PartitionSpec as P

MESH = pl.DeviceIdType.MESH
contract_last = (((1,), (1,)), ((), ()))
DEPTH_CHUNKS = 2
CHAIN_CHUNKS = 4
HELPERS = 2
KEPT = 2
COUP, INV, LENT = 0, 1, 2


def dot_t(a, b):
    return lax.dot_general(a, b, contract_last, preferred_element_type=jnp.float32)


def st_fold(rows):
    return max(1, 128 // rows)


def halves(x):
    hi = x.astype(jnp.bfloat16)
    return hi, (x - hi.astype(jnp.float32)).astype(jnp.bfloat16)


def product3(a_hi, a_lo, b_hi, b_lo):
    mm = functools.partial(jnp.dot, preferred_element_type=jnp.float32)
    return mm(a_hi, b_hi) + (mm(a_hi, b_lo) + mm(a_lo, b_hi))


def dot3(x, w_hi, w_lo):
    hi, lo = halves(x)
    return dot_t(hi, w_hi) + (dot_t(hi, w_lo) + dot_t(lo, w_hi))


def kernel(
    n, n_slab, split_ahead,
    src, leaf, slot_in, merge, lift, coup, inv, bnd_in, out,
    sv, lv, mv, ltv, slot, bnd, full, lent, split, lift_split, lsend, lrecv,
    bst, br, bv, dst, dv, pv, st, cz, ob, rb,
    loc, lev_s, lev_r, g_s, g_r, p_s, p_r, ch_s, ch_r, o_s, o_r, b_s, b_r, x_s, x_r,
):
    me, slab = lax.axis_index("box"), lax.axis_index("slab")
    chips = n // 2
    chip = me // 2
    core = me - 2 * chip
    mate = me + 1 - 2 * core
    rows, points = pv.shape
    width = points // n
    total, edges = lsend.shape
    depth = lv.shape[1]
    kd = depth // DEPTH_CHUNKS
    levels = n.bit_length() - 1
    block = min(points, 256)
    depth_lent = lent.shape[2]
    units = points // depth_lent
    helpers = units - KEPT
    helping = n // units
    helper0 = n_slab - helpers
    is_helper = slab >= helper0
    is_first = slab == 0
    edge_box = jnp.where(is_first, 0, (KEPT + slab - helper0) * helping)
    edge_count = jnp.where(is_first, KEPT, 1) * helping
    is_sender = (is_helper | is_first) & (me >= edge_box) & (me < edge_box + edge_count)
    is_later = slab > 0
    fold = st_fold(rows)
    part = width // fold

    def flip(mask):
        to = me
        for q in range(levels):
            if (mask >> q) & 1:
                to = to + 2**q - 2 ** (q + 1) * lax.rem(me // 2**q, 2)
        return to

    def peer(level):
        mask = 2 ** (levels - 1 - level)
        return me + mask - 2 * mask * lax.rem(me // mask, 2)

    def block_of(position):
        block = 0
        for q in range(levels):
            bit = lax.rem(me // 2**q, 2)
            block = block + 2**q * (bit if (position >> q) & 1 else 1 - bit)
        return block

    def read(k, pairs):
        copies = [pltpu.make_async_copy(a, b, loc.at[k]) for a, b in pairs]
        for c in copies:
            c.start()

    def rows_of(who):
        return pl.ds(pl.multiple_of(who * rows, rows), rows)

    def points_at(i, at):
        return lent.at[i - LENT, at, :] if i >= LENT else full.at[i, at, :]

    def shard_at(i, owner):
        return points_at(i, pl.ds(pl.multiple_of(owner * width, width), width))

    def src_part(which, k):
        return sv.at[pl.ds(which * total // 2, total // 2), pl.ds(k * kd, kd)]

    def leaf_part(k):
        return lv.at[:, pl.ds(k * kd, kd)]

    SLOT, MERGE, LIFT, OWN, BND, SRC = 0, 1, 2, 3, 5, 6
    LEAF = SRC + 2 * DEPTH_CHUNKS
    arrays = {SLOT: slot, MERGE: mv, LIFT: ltv, OWN: shard_at(0, me), OWN + 1: shard_at(1, me), BND: bnd}
    for k in range(DEPTH_CHUNKS):
        arrays[LEAF + k] = leaf_part(k)
        for which in range(2):
            arrays[SRC + which * DEPTH_CHUNKS + k] = src_part(which, k)

    def read_done(k):
        pltpu.make_async_copy(arrays[k], arrays[k], loc.at[k]).wait()

    barrier = pltpu.get_barrier_semaphore()
    for d in range(1, n):
        pl.semaphore_signal(
            barrier, inc=1, device_id={"box": lax.rem(me + d, n)}, device_id_type=MESH
        )
    for d in range(1, n_slab):
        pl.semaphore_signal(
            barrier, inc=1, device_id={"slab": lax.rem(slab + d, n_slab)}, device_id_type=MESH
        )

    pl.when(is_sender)(lambda: read(BND, [(bnd_in, bnd)]))
    read(SLOT, [(slot_in, slot)])
    read(MERGE, [(merge, mv)])
    for which in range(2):
        for k in range(DEPTH_CHUNKS):
            cols = pl.ds(k * kd, kd)
            if which == 0:
                read(LEAF + k, [(leaf.at[:, cols], lv.at[:, cols])])
            read(SRC + which * DEPTH_CHUNKS + k, [
                (src.at[rows_of(block_of(p)), cols], sv.at[pl.ds(p * rows, rows), cols])
                for p in range(which * n // 2, (which + 1) * n // 2)
            ])
    read(LIFT, [(lift, ltv)])
    for i, m in enumerate((coup, inv)):
        read(OWN + i, [(m, shard_at(i, me))])

    pl.semaphore_wait(barrier, n + n_slab - 2)

    def remote(a, b, s, r, to, axis="box"):
        return pltpu.make_async_remote_copy(
            src_ref=a, dst_ref=b, send_sem=s, recv_sem=r,
            device_id={axis: to}, device_id_type=MESH,
        )

    def line(direction, t, i):
        step = 1 if direction == 0 else -1
        owner = me - 2 * step * t
        ok_chip = chip - step * t
        to_chip = chip + step
        a = (coup, inv)[i] if t == 0 else shard_at(i, owner)
        ok = (ok_chip >= 0) & (ok_chip < chips) & (to_chip >= 0) & (to_chip < chips)
        return ok, remote(
            a, shard_at(i, owner), g_s.at[i, ok_chip + direction], g_r.at[i, ok_chip], me + 2 * step
        )

    def arrival(direction, t, i):
        step = 1 if direction == 0 else -1
        ref = shard_at(i, me - 2 * step * (t + 1))
        return remote(
            ref, ref, g_s.at[i, chip], g_r.at[i, chip - step * (t + 1)], me - 2 * step
        )

    def came(direction, t):
        owner_chip = chip - (t + 1 if direction == 0 else -t - 1)
        return (owner_chip >= 0) & (owner_chip < chips)

    def share(direction, t, i):
        step = 1 if direction == 0 else -1
        owner = me - 2 * step * (t + 1)
        a = (coup, inv)[i] if t < 0 else shard_at(i, owner)
        return remote(a, shard_at(i, owner), p_s.at[i], p_r.at[i], mate)

    def all_shares(i):
        half = points_at(i, pl.ds(0, points // 2))
        return remote(half, half, p_s.at[i], p_r.at[i], mate)

    def launch(t, i):
        if t == 0:
            share(0, -1, i).start()
        for direction in range(2):
            ok, copy = line(direction, t, i)
            pl.when(ok)(copy.start)

    def take(t, i):
        for direction in range(2):
            pl.when(came(direction, t))(arrival(direction, t, i).wait_recv)
        if t + 1 < chips - 1:
            launch(t + 1, i)
        for direction in range(2):
            pl.when(came(direction, t))(share(direction, t, i).start)

    def all_here(i):
        all_shares(i).wait_recv()

    def all_sent(i):
        all_shares(i).wait_send()
        for t in range(chips - 1):
            for direction in range(2):
                ok, copy = line(direction, t, i)
                pl.when(ok)(copy.wait_send)

    def unit_columns(k):
        return pl.ds(k * depth_lent, depth_lent)

    def keep_unit(k):
        return pltpu.make_async_copy(
            coup.at[:, unit_columns(k)], shard_at(LENT + k, me), x_s.at[2 + KEPT + k]
        )

    def lend(h):
        return remote(
            coup.at[:, unit_columns(KEPT + h)], shard_at(LENT, me),
            x_s.at[0], x_r.at[0], helper0 + h, "slab",
        )

    def lend_all():
        lent_columns = coup.at[:, pl.ds(KEPT * depth_lent, helpers * depth_lent)]
        here = full.at[COUP, pl.ds(0, width), pl.ds(KEPT * depth_lent, helpers * depth_lent)]
        return remote(lent_columns, here, x_s.at[0], x_r.at[0], helper0, "slab")

    def answer(h):
        return remote(dst, dv.at[h], x_s.at[1], x_r.at[1 + h], 0, "slab")

    def spread(u, k):
        own_rows = shard_at(LENT + u, me)
        return remote(
            own_rows, own_rows, x_s.at[2 + u], x_r.at[1 + helpers + u], lax.rem(me + 2 * k, n)
        )

    def spread_rest(u):
        others = points_at(LENT + u, pl.ds(0, (chips - 1) * width))
        return remote(others, others, x_s.at[2 + u], x_r.at[1 + helpers + u], mate)

    def lent_share(u, k):
        same = shard_at(LENT + u, lax.rem(me + 2 * k, n))
        return remote(same, same, p_s.at[LENT + u], p_r.at[LENT + u], mate)

    def spread_unit(u):
        lent_share(u, 0).start()
        for k in range(1, chips):
            spread(u, k).start()

    def share_unit(u):
        spread_rest(u).wait_recv()
        for k in range(1, chips):
            lent_share(u, k).start()

    edge_at = jnp.maximum(me - edge_box, 0)

    def edges_here(count):
        @pl.when(is_sender)
        def _():
            own_edge.wait()
            edge_blocks(count * helping - 1).wait_recv()

        @pl.when(~is_sender)
        def _():
            edge_blocks(count * helping).wait_recv()

        for j in range(count * helping):
            for q in range(fold):
                at = j * width + q * part
                bv[at : at + part, :] = br[j, :, q * rows : (q + 1) * rows]

    def edge_term(u, r):
        edge = bv[u * depth_lent : (u + 1) * depth_lent, :].T
        return dot3(edge, *halves(lent[u, r : r + block, :]))

    def edge_block(d):
        to = lax.rem(me + d, n)
        return remote(bst.at[to], br.at[edge_at], b_s.at[0], b_r.at[0], to)

    own_edge = pltpu.make_async_copy(bst.at[me], br.at[edge_at], b_s.at[1])

    def edge_blocks(count):
        blocks = bst.at[pl.ds(0, count)]
        return remote(blocks, blocks, b_s.at[0], b_r.at[0], mate)

    @pl.when(is_first)
    def _():
        for h in range(helpers):
            lend(h).start()
        for u in range(KEPT):
            keep_unit(u).start()

    launch(0, INV)
    pl.when(is_later & ~is_helper)(lambda: launch(0, COUP))

    @pl.when(is_sender)
    def _():
        read_done(BND)
        for j in range(n):
            for q in range(fold):
                bst[j, :, q * rows : (q + 1) * rows] = bnd[
                    q * part : (q + 1) * part, j * rows : (j + 1) * rows
                ]
        own_edge.start()
        for d in range(1, n):
            edge_block(d).start()

    read_done(MERGE)
    read_done(SLOT)
    m_hi, m_lo = halves(mv[...])
    place = (
        lax.broadcasted_iota(jnp.int32, (edges, edges), 0) == slot[...]
    ).astype(jnp.float32).astype(jnp.bfloat16)
    first = (dot_t(m_hi, place).astype(jnp.bfloat16), dot_t(m_lo, place).astype(jnp.bfloat16))

    def flux(which):
        acc = None
        for k in range(DEPTH_CHUNKS):
            if which == 0:
                read_done(LEAF + k)
            read_done(SRC + which * DEPTH_CHUNKS + k)
            cols = slice(k * kd, (k + 1) * kd)
            part = dot_t(sv[which * total // 2 : (which + 1) * total // 2, cols], lv[:, cols])
            acc = part if acc is None else acc + part
        return acc

    offset = 0
    place_of = []
    for level in range(levels):
        half = total >> (level + 1)
        pieces = 2 if level < levels - 1 else 1
        place_of.append((offset, half // pieces, pieces))
        offset += half

    def give(level, y):
        start, size, pieces = place_of[level]
        lsend[start : start + size * pieces, :] = y
        copies = []
        for c in range(pieces):
            at = pl.ds(start + c * size, size)
            copy = remote(
                lsend.at[at, :], lrecv.at[at, :], lev_s.at[0], lev_r.at[level, c], peer(level)
            )
            copies.append(copy)
            copy.start()
        return copies

    def got(level, c):
        start, size, _ = place_of[level]
        return lrecv[start + c * size : start + (c + 1) * size, :]

    copies = give(0, dot3(flux(0), *first))
    keep = dot3(flux(1), *first)
    read_done(LIFT)
    lift_split[0], lift_split[1] = halves(ltv[...])
    for i in range(2):
        read_done(OWN + i)

    @pl.when(is_helper)
    def _():
        lend(0).wait_recv()
        spread_unit(0)

    def takes(t):
        take(t, INV)
        pl.when(is_later & ~is_helper)(lambda: take(t, COUP))

        if t > 0:
            pl.when(is_helper)(lambda: take(t - 1, COUP))
            return

        @pl.when(is_helper)
        def _():
            launch(0, COUP)
            share_unit(0)

        @pl.when(is_first)
        def _():
            for u in range(KEPT):
                keep_unit(u).wait()
                spread_unit(u)

    def share_kept():
        for u in range(KEPT):
            share_unit(u)

    def help_first():
        edges_here(1)
        all_shares(LENT).wait_recv()
        for r in range(0, points, block):
            dst[:, r : r + block] = edge_term(0, r)
        answer(slab - helper0).start()

    taken = 0
    for level in range(levels):
        size = place_of[level][1]
        if taken < chips - 1:
            takes(taken)
            taken += 1
        copies[0].wait_recv()
        x = keep[:size] + got(level, 0)
        if level < levels - 1:
            later = give(level + 1, dot3(x, m_hi, m_lo))
            copies[1].wait_recv()
            keep = dot3(keep[size:] + got(level, 1), m_hi, m_lo)
            if level == 0:
                pl.when(is_helper)(help_first)
            if level == levels - 2:
                pl.when(is_first)(share_kept)
            copies = later
    load = dot3(x, lift_split[0], lift_split[1])

    for t in range(taken, chips - 1):
        takes(t)
    pl.when(is_helper)(lambda: take(chips - 2, COUP))

    def prepare(i):
        for r in range(0, points, block):
            hi, lo = halves(full[i, r : r + block, :])
            split[2 * i, r : r + block, :] = hi
            split[2 * i + 1, r : r + block, :] = lo

    def times(x, i):
        if split_ahead:
            return dot3(x, split[2 * i], split[2 * i + 1])
        return jnp.concatenate(
            [dot3(x, *halves(full[i, r : r + block, :])) for r in range(0, points, block)], axis=1
        )

    all_shares(INV).wait_recv()
    if split_ahead:
        prepare(INV)

    @pl.when(is_first)
    def _():
        edges_here(KEPT)
        for u in range(KEPT):
            all_shares(LENT + u).wait_recv()
        for r in range(0, points, block):
            rest = load[:, r : r + block]
            for u in range(KEPT):
                rest = rest - edge_term(u, r)
            cz[:, r : r + block] = rest
        for h in range(helpers):
            answer(h).wait_recv()
            cz[...] = cz[...] - dv[h]

    @pl.when(is_later)
    def _():
        cz[...] = times(load, INV) if split_ahead else load
        all_shares(COUP).wait_recv()
        if split_ahead:
            prepare(COUP)
            for r in range(0, points, block):
                at = slice(r, r + block)
                joint = product3(
                    split[2 * INV, at, :], split[2 * INV + 1, at, :],
                    split[2 * COUP], split[2 * COUP + 1],
                )
                split[4, at, :], split[5, at, :] = halves(joint)

    chunks = max(1, min(CHAIN_CHUNKS, rows // 16))
    size = rows // chunks

    def hop(c):
        at = pl.ds(c * size, size)
        return remote(
            st.at[at, :], pv.at[at, :], ch_s.at[0], ch_r.at[c],
            lax.rem(slab + 1, n_slab), "slab",
        )

    all_hops = remote(st, pv, ch_s.at[0], ch_r.at[0], lax.rem(slab + 1, n_slab), "slab")
    for c in range(chunks):
        at = slice(c * size, (c + 1) * size)

        @pl.when(is_first)
        def _():
            st[at, :] = times(cz[at, :], INV)

        @pl.when(is_later)
        def _():
            hop(c).wait_recv()
            if split_ahead:
                st[at, :] = cz[at, :] - times(pv[at, :], 2)
            else:
                st[at, :] = times(cz[at, :] - times(pv[at, :], COUP), INV)

        pl.when(slab < n_slab - 1)(hop(c).start)

    turned = st[...].T
    for j in range(n):
        for q in range(fold):
            at = j * width + q * part
            ob[j, :, q * rows : (q + 1) * rows] = turned[at : at + part]
    own = pltpu.make_async_copy(ob.at[me], rb.at[me], o_s.at[1])
    for mask in [m ^ 1 for m in range(n - 1, 1, -1)] + [1]:
        to = flip(mask)
        remote(ob.at[to], rb.at[me], o_s.at[0], o_r.at[0], to).start()
    own.start()

    exchanged = lsend.at[pl.ds(0, offset), :]
    remote(exchanged, exchanged, lev_s.at[0], lev_r.at[0, 0], mate).wait_send()
    all_sent(INV)
    pl.when(is_later)(lambda: all_sent(COUP))

    @pl.when(is_first)
    def _():
        lend_all().wait_send()
        for u in range(KEPT):
            all_shares(LENT + u).wait_send()
            spread_rest(u).wait_send()


    @pl.when(is_helper)
    def _():
        all_shares(LENT).wait_send()
        spread_rest(0).wait_send()
        answer(0).wait_send()

    pl.when(is_sender)(lambda: edge_blocks(n - 1).wait_send())
    pl.when(slab < n_slab - 1)(all_hops.wait_send)
    own.wait()
    rest = remote(ob.at[pl.ds(0, n - 1)], rb.at[pl.ds(0, n - 1)], o_s.at[0], o_r.at[0], mate)
    rest.wait_recv()
    for j in range(n):
        for q in range(fold):
            out[q * part : (q + 1) * part, j * rows : (j + 1) * rows] = rb[
                j, :, q * rows : (q + 1) * rows
            ]
    rest.wait_send()


def on_device(sources, leaf_ops, edge_slot, merge_ops, lift_ops, coupling, inverse, boundary):
    n, n_slab = lax.axis_size("box"), lax.axis_size("slab")
    total, depth = sources.shape[2:]
    edges = leaf_ops.shape[2]
    points = lift_ops.shape[2]
    rows, width = total // n, points // n
    chips, levels = n // 2, n.bit_length() - 1
    split_ahead = points * points <= 2**20
    f32, bf16 = jnp.float32, jnp.bfloat16
    hbm = pl.BlockSpec(memory_space=pl.ANY)
    dma = lambda *s: pltpu.SemaphoreType.DMA(s)
    vmem = pl.BlockSpec(memory_space=pltpu.VMEM)
    fold = st_fold(rows)
    helpers = min(HELPERS, n_slab - 1)
    units = KEPT + helpers
    result = pl.pallas_call(
        functools.partial(kernel, n, n_slab, split_ahead),
        out_shape=pltpu.VMEM((width, total), f32),
        in_specs=[hbm] * 8,
        out_specs=vmem,
        scratch_shapes=[
            pltpu.VMEM((total, depth), bf16),
            pltpu.VMEM((edges, depth), bf16),
            pltpu.VMEM((edges, edges), f32),
            pltpu.VMEM((points, edges), f32),
            pltpu.VMEM((1, edges), jnp.int32),
            pltpu.VMEM((width, total), f32),
            pltpu.VMEM((2, points, points), f32),
            pltpu.VMEM((KEPT, points, points // units), f32),
            pltpu.VMEM((6, points, points) if split_ahead else (6, 16, 128), bf16),
            pltpu.VMEM((2, points, edges), bf16),
            pltpu.VMEM((total, edges), f32),
            pltpu.VMEM((total, edges), f32),
            pltpu.VMEM((n, width // fold, rows * fold), f32),
            pltpu.VMEM((KEPT * n // units, width // fold, rows * fold), f32),
            pltpu.VMEM((KEPT * points // units, rows), f32),
            pltpu.VMEM((rows, points), f32),
            pltpu.VMEM((helpers, rows, points), f32),
            pltpu.VMEM((rows, points), f32),
            pltpu.VMEM((rows, points), f32),
            pltpu.VMEM((rows, points), f32),
            pltpu.VMEM((n, width // fold, rows * fold), f32),
            pltpu.VMEM((n, width // fold, rows * fold), f32),
            dma(3 * DEPTH_CHUNKS + 6),
            dma(1), dma(levels, 2),
            dma(2, chips + 1), dma(2, chips),
            dma(2 + KEPT), dma(2 + KEPT),
            dma(1), dma(CHAIN_CHUNKS),
            dma(2), dma(1), dma(2), dma(1), dma(2 + 2 * KEPT), dma(1 + helpers + KEPT),
        ],
        compiler_params=pltpu.CompilerParams(collective_id=0, has_side_effects=True),
        name="slab_solve",
    )(
        sources[0, 0], leaf_ops[0, 0], edge_slot[0], merge_ops[0, 0], lift_ops[0, 0],
        coupling[0], inverse[0], boundary.T,
    )
    return result.T[None]


def solution(mesh):
    return jax.shard_map(
        on_device,
        mesh=mesh,
        in_specs=(
            P("slab", "box", None, None),
            P("slab", "box", None, None),
            P("slab", "box", None),
            P("slab", "box", None, None),
            P("slab", "box", None, None),
            P("slab", "box", None),
            P("slab", "box", None),
            P(None, "box"),
        ),
        out_specs=P("slab", None, "box"),
        check_vma=False,
    )
```

```python
import functools

import jax
import jax.numpy as jnp
from jax import lax
from jax.experimental import pallas as pl
from jax.experimental.pallas import tpu as pltpu
from jax.sharding import PartitionSpec as P

MESH = pl.DeviceIdType.MESH
contract_last = (((1,), (1,)), ((), ()))
DEPTH_CHUNKS = 2
CHAIN_CHUNKS = 4
HELPERS = 2
KEPT = 2
COUP, INV, LENT = 0, 1, 2


def dot_t(a, b):
    return lax.dot_general(a, b, contract_last, preferred_element_type=jnp.float32)


def st_fold(rows):
    return max(1, 128 // rows)


def halves(x):
    hi = x.astype(jnp.bfloat16)
    return hi, (x - hi.astype(jnp.float32)).astype(jnp.bfloat16)


def product3(a_hi, a_lo, b_hi, b_lo):
    mm = functools.partial(jnp.dot, preferred_element_type=jnp.float32)
    return mm(a_hi, b_hi) + (mm(a_hi, b_lo) + mm(a_lo, b_hi))


def dot3(x, w_hi, w_lo):
    hi, lo = halves(x)
    if x.shape[0] <= 64:
        both = dot_t(jnp.concatenate([hi, lo], axis=0), w_hi)
        return both[: x.shape[0]] + (dot_t(hi, w_lo) + both[x.shape[0] :])
    return dot_t(hi, w_hi) + (dot_t(hi, w_lo) + dot_t(lo, w_hi))


def kernel(
    n, n_slab, split_ahead,
    src, leaf, slot_in, merge, lift, coup, inv, bnd_in, out,
    sv, lv, mv, ltv, slot, bnd, full, lent, split, lift_split, lsend, lrecv,
    bst, br, bv, dst, dv, pv, st, cz, ob, rb,
    loc, lev_s, lev_r, g_s, g_r, p_s, p_r, ch_s, ch_r, o_s, o_r, b_s, b_r, x_s, x_r,
):
    me, slab = lax.axis_index("box"), lax.axis_index("slab")
    chips = n // 2
    skip_ends = chips == 4
    chip = me // 2
    core = me - 2 * chip
    mate = me + 1 - 2 * core
    rows, points = pv.shape
    width = points // n
    total, edges = lsend.shape
    depth = lv.shape[1]
    kd = depth // DEPTH_CHUNKS
    levels = n.bit_length() - 1
    block = min(points, 256)
    depth_lent = lent.shape[2]
    units = points // depth_lent
    helpers = units - KEPT
    helping = n // units
    helper0 = n_slab - helpers
    is_helper = slab >= helper0
    is_first = slab == 0
    edge_box = jnp.where(is_first, 0, (KEPT + slab - helper0) * helping)
    edge_count = jnp.where(is_first, KEPT, 1) * helping
    is_sender = (is_helper | is_first) & (me >= edge_box) & (me < edge_box + edge_count)
    is_later = slab > 0
    fold = st_fold(rows)
    part = width // fold

    leaping = is_first | is_helper

    def flip(mask):
        to = me
        for q in range(levels):
            if (mask >> q) & 1:
                to = to + 2**q - 2 ** (q + 1) * lax.rem(me // 2**q, 2)
        return to

    def peer(level):
        mask = 2 ** (levels - 1 - level)
        return me + mask - 2 * mask * lax.rem(me // mask, 2)

    def block_of(position):
        block = 0
        for q in range(levels):
            bit = lax.rem(me // 2**q, 2)
            block = block + 2**q * (bit if (position >> q) & 1 else 1 - bit)
        return block

    def read(k, pairs):
        copies = [pltpu.make_async_copy(a, b, loc.at[k]) for a, b in pairs]
        for c in copies:
            c.start()

    def rows_of(who):
        return pl.ds(pl.multiple_of(who * rows, rows), rows)

    def points_at(i, at):
        return lent.at[i - LENT, at, :] if i >= LENT else full.at[i, at, :]

    def shard_at(i, owner):
        return points_at(i, pl.ds(pl.multiple_of(owner * width, width), width))

    def src_part(which, k):
        return sv.at[pl.ds(which * total // 2, total // 2), pl.ds(k * kd, kd)]

    def leaf_part(k):
        return lv.at[:, pl.ds(k * kd, kd)]

    SLOT, MERGE, LIFT, OWN, BND, SRC = 0, 1, 2, 3, 5, 6
    LEAF = SRC + 2 * DEPTH_CHUNKS
    arrays = {SLOT: slot, MERGE: mv, LIFT: ltv, OWN: shard_at(0, me), OWN + 1: shard_at(1, me), BND: bnd}
    for k in range(DEPTH_CHUNKS):
        arrays[LEAF + k] = leaf_part(k)
        for which in range(2):
            arrays[SRC + which * DEPTH_CHUNKS + k] = src_part(which, k)

    def read_done(k):
        pltpu.make_async_copy(arrays[k], arrays[k], loc.at[k]).wait()

    barrier = pltpu.get_barrier_semaphore()
    for d in range(1, n):
        pl.semaphore_signal(
            barrier, inc=1, device_id={"box": lax.rem(me + d, n)}, device_id_type=MESH
        )
    for d in range(1, n_slab):
        pl.semaphore_signal(
            barrier, inc=1, device_id={"slab": lax.rem(slab + d, n_slab)}, device_id_type=MESH
        )

    pl.when(is_sender)(lambda: read(BND, [(bnd_in, bnd)]))
    read(SLOT, [(slot_in, slot)])
    read(MERGE, [(merge, mv)])
    for which in range(2):
        for k in range(DEPTH_CHUNKS):
            cols = pl.ds(k * kd, kd)
            if which == 0:
                read(LEAF + k, [(leaf.at[:, cols], lv.at[:, cols])])
            read(SRC + which * DEPTH_CHUNKS + k, [
                (src.at[rows_of(block_of(p)), cols], sv.at[pl.ds(p * rows, rows), cols])
                for p in range(which * n // 2, (which + 1) * n // 2)
            ])
    read(LIFT, [(lift, ltv)])
    for i, m in enumerate((coup, inv)):
        read(OWN + i, [(m, shard_at(i, me))])

    pl.semaphore_wait(barrier, n + n_slab - 2)

    def remote(a, b, s, r, to, axis="box"):
        return pltpu.make_async_remote_copy(
            src_ref=a, dst_ref=b, send_sem=s, recv_sem=r,
            device_id={axis: to}, device_id_type=MESH,
        )

    def line(direction, t, i):
        step = 1 if direction == 0 else -1
        owner = me - 2 * step * t
        ok_chip = chip - step * t
        to_chip = chip + step
        a = (coup, inv)[i] if t == 0 else shard_at(i, owner)
        ok = (ok_chip >= 0) & (ok_chip < chips) & (to_chip >= 0) & (to_chip < chips)
        if skip_ends and t == 1:
            ok = ok & (~leaping | ((ok_chip > 0) & (ok_chip < chips - 1)))
        return ok, remote(
            a, shard_at(i, owner), g_s.at[i, ok_chip + direction], g_r.at[i, ok_chip], me + 2 * step
        )

    def leap(i):
        inward = jnp.where(chip == 0, 2, -2)
        return remote(
            (coup, inv)[i], shard_at(i, me), g_s.at[i, jnp.where(chip == 0, 1, chips - 1)],
            g_r.at[i, chip], me + 2 * inward,
        )

    at_end = leaping & ((chip == 0) | (chip == chips - 1))

    def arrival(direction, t, i):
        step = 1 if direction == 0 else -1
        ref = shard_at(i, me - 2 * step * (t + 1))
        return remote(
            ref, ref, g_s.at[i, chip], g_r.at[i, chip - step * (t + 1)], me - 2 * step
        )

    def came(direction, t):
        owner_chip = chip - (t + 1 if direction == 0 else -t - 1)
        return (owner_chip >= 0) & (owner_chip < chips)

    def share(direction, t, i):
        step = 1 if direction == 0 else -1
        owner = me - 2 * step * (t + 1)
        a = (coup, inv)[i] if t < 0 else shard_at(i, owner)
        return remote(a, shard_at(i, owner), p_s.at[i], p_r.at[i], mate)

    def all_shares(i):
        half = points_at(i, pl.ds(0, points // 2))
        return remote(half, half, p_s.at[i], p_r.at[i], mate)

    def launch(t, i):
        if t == 0:
            share(0, -1, i).start()
        for direction in range(2):
            ok, copy = line(direction, t, i)
            pl.when(ok)(copy.start)

    def take(t, i):
        if t == 0 and skip_ends:
            pl.when(at_end)(leap(i).start)
        for direction in range(2):
            pl.when(came(direction, t))(arrival(direction, t, i).wait_recv)
        if t + 1 < chips - 1:
            launch(t + 1, i)
        for direction in range(2):
            pl.when(came(direction, t))(share(direction, t, i).start)

    def all_here(i):
        all_shares(i).wait_recv()

    def all_sent(i):
        all_shares(i).wait_send()
        if skip_ends:
            pl.when(at_end)(leap(i).wait_send)
        for t in range(chips - 1):
            for direction in range(2):
                ok, copy = line(direction, t, i)
                pl.when(ok)(copy.wait_send)

    def unit_columns(k):
        return pl.ds(k * depth_lent, depth_lent)

    def keep_unit(k):
        return pltpu.make_async_copy(
            coup.at[:, unit_columns(k)], shard_at(LENT + k, me), x_s.at[2 + KEPT + k]
        )

    def lend(h):
        return remote(
            coup.at[:, unit_columns(KEPT + h)], shard_at(LENT, me),
            x_s.at[0], x_r.at[0], helper0 + h, "slab",
        )

    def lend_all():
        lent_columns = coup.at[:, pl.ds(KEPT * depth_lent, helpers * depth_lent)]
        here = full.at[COUP, pl.ds(0, width), pl.ds(KEPT * depth_lent, helpers * depth_lent)]
        return remote(lent_columns, here, x_s.at[0], x_r.at[0], helper0, "slab")

    def answer(h):
        return remote(dst, dv.at[h], x_s.at[1], x_r.at[1 + h], 0, "slab")

    def spread(u, k):
        own_rows = shard_at(LENT + u, me)
        return remote(
            own_rows, own_rows, x_s.at[2 + u], x_r.at[1 + helpers + u], lax.rem(me + 2 * k, n)
        )

    def spread_rest(u):
        others = points_at(LENT + u, pl.ds(0, (chips - 1) * width))
        return remote(others, others, x_s.at[2 + u], x_r.at[1 + helpers + u], mate)

    def lent_share(u, k):
        same = shard_at(LENT + u, lax.rem(me + 2 * k, n))
        return remote(same, same, p_s.at[LENT + u], p_r.at[LENT + u], mate)

    def spread_unit(u):
        lent_share(u, 0).start()
        for k in range(1, chips):
            spread(u, k).start()

    def share_unit(u):
        spread_rest(u).wait_recv()
        for k in range(1, chips):
            lent_share(u, k).start()

    edge_at = jnp.maximum(me - edge_box, 0)

    def edges_here(count):
        @pl.when(is_sender)
        def _():
            own_edge.wait()
            edge_blocks(count * helping - 1).wait_recv()

        @pl.when(~is_sender)
        def _():
            edge_blocks(count * helping).wait_recv()

        for j in range(count * helping):
            for q in range(fold):
                at = j * width + q * part
                bv[at : at + part, :] = br[j, :, q * rows : (q + 1) * rows]

    def edge_term(u, r):
        edge = bv[u * depth_lent : (u + 1) * depth_lent, :].T
        return dot3(edge, *halves(lent[u, r : r + block, :]))

    def edge_block(d):
        to = lax.rem(me + d, n)
        return remote(bst.at[to], br.at[edge_at], b_s.at[0], b_r.at[0], to)

    own_edge = pltpu.make_async_copy(bst.at[me], br.at[edge_at], b_s.at[1])

    def edge_blocks(count):
        blocks = bst.at[pl.ds(0, count)]
        return remote(blocks, blocks, b_s.at[0], b_r.at[0], mate)

    @pl.when(is_first)
    def _():
        for h in range(helpers):
            lend(h).start()
        for u in range(KEPT):
            keep_unit(u).start()

    launch(0, INV)
    pl.when(is_later & ~is_helper)(lambda: launch(0, COUP))

    @pl.when(is_sender)
    def _():
        read_done(BND)
        for j in range(n):
            for q in range(fold):
                bst[j, :, q * rows : (q + 1) * rows] = bnd[
                    q * part : (q + 1) * part, j * rows : (j + 1) * rows
                ]
        own_edge.start()
        for d in range(1, n):
            edge_block(d).start()

    read_done(MERGE)
    read_done(SLOT)
    m_hi, m_lo = halves(mv[...])
    place = (
        lax.broadcasted_iota(jnp.int32, (edges, edges), 0) == slot[...]
    ).astype(jnp.float32).astype(jnp.bfloat16)
    first = (dot_t(m_hi, place).astype(jnp.bfloat16), dot_t(m_lo, place).astype(jnp.bfloat16))

    def flux(which):
        acc = None
        for k in range(DEPTH_CHUNKS):
            if which == 0:
                read_done(LEAF + k)
            read_done(SRC + which * DEPTH_CHUNKS + k)
            cols = slice(k * kd, (k + 1) * kd)
            part = dot_t(sv[which * total // 2 : (which + 1) * total // 2, cols], lv[:, cols])
            acc = part if acc is None else acc + part
        return acc

    offset = 0
    place_of = []
    for level in range(levels):
        half = total >> (level + 1)
        pieces = 2 if level < levels - 1 else 1
        place_of.append((offset, half // pieces, pieces))
        offset += half

    def give(level, y):
        start, size, pieces = place_of[level]
        lsend[start : start + size * pieces, :] = y
        copies = []
        for c in range(pieces):
            at = pl.ds(start + c * size, size)
            copy = remote(
                lsend.at[at, :], lrecv.at[at, :], lev_s.at[0], lev_r.at[level, c], peer(level)
            )
            copies.append(copy)
            if level == 0:
                pl.when(~is_helper)(copy.start)
            else:
                copy.start()
        return copies

    def got(level, c):
        start, size, _ = place_of[level]
        return lrecv[start + c * size : start + (c + 1) * size, :]

    copies = give(0, dot3(flux(0), *first))
    keep = dot3(flux(1), *first)
    read_done(LIFT)
    lift_split[0], lift_split[1] = halves(ltv[...])
    for i in range(2):
        read_done(OWN + i)

    @pl.when(is_helper)
    def _():
        lend(0).wait_recv()
        spread_unit(0)
        for copy in copies:
            copy.start()

    def spread_kept(u):
        keep_unit(u).wait()
        spread_unit(u)

    def takes(t):
        take(t, INV)
        pl.when(is_later & ~is_helper)(lambda: take(t, COUP))

        if t > 0:
            pl.when(is_helper)(lambda: take(t - 1, COUP))
            return

        @pl.when(is_helper)
        def _():
            launch(0, COUP)
            share_unit(0)

        pl.when(is_first)(lambda: spread_kept(0))

    def share_kept():
        for u in range(KEPT):
            share_unit(u)

    def keep_first():
        share_kept()
        edges_here(KEPT)
        for u in range(KEPT):
            all_shares(LENT + u).wait_recv()
        for r in range(0, points, block):
            cz[:, r : r + block] = sum(edge_term(u, r) for u in range(KEPT))

    def help_first():
        edges_here(1)
        all_shares(LENT).wait_recv()
        for r in range(0, points, block):
            dst[:, r : r + block] = edge_term(0, r)
        answer(slab - helper0).start()

    taken = 0
    for level in range(levels):
        size = place_of[level][1]
        if taken < chips - 1:
            takes(taken)
            taken += 1
        copies[0].wait_recv()
        if level == 0:
            pl.when(is_first)(lambda: spread_kept(1))
        x = keep[:size] + got(level, 0)
        if level < levels - 1:
            later = give(level + 1, dot3(x, m_hi, m_lo))
            if level == 0:
                pl.when(is_helper)(help_first)
            copies[1].wait_recv()
            keep = dot3(keep[size:] + got(level, 1), m_hi, m_lo)
            if level == levels - 2:
                pl.when(is_first)(keep_first)
            copies = later
    load = dot3(x, lift_split[0], lift_split[1])

    for t in range(taken, chips - 1):
        takes(t)
    pl.when(is_helper)(lambda: take(chips - 2, COUP))

    def prepare(i):
        for r in range(0, points, block):
            hi, lo = halves(full[i, r : r + block, :])
            split[2 * i, r : r + block, :] = hi
            split[2 * i + 1, r : r + block, :] = lo

    def times(x, i):
        if split_ahead:
            return dot3(x, split[2 * i], split[2 * i + 1])
        return jnp.concatenate(
            [dot3(x, *halves(full[i, r : r + block, :])) for r in range(0, points, block)], axis=1
        )

    all_shares(INV).wait_recv()
    if split_ahead:
        prepare(INV)

    @pl.when(is_first)
    def _():
        cz[...] = load - cz[...]
        for h in range(helpers):
            answer(h).wait_recv()
            cz[...] = cz[...] - dv[h]

    @pl.when(is_later)
    def _():
        cz[...] = times(load, INV) if split_ahead else load
        all_shares(COUP).wait_recv()
        if split_ahead:
            prepare(COUP)
            for r in range(0, points, block):
                at = slice(r, r + block)
                joint = product3(
                    split[2 * INV, at, :], split[2 * INV + 1, at, :],
                    split[2 * COUP], split[2 * COUP + 1],
                )
                split[4, at, :], split[5, at, :] = halves(joint)

    chunks = max(1, min(CHAIN_CHUNKS, rows // 16))
    size = rows // chunks

    def hop(c):
        at = pl.ds(c * size, size)
        return remote(
            st.at[at, :], pv.at[at, :], ch_s.at[0], ch_r.at[c],
            lax.rem(slab + 1, n_slab), "slab",
        )

    all_hops = remote(st, pv, ch_s.at[0], ch_r.at[0], lax.rem(slab + 1, n_slab), "slab")
    for c in range(chunks):
        at = slice(c * size, (c + 1) * size)

        @pl.when(is_first)
        def _():
            st[at, :] = times(cz[at, :], INV)

        @pl.when(is_later)
        def _():
            hop(c).wait_recv()
            if split_ahead:
                st[at, :] = cz[at, :] - times(pv[at, :], 2)
            else:
                st[at, :] = times(cz[at, :] - times(pv[at, :], COUP), INV)

        pl.when(slab < n_slab - 1)(hop(c).start)

    turned = st[...].T
    for j in range(n):
        for q in range(fold):
            at = j * width + q * part
            ob[j, :, q * rows : (q + 1) * rows] = turned[at : at + part]
    own = pltpu.make_async_copy(ob.at[me], rb.at[me], o_s.at[1])
    for mask in [m ^ 1 for m in range(n - 1, 1, -1)] + [1]:
        to = flip(mask)
        remote(ob.at[to], rb.at[me], o_s.at[0], o_r.at[0], to).start()
    own.start()

    exchanged = lsend.at[pl.ds(0, offset), :]
    remote(exchanged, exchanged, lev_s.at[0], lev_r.at[0, 0], mate).wait_send()
    all_sent(INV)
    pl.when(is_later)(lambda: all_sent(COUP))

    @pl.when(is_first)
    def _():
        lend_all().wait_send()
        for u in range(KEPT):
            all_shares(LENT + u).wait_send()
            spread_rest(u).wait_send()


    @pl.when(is_helper)
    def _():
        all_shares(LENT).wait_send()
        spread_rest(0).wait_send()
        answer(0).wait_send()

    pl.when(is_sender)(lambda: edge_blocks(n - 1).wait_send())
    pl.when(slab < n_slab - 1)(all_hops.wait_send)
    own.wait()
    rest = remote(ob.at[pl.ds(0, n - 1)], rb.at[pl.ds(0, n - 1)], o_s.at[0], o_r.at[0], mate)
    rest.wait_recv()
    for j in range(n):
        for q in range(fold):
            out[q * part : (q + 1) * part, j * rows : (j + 1) * rows] = rb[
                j, :, q * rows : (q + 1) * rows
            ]
    rest.wait_send()


def on_device(sources, leaf_ops, edge_slot, merge_ops, lift_ops, coupling, inverse, boundary):
    n, n_slab = lax.axis_size("box"), lax.axis_size("slab")
    total, depth = sources.shape[2:]
    edges = leaf_ops.shape[2]
    points = lift_ops.shape[2]
    rows, width = total // n, points // n
    chips, levels = n // 2, n.bit_length() - 1
    split_ahead = points * points <= 2**20
    f32, bf16 = jnp.float32, jnp.bfloat16
    hbm = pl.BlockSpec(memory_space=pl.ANY)
    dma = lambda *s: pltpu.SemaphoreType.DMA(s)
    vmem = pl.BlockSpec(memory_space=pltpu.VMEM)
    fold = st_fold(rows)
    helpers = min(HELPERS, n_slab - 1)
    units = KEPT + helpers
    result = pl.pallas_call(
        functools.partial(kernel, n, n_slab, split_ahead),
        out_shape=pltpu.VMEM((width, total), f32),
        in_specs=[hbm] * 8,
        out_specs=vmem,
        scratch_shapes=[
            pltpu.VMEM((total, depth), bf16),
            pltpu.VMEM((edges, depth), bf16),
            pltpu.VMEM((edges, edges), f32),
            pltpu.VMEM((points, edges), f32),
            pltpu.VMEM((1, edges), jnp.int32),
            pltpu.VMEM((width, total), f32),
            pltpu.VMEM((2, points, points), f32),
            pltpu.VMEM((KEPT, points, points // units), f32),
            pltpu.VMEM((6, points, points) if split_ahead else (6, 16, 128), bf16),
            pltpu.VMEM((2, points, edges), bf16),
            pltpu.VMEM((total, edges), f32),
            pltpu.VMEM((total, edges), f32),
            pltpu.VMEM((n, width // fold, rows * fold), f32),
            pltpu.VMEM((KEPT * n // units, width // fold, rows * fold), f32),
            pltpu.VMEM((KEPT * points // units, rows), f32),
            pltpu.VMEM((rows, points), f32),
            pltpu.VMEM((helpers, rows, points), f32),
            pltpu.VMEM((rows, points), f32),
            pltpu.VMEM((rows, points), f32),
            pltpu.VMEM((rows, points), f32),
            pltpu.VMEM((n, width // fold, rows * fold), f32),
            pltpu.VMEM((n, width // fold, rows * fold), f32),
            dma(3 * DEPTH_CHUNKS + 6),
            dma(1), dma(levels, 2),
            dma(2, chips + 1), dma(2, chips),
            dma(2 + KEPT), dma(2 + KEPT),
            dma(1), dma(CHAIN_CHUNKS),
            dma(2), dma(1), dma(2), dma(1), dma(2 + 2 * KEPT), dma(1 + helpers + KEPT),
        ],
        compiler_params=pltpu.CompilerParams(collective_id=0, has_side_effects=True),
        name="slab_solve",
    )(
        sources[0, 0], leaf_ops[0, 0], edge_slot[0], merge_ops[0, 0], lift_ops[0, 0],
        coupling[0], inverse[0], boundary.T,
    )
    return result.T[None]


def solution(mesh):
    return jax.shard_map(
        on_device,
        mesh=mesh,
        in_specs=(
            P("slab", "box", None, None),
            P("slab", "box", None, None),
            P("slab", "box", None),
            P("slab", "box", None, None),
            P("slab", "box", None, None),
            P("slab", "box", None),
            P("slab", "box", None),
            P(None, "box"),
        ),
        out_specs=P("slab", None, "box"),
        check_vma=False,
    )
```

```python
import functools

import jax
import jax.numpy as jnp
from jax import lax
from jax.experimental import pallas as pl
from jax.experimental.pallas import tpu as pltpu
from jax.sharding import PartitionSpec as P

MESH = pl.DeviceIdType.MESH
contract_last = (((1,), (1,)), ((), ()))
DEPTH_CHUNKS = 2
CHAIN_CHUNKS = 4
HELPERS = 2
KEPT = 2
COUP, INV, LENT = 0, 1, 2


def dot_t(a, b):
    return lax.dot_general(a, b, contract_last, preferred_element_type=jnp.float32)


def st_fold(rows):
    return max(1, 128 // rows)


def halves(x):
    hi = x.astype(jnp.bfloat16)
    return hi, (x - hi.astype(jnp.float32)).astype(jnp.bfloat16)


def product3(a_hi, a_lo, b_hi, b_lo):
    mm = functools.partial(jnp.dot, preferred_element_type=jnp.float32)
    return mm(a_hi, b_hi) + (mm(a_hi, b_lo) + mm(a_lo, b_hi))


def dot3(x, w_hi, w_lo):
    hi, lo = halves(x)
    if x.shape[0] <= 64:
        both = dot_t(jnp.concatenate([hi, lo], axis=0), w_hi)
        return both[: x.shape[0]] + (dot_t(hi, w_lo) + both[x.shape[0] :])
    return dot_t(hi, w_hi) + (dot_t(hi, w_lo) + dot_t(lo, w_hi))


def kernel(
    n, n_slab, split_ahead,
    src, leaf, slot_in, merge, lift, coup, inv, bnd_in, out,
    sv, lv, mv, ltv, slot, bnd, full, lent, split, lift_split, lsend, lrecv,
    bst, br, bv, dst, dv, pv, st, cz, ob, rb,
    loc, lev_s, lev_r, g_s, g_r, p_s, p_r, ch_s, ch_r, o_s, o_r, b_s, b_r, x_s, x_r,
):
    me, slab = lax.axis_index("box"), lax.axis_index("slab")
    chips = n // 2
    skip_ends = chips == 4
    chip = me // 2
    core = me - 2 * chip
    mate = me + 1 - 2 * core
    rows, points = pv.shape
    width = points // n
    total, edges = lsend.shape
    depth = lv.shape[1]
    kd = depth // DEPTH_CHUNKS
    levels = n.bit_length() - 1
    block = min(points, 256)
    depth_lent = lent.shape[2]
    units = points // depth_lent
    helpers = units - KEPT
    helping = n // units
    helper0 = n_slab - helpers
    is_helper = slab >= helper0
    is_first = slab == 0
    edge_box = jnp.where(is_first, 0, (KEPT + slab - helper0) * helping)
    edge_count = jnp.where(is_first, KEPT, 1) * helping
    is_sender = (is_helper | is_first) & (me >= edge_box) & (me < edge_box + edge_count)
    is_later = slab > 0
    fold = st_fold(rows)
    part = width // fold

    leaping = is_first | is_helper

    def flip(mask):
        to = me
        for q in range(levels):
            if (mask >> q) & 1:
                to = to + 2**q - 2 ** (q + 1) * lax.rem(me // 2**q, 2)
        return to

    def peer(level):
        mask = 2 ** (levels - 1 - level)
        return me + mask - 2 * mask * lax.rem(me // mask, 2)

    def block_of(position):
        block = 0
        for q in range(levels):
            bit = lax.rem(me // 2**q, 2)
            block = block + 2**q * (bit if (position >> q) & 1 else 1 - bit)
        return block

    def read(k, pairs):
        copies = [pltpu.make_async_copy(a, b, loc.at[k]) for a, b in pairs]
        for c in copies:
            c.start()

    def rows_of(who):
        return pl.ds(pl.multiple_of(who * rows, rows), rows)

    def points_at(i, at):
        return lent.at[i - LENT, at, :] if i >= LENT else full.at[i, at, :]

    def shard_at(i, owner):
        return points_at(i, pl.ds(pl.multiple_of(owner * width, width), width))

    def src_part(which, k):
        return sv.at[pl.ds(which * total // 2, total // 2), pl.ds(k * kd, kd)]

    def leaf_part(k):
        return lv.at[:, pl.ds(k * kd, kd)]

    SLOT, MERGE, LIFT, OWN, BND, SRC = 0, 1, 2, 3, 5, 6
    LEAF = SRC + 2 * DEPTH_CHUNKS
    arrays = {SLOT: slot, MERGE: mv, LIFT: ltv, OWN: shard_at(0, me), OWN + 1: shard_at(1, me), BND: bnd}
    for k in range(DEPTH_CHUNKS):
        arrays[LEAF + k] = leaf_part(k)
        for which in range(2):
            arrays[SRC + which * DEPTH_CHUNKS + k] = src_part(which, k)

    def read_done(k):
        pltpu.make_async_copy(arrays[k], arrays[k], loc.at[k]).wait()

    barrier = pltpu.get_barrier_semaphore()
    for d in range(1, n):
        pl.semaphore_signal(
            barrier, inc=1, device_id={"box": lax.rem(me + d, n)}, device_id_type=MESH
        )
    for d in range(1, n_slab):
        pl.semaphore_signal(
            barrier, inc=1, device_id={"slab": lax.rem(slab + d, n_slab)}, device_id_type=MESH
        )

    pl.when(is_sender)(lambda: read(BND, [(bnd_in, bnd)]))
    read(SLOT, [(slot_in, slot)])
    read(MERGE, [(merge, mv)])
    for which in range(2):
        for k in range(DEPTH_CHUNKS):
            cols = pl.ds(k * kd, kd)
            if which == 0:
                read(LEAF + k, [(leaf.at[:, cols], lv.at[:, cols])])
            read(SRC + which * DEPTH_CHUNKS + k, [
                (src.at[rows_of(block_of(p)), cols], sv.at[pl.ds(p * rows, rows), cols])
                for p in range(which * n // 2, (which + 1) * n // 2)
            ])
    read(LIFT, [(lift, ltv)])
    for i, m in enumerate((coup, inv)):
        read(OWN + i, [(m, shard_at(i, me))])

    def unit_columns(k):
        return pl.ds(k * depth_lent, depth_lent)

    def keep_unit(k):
        return pltpu.make_async_copy(
            coup.at[:, unit_columns(k)], shard_at(LENT + k, me), x_s.at[2 + KEPT + k]
        )

    @pl.when(is_first)
    def _():
        for u in range(KEPT):
            keep_unit(u).start()

    pl.semaphore_wait(barrier, n + n_slab - 2)

    def remote(a, b, s, r, to, axis="box"):
        return pltpu.make_async_remote_copy(
            src_ref=a, dst_ref=b, send_sem=s, recv_sem=r,
            device_id={axis: to}, device_id_type=MESH,
        )

    def line(direction, t, i):
        step = 1 if direction == 0 else -1
        owner = me - 2 * step * t
        ok_chip = chip - step * t
        to_chip = chip + step
        a = (coup, inv)[i] if t == 0 else shard_at(i, owner)
        ok = (ok_chip >= 0) & (ok_chip < chips) & (to_chip >= 0) & (to_chip < chips)
        if skip_ends and t == 1:
            ok = ok & (~leaping | ((ok_chip > 0) & (ok_chip < chips - 1)))
        return ok, remote(
            a, shard_at(i, owner), g_s.at[i, ok_chip + direction], g_r.at[i, ok_chip], me + 2 * step
        )

    def leap(i):
        inward = jnp.where(chip == 0, 2, -2)
        return remote(
            (coup, inv)[i], shard_at(i, me), g_s.at[i, jnp.where(chip == 0, 1, chips - 1)],
            g_r.at[i, chip], me + 2 * inward,
        )

    at_end = leaping & ((chip == 0) | (chip == chips - 1))

    def arrival(direction, t, i):
        step = 1 if direction == 0 else -1
        ref = shard_at(i, me - 2 * step * (t + 1))
        return remote(
            ref, ref, g_s.at[i, chip], g_r.at[i, chip - step * (t + 1)], me - 2 * step
        )

    def came(direction, t):
        owner_chip = chip - (t + 1 if direction == 0 else -t - 1)
        return (owner_chip >= 0) & (owner_chip < chips)

    def share(direction, t, i):
        step = 1 if direction == 0 else -1
        owner = me - 2 * step * (t + 1)
        a = (coup, inv)[i] if t < 0 else shard_at(i, owner)
        return remote(a, shard_at(i, owner), p_s.at[i], p_r.at[i], mate)

    def all_shares(i):
        half = points_at(i, pl.ds(0, points // 2))
        return remote(half, half, p_s.at[i], p_r.at[i], mate)

    def launch(t, i):
        if t == 0:
            share(0, -1, i).start()
        for direction in range(2):
            ok, copy = line(direction, t, i)
            pl.when(ok)(copy.start)

    def take(t, i):
        if t == 0 and skip_ends:
            pl.when(at_end)(leap(i).start)
        for direction in range(2):
            pl.when(came(direction, t))(arrival(direction, t, i).wait_recv)
        if t + 1 < chips - 1:
            launch(t + 1, i)
        for direction in range(2):
            pl.when(came(direction, t))(share(direction, t, i).start)

    def all_here(i):
        all_shares(i).wait_recv()

    def all_sent(i):
        all_shares(i).wait_send()
        if skip_ends:
            pl.when(at_end)(leap(i).wait_send)
        for t in range(chips - 1):
            for direction in range(2):
                ok, copy = line(direction, t, i)
                pl.when(ok)(copy.wait_send)

    def lend(h):
        return remote(
            coup.at[:, unit_columns(KEPT + h)], shard_at(LENT, me),
            x_s.at[0], x_r.at[0], helper0 + h, "slab",
        )

    def lend_all():
        lent_columns = coup.at[:, pl.ds(KEPT * depth_lent, helpers * depth_lent)]
        here = full.at[COUP, pl.ds(0, width), pl.ds(KEPT * depth_lent, helpers * depth_lent)]
        return remote(lent_columns, here, x_s.at[0], x_r.at[0], helper0, "slab")

    def answer(h):
        return remote(dst, dv.at[h], x_s.at[1], x_r.at[1 + h], 0, "slab")

    def spread(u, owner, to):
        shard = shard_at(LENT + u, owner)
        return remote(shard, shard, x_s.at[2 + u], x_r.at[1 + helpers + u], to)

    def spread_rows(u, count):
        some = points_at(LENT + u, pl.ds(0, count * width))
        return remote(some, some, x_s.at[2 + u], x_r.at[1 + helpers + u], mate)

    relayed = is_first & skip_ends
    middle = (chip > 0) & (chip < chips - 1)
    pair = me + 2 - 4 * lax.rem(chip, 2)
    low = chip < chips // 2
    across = me + 2 * (jnp.where(low, chips // 2, chips // 2 - 1) - chip)
    other_half = me + 2 * (jnp.where(low, chips // 2, 0) - chip)

    def lent_share(u, k):
        same = shard_at(LENT + u, lax.rem(me + 2 * k, n))
        return remote(same, same, p_s.at[LENT + u], p_r.at[LENT + u], mate)

    def spread_unit(u):
        lent_share(u, 0).start()

        @pl.when(relayed)
        def _():
            spread(u, me, across).start()
            spread(u, me, pair).start()

        @pl.when(~relayed)
        def _():
            for k in range(1, chips):
                spread(u, me, lax.rem(me + 2 * k, n)).start()

    def share_unit(u):
        spread_rows(u, chips - 1).wait_recv()
        @pl.when(relayed & middle)
        def _():
            for k in range(chips // 2):
                spread(u, other_half + 2 * k, pair).start()

        for k in range(1, chips):
            lent_share(u, k).start()

    def unit_sent(u):
        all_shares(LENT + u).wait_send()
        pl.when(relayed & middle)(lambda: spread_rows(u, chips).wait_send())
        pl.when(relayed & ~middle)(lambda: spread_rows(u, chips // 2).wait_send())
        pl.when(~relayed)(lambda: spread_rows(u, chips - 1).wait_send())

    edge_at = jnp.maximum(me - edge_box, 0)

    def edges_here(count):
        @pl.when(is_sender)
        def _():
            own_edge.wait()
            edge_blocks(count * helping - 1).wait_recv()

        @pl.when(~is_sender)
        def _():
            edge_blocks(count * helping).wait_recv()

        for j in range(count * helping):
            for q in range(fold):
                at = j * width + q * part
                bv[at : at + part, :] = br[j, :, q * rows : (q + 1) * rows]

    def edge_term(u, r):
        edge = bv[u * depth_lent : (u + 1) * depth_lent, :].T
        return dot3(edge, *halves(lent[u, r : r + block, :]))

    def edge_block(d):
        to = lax.rem(me + d, n)
        return remote(bst.at[to], br.at[edge_at], b_s.at[0], b_r.at[0], to)

    own_edge = pltpu.make_async_copy(bst.at[me], br.at[edge_at], b_s.at[1])

    def edge_blocks(count):
        blocks = bst.at[pl.ds(0, count)]
        return remote(blocks, blocks, b_s.at[0], b_r.at[0], mate)

    launch(0, INV)

    @pl.when(is_first)
    def _():
        for h in range(helpers):
            lend(h).start()
        for u in range(KEPT):
            keep_unit(u).wait()
            spread_unit(u)

    pl.when(is_later & ~is_helper)(lambda: launch(0, COUP))

    @pl.when(is_sender)
    def _():
        read_done(BND)
        for j in range(n):
            for q in range(fold):
                bst[j, :, q * rows : (q + 1) * rows] = bnd[
                    q * part : (q + 1) * part, j * rows : (j + 1) * rows
                ]
        own_edge.start()
        for d in range(1, n):
            edge_block(d).start()

    read_done(MERGE)
    read_done(SLOT)
    m_hi, m_lo = halves(mv[...])
    place = (
        lax.broadcasted_iota(jnp.int32, (edges, edges), 0) == slot[...]
    ).astype(jnp.float32).astype(jnp.bfloat16)
    first = (dot_t(m_hi, place).astype(jnp.bfloat16), dot_t(m_lo, place).astype(jnp.bfloat16))

    def flux(which):
        acc = None
        for k in range(DEPTH_CHUNKS):
            if which == 0:
                read_done(LEAF + k)
            read_done(SRC + which * DEPTH_CHUNKS + k)
            cols = slice(k * kd, (k + 1) * kd)
            part = dot_t(sv[which * total // 2 : (which + 1) * total // 2, cols], lv[:, cols])
            acc = part if acc is None else acc + part
        return acc

    offset = 0
    place_of = []
    for level in range(levels):
        half = total >> (level + 1)
        pieces = 2 if level < levels - 1 else 1
        place_of.append((offset, half // pieces, pieces))
        offset += half

    def give(level, y):
        start, size, pieces = place_of[level]
        lsend[start : start + size * pieces, :] = y
        copies = []
        for c in range(pieces):
            at = pl.ds(start + c * size, size)
            copy = remote(
                lsend.at[at, :], lrecv.at[at, :], lev_s.at[0], lev_r.at[level, c], peer(level)
            )
            copies.append(copy)
            if level == 0:
                pl.when(~is_helper)(copy.start)
            else:
                copy.start()
        return copies

    def got(level, c):
        start, size, _ = place_of[level]
        return lrecv[start + c * size : start + (c + 1) * size, :]

    copies = give(0, dot3(flux(0), *first))
    keep = dot3(flux(1), *first)
    read_done(LIFT)
    lift_split[0], lift_split[1] = halves(ltv[...])
    for i in range(2):
        read_done(OWN + i)

    @pl.when(is_helper)
    def _():
        lend(0).wait_recv()
        spread_unit(0)
        for copy in copies:
            copy.start()

    def takes(t):
        take(t, INV)
        pl.when(is_later & ~is_helper)(lambda: take(t, COUP))

        if t > 0:
            pl.when(is_helper)(lambda: take(t - 1, COUP))
            return

        @pl.when(is_helper)
        def _():
            launch(0, COUP)
            share_unit(0)

    def share_kept():
        for u in range(KEPT):
            share_unit(u)

    def keep_first():
        pl.when(~(middle & relayed))(share_kept)
        edges_here(KEPT)
        for u in range(KEPT):
            all_shares(LENT + u).wait_recv()
        for r in range(0, points, block):
            cz[:, r : r + block] = sum(edge_term(u, r) for u in range(KEPT))

    def help_first():
        edges_here(1)
        all_shares(LENT).wait_recv()
        for r in range(0, points, block):
            dst[:, r : r + block] = edge_term(0, r)
        answer(slab - helper0).start()

    taken = 0
    for level in range(levels):
        size = place_of[level][1]
        if taken < chips - 1:
            takes(taken)
            if taken == 0:
                pl.when(relayed & middle)(share_kept)
            taken += 1
        copies[0].wait_recv()
        x = keep[:size] + got(level, 0)
        if level < levels - 1:
            later = give(level + 1, dot3(x, m_hi, m_lo))
            if level == 0:
                pl.when(is_helper)(help_first)
            copies[1].wait_recv()
            keep = dot3(keep[size:] + got(level, 1), m_hi, m_lo)
            if level == levels - 2:
                pl.when(is_first)(keep_first)
            copies = later
    load = dot3(x, lift_split[0], lift_split[1])

    for t in range(taken, chips - 1):
        takes(t)
    pl.when(is_helper)(lambda: take(chips - 2, COUP))

    def prepare(i):
        for r in range(0, points, block):
            hi, lo = halves(full[i, r : r + block, :])
            split[2 * i, r : r + block, :] = hi
            split[2 * i + 1, r : r + block, :] = lo

    def times(x, i):
        if split_ahead:
            return dot3(x, split[2 * i], split[2 * i + 1])
        return jnp.concatenate(
            [dot3(x, *halves(full[i, r : r + block, :])) for r in range(0, points, block)], axis=1
        )

    all_shares(INV).wait_recv()
    if split_ahead:
        prepare(INV)

    @pl.when(is_first)
    def _():
        cz[...] = load - cz[...]
        for h in range(helpers):
            answer(h).wait_recv()
            cz[...] = cz[...] - dv[h]

    @pl.when(is_later)
    def _():
        cz[...] = times(load, INV) if split_ahead else load
        all_shares(COUP).wait_recv()
        if split_ahead:
            prepare(COUP)
            for r in range(0, points, block):
                at = slice(r, r + block)
                joint = product3(
                    split[2 * INV, at, :], split[2 * INV + 1, at, :],
                    split[2 * COUP], split[2 * COUP + 1],
                )
                split[4, at, :], split[5, at, :] = halves(joint)

    chunks = max(1, min(CHAIN_CHUNKS, rows // 16))
    size = rows // chunks

    def hop(c):
        at = pl.ds(c * size, size)
        return remote(
            st.at[at, :], pv.at[at, :], ch_s.at[0], ch_r.at[c],
            lax.rem(slab + 1, n_slab), "slab",
        )

    all_hops = remote(st, pv, ch_s.at[0], ch_r.at[0], lax.rem(slab + 1, n_slab), "slab")
    for c in range(chunks):
        at = slice(c * size, (c + 1) * size)

        @pl.when(is_first)
        def _():
            st[at, :] = times(cz[at, :], INV)

        @pl.when(is_later)
        def _():
            hop(c).wait_recv()
            if split_ahead:
                st[at, :] = cz[at, :] - times(pv[at, :], 2)
            else:
                st[at, :] = times(cz[at, :] - times(pv[at, :], COUP), INV)

        pl.when(slab < n_slab - 1)(hop(c).start)

    turned = st[...].T
    for j in range(n):
        for q in range(fold):
            at = j * width + q * part
            ob[j, :, q * rows : (q + 1) * rows] = turned[at : at + part]
    own = pltpu.make_async_copy(ob.at[me], rb.at[me], o_s.at[1])
    for mask in [m ^ 1 for m in range(n - 1, 1, -1)] + [1]:
        to = flip(mask)
        remote(ob.at[to], rb.at[me], o_s.at[0], o_r.at[0], to).start()
    own.start()

    exchanged = lsend.at[pl.ds(0, offset), :]
    remote(exchanged, exchanged, lev_s.at[0], lev_r.at[0, 0], mate).wait_send()
    all_sent(INV)
    pl.when(is_later)(lambda: all_sent(COUP))

    @pl.when(is_first)
    def _():
        lend_all().wait_send()
        for u in range(KEPT):
            unit_sent(u)


    @pl.when(is_helper)
    def _():
        unit_sent(0)
        answer(0).wait_send()

    pl.when(is_sender)(lambda: edge_blocks(n - 1).wait_send())
    pl.when(slab < n_slab - 1)(all_hops.wait_send)
    own.wait()
    rest = remote(ob.at[pl.ds(0, n - 1)], rb.at[pl.ds(0, n - 1)], o_s.at[0], o_r.at[0], mate)
    rest.wait_recv()
    for j in range(n):
        for q in range(fold):
            out[q * part : (q + 1) * part, j * rows : (j + 1) * rows] = rb[
                j, :, q * rows : (q + 1) * rows
            ]
    rest.wait_send()


def on_device(sources, leaf_ops, edge_slot, merge_ops, lift_ops, coupling, inverse, boundary):
    n, n_slab = lax.axis_size("box"), lax.axis_size("slab")
    total, depth = sources.shape[2:]
    edges = leaf_ops.shape[2]
    points = lift_ops.shape[2]
    rows, width = total // n, points // n
    chips, levels = n // 2, n.bit_length() - 1
    split_ahead = points * points <= 2**20
    f32, bf16 = jnp.float32, jnp.bfloat16
    hbm = pl.BlockSpec(memory_space=pl.ANY)
    dma = lambda *s: pltpu.SemaphoreType.DMA(s)
    vmem = pl.BlockSpec(memory_space=pltpu.VMEM)
    fold = st_fold(rows)
    helpers = min(HELPERS, n_slab - 1)
    units = KEPT + helpers
    result = pl.pallas_call(
        functools.partial(kernel, n, n_slab, split_ahead),
        out_shape=pltpu.VMEM((width, total), f32),
        in_specs=[hbm] * 8,
        out_specs=vmem,
        scratch_shapes=[
            pltpu.VMEM((total, depth), bf16),
            pltpu.VMEM((edges, depth), bf16),
            pltpu.VMEM((edges, edges), f32),
            pltpu.VMEM((points, edges), f32),
            pltpu.VMEM((1, edges), jnp.int32),
            pltpu.VMEM((width, total), f32),
            pltpu.VMEM((2, points, points), f32),
            pltpu.VMEM((KEPT, points, points // units), f32),
            pltpu.VMEM((6, points, points) if split_ahead else (6, 16, 128), bf16),
            pltpu.VMEM((2, points, edges), bf16),
            pltpu.VMEM((total, edges), f32),
            pltpu.VMEM((total, edges), f32),
            pltpu.VMEM((n, width // fold, rows * fold), f32),
            pltpu.VMEM((KEPT * n // units, width // fold, rows * fold), f32),
            pltpu.VMEM((KEPT * points // units, rows), f32),
            pltpu.VMEM((rows, points), f32),
            pltpu.VMEM((helpers, rows, points), f32),
            pltpu.VMEM((rows, points), f32),
            pltpu.VMEM((rows, points), f32),
            pltpu.VMEM((rows, points), f32),
            pltpu.VMEM((n, width // fold, rows * fold), f32),
            pltpu.VMEM((n, width // fold, rows * fold), f32),
            dma(3 * DEPTH_CHUNKS + 6),
            dma(1), dma(levels, 2),
            dma(2, chips + 1), dma(2, chips),
            dma(2 + KEPT), dma(2 + KEPT),
            dma(1), dma(CHAIN_CHUNKS),
            dma(2), dma(1), dma(2), dma(1), dma(2 + 2 * KEPT), dma(1 + helpers + KEPT),
        ],
        compiler_params=pltpu.CompilerParams(collective_id=0, has_side_effects=True),
        name="slab_solve",
    )(
        sources[0, 0], leaf_ops[0, 0], edge_slot[0], merge_ops[0, 0], lift_ops[0, 0],
        coupling[0], inverse[0], boundary.T,
    )
    return result.T[None]


def solution(mesh):
    return jax.shard_map(
        on_device,
        mesh=mesh,
        in_specs=(
            P("slab", "box", None, None),
            P("slab", "box", None, None),
            P("slab", "box", None),
            P("slab", "box", None, None),
            P("slab", "box", None, None),
            P("slab", "box", None),
            P("slab", "box", None),
            P(None, "box"),
        ),
        out_specs=P("slab", None, "box"),
        check_vma=False,
    )
```

```python
import functools

import jax
import jax.numpy as jnp
from jax import lax
from jax.experimental import pallas as pl
from jax.experimental.pallas import tpu as pltpu
from jax.sharding import PartitionSpec as P

MESH = pl.DeviceIdType.MESH
contract_last = (((1,), (1,)), ((), ()))
DEPTH_CHUNKS = 2
CHAIN_CHUNKS = 4
HELPERS = 2
KEPT = 2
COUP, INV, LENT = 0, 1, 2


def dot_t(a, b):
    return lax.dot_general(a, b, contract_last, preferred_element_type=jnp.float32)


def st_fold(rows):
    return max(1, 128 // rows)


def halves(x):
    hi = x.astype(jnp.bfloat16)
    return hi, (x - hi.astype(jnp.float32)).astype(jnp.bfloat16)


def product3(a_hi, a_lo, b_hi, b_lo):
    mm = functools.partial(jnp.dot, preferred_element_type=jnp.float32)
    return mm(a_hi, b_hi) + (mm(a_hi, b_lo) + mm(a_lo, b_hi))


def dot3(x, w_hi, w_lo):
    hi, lo = halves(x)
    if x.shape[0] <= 64:
        both = dot_t(jnp.concatenate([hi, lo], axis=0), w_hi)
        return both[: x.shape[0]] + (dot_t(hi, w_lo) + both[x.shape[0] :])
    return dot_t(hi, w_hi) + (dot_t(hi, w_lo) + dot_t(lo, w_hi))


def kernel(
    n, n_slab, split_ahead,
    src, leaf, slot_in, merge, lift, coup, inv, bnd_in, out,
    sv, lv, mv, ltv, slot, bnd, full, lent, split, lift_split, lsend, lrecv,
    bst, br, bv, dst, dv, pv, st, cz, ob, rb,
    loc, lev_s, lev_r, g_s, g_r, p_s, p_r, ch_s, ch_r, o_s, o_r, b_s, b_r, x_s, x_r,
):
    me, slab = lax.axis_index("box"), lax.axis_index("slab")
    chips = n // 2
    skip_ends = chips == 4
    chip = me // 2
    core = me - 2 * chip
    mate = me + 1 - 2 * core
    rows, points = pv.shape
    width = points // n
    total, edges = lsend.shape
    depth = lv.shape[1]
    kd = depth // DEPTH_CHUNKS
    levels = n.bit_length() - 1
    block = min(points, 256)
    depth_lent = lent.shape[2]
    units = points // depth_lent
    helpers = units - KEPT
    helping = n // units
    helper0 = n_slab - helpers
    is_helper = slab >= helper0
    is_first = slab == 0
    kept = (0, units - 1)
    my_unit = me // helping
    is_sender = (is_first & ((my_unit == kept[0]) | (my_unit == kept[1]))) | (
        is_helper & (my_unit == helpers - slab + helper0)
    )
    edge_at = lax.rem(me, helping) + jnp.where(is_first & (my_unit == kept[1]), helping, 0)
    is_later = slab > 0
    fold = st_fold(rows)
    part = width // fold

    leaping = is_first | is_helper

    def flip(mask):
        to = me
        for q in range(levels):
            if (mask >> q) & 1:
                to = to + 2**q - 2 ** (q + 1) * lax.rem(me // 2**q, 2)
        return to

    def peer(level):
        mask = 2 ** (levels - 1 - level)
        return me + mask - 2 * mask * lax.rem(me // mask, 2)

    def block_of(position):
        block = 0
        for q in range(levels):
            bit = lax.rem(me // 2**q, 2)
            block = block + 2**q * (bit if (position >> q) & 1 else 1 - bit)
        return block

    def read(k, pairs):
        copies = [pltpu.make_async_copy(a, b, loc.at[k]) for a, b in pairs]
        for c in copies:
            c.start()

    def rows_of(who):
        return pl.ds(pl.multiple_of(who * rows, rows), rows)

    def points_at(i, at):
        return lent.at[i - LENT, at, :] if i >= LENT else full.at[i, at, :]

    def shard_at(i, owner):
        return points_at(i, pl.ds(pl.multiple_of(owner * width, width), width))

    def src_part(which, k):
        return sv.at[pl.ds(which * total // 2, total // 2), pl.ds(k * kd, kd)]

    def leaf_part(k):
        return lv.at[:, pl.ds(k * kd, kd)]

    SLOT, MERGE, LIFT, OWN, BND, SRC = 0, 1, 2, 3, 5, 6
    LEAF = SRC + 2 * DEPTH_CHUNKS
    arrays = {SLOT: slot, MERGE: mv, LIFT: ltv, OWN: shard_at(0, me), OWN + 1: shard_at(1, me), BND: bnd}
    for k in range(DEPTH_CHUNKS):
        arrays[LEAF + k] = leaf_part(k)
        for which in range(2):
            arrays[SRC + which * DEPTH_CHUNKS + k] = src_part(which, k)

    def read_done(k):
        pltpu.make_async_copy(arrays[k], arrays[k], loc.at[k]).wait()

    barrier = pltpu.get_barrier_semaphore()
    for d in range(1, n):
        pl.semaphore_signal(
            barrier, inc=1, device_id={"box": lax.rem(me + d, n)}, device_id_type=MESH
        )
    for d in range(1, n_slab):
        pl.semaphore_signal(
            barrier, inc=1, device_id={"slab": lax.rem(slab + d, n_slab)}, device_id_type=MESH
        )

    pl.when(is_sender)(lambda: read(BND, [(bnd_in, bnd)]))
    read(SLOT, [(slot_in, slot)])
    read(MERGE, [(merge, mv)])
    for which in range(2):
        for k in range(DEPTH_CHUNKS):
            cols = pl.ds(k * kd, kd)
            if which == 0:
                read(LEAF + k, [(leaf.at[:, cols], lv.at[:, cols])])
            read(SRC + which * DEPTH_CHUNKS + k, [
                (src.at[rows_of(block_of(p)), cols], sv.at[pl.ds(p * rows, rows), cols])
                for p in range(which * n // 2, (which + 1) * n // 2)
            ])
    read(LIFT, [(lift, ltv)])
    for i, m in enumerate((coup, inv)):
        read(OWN + i, [(m, shard_at(i, me))])

    def unit_columns(k):
        return pl.ds(k * depth_lent, depth_lent)

    def keep_unit(k):
        return pltpu.make_async_copy(
            coup.at[:, unit_columns(kept[k])], shard_at(LENT + k, me), x_s.at[2 + KEPT + k]
        )

    @pl.when(is_first)
    def _():
        for u in range(KEPT):
            keep_unit(u).start()

    pl.semaphore_wait(barrier, n + n_slab - 2)

    def remote(a, b, s, r, to, axis="box"):
        return pltpu.make_async_remote_copy(
            src_ref=a, dst_ref=b, send_sem=s, recv_sem=r,
            device_id={axis: to}, device_id_type=MESH,
        )

    def line(direction, t, i):
        step = 1 if direction == 0 else -1
        owner = me - 2 * step * t
        ok_chip = chip - step * t
        to_chip = chip + step
        a = (coup, inv)[i] if t == 0 else shard_at(i, owner)
        ok = (ok_chip >= 0) & (ok_chip < chips) & (to_chip >= 0) & (to_chip < chips)
        if skip_ends and t == 1:
            ok = ok & (~leaping | ((ok_chip > 0) & (ok_chip < chips - 1)))
        return ok, remote(
            a, shard_at(i, owner), g_s.at[i, ok_chip + direction], g_r.at[i, ok_chip], me + 2 * step
        )

    def leap(i):
        inward = jnp.where(chip == 0, 2, -2)
        return remote(
            (coup, inv)[i], shard_at(i, me), g_s.at[i, jnp.where(chip == 0, 1, chips - 1)],
            g_r.at[i, chip], me + 2 * inward,
        )

    at_end = leaping & ((chip == 0) | (chip == chips - 1))

    def arrival(direction, t, i):
        step = 1 if direction == 0 else -1
        ref = shard_at(i, me - 2 * step * (t + 1))
        return remote(
            ref, ref, g_s.at[i, chip], g_r.at[i, chip - step * (t + 1)], me - 2 * step
        )

    def came(direction, t):
        owner_chip = chip - (t + 1 if direction == 0 else -t - 1)
        return (owner_chip >= 0) & (owner_chip < chips)

    def share(direction, t, i):
        step = 1 if direction == 0 else -1
        owner = me - 2 * step * (t + 1)
        a = (coup, inv)[i] if t < 0 else shard_at(i, owner)
        return remote(a, shard_at(i, owner), p_s.at[i], p_r.at[i], mate)

    def all_shares(i):
        half = points_at(i, pl.ds(0, points // 2))
        return remote(half, half, p_s.at[i], p_r.at[i], mate)

    def launch(t, i):
        if t == 0:
            share(0, -1, i).start()
        for direction in range(2):
            ok, copy = line(direction, t, i)
            pl.when(ok)(copy.start)

    def take(t, i):
        if t == 0 and skip_ends:
            pl.when(at_end)(leap(i).start)
        for direction in range(2):
            pl.when(came(direction, t))(arrival(direction, t, i).wait_recv)
        if t + 1 < chips - 1:
            launch(t + 1, i)
        for direction in range(2):
            pl.when(came(direction, t))(share(direction, t, i).start)

    def all_here(i):
        all_shares(i).wait_recv()

    def all_sent(i):
        all_shares(i).wait_send()
        if skip_ends:
            pl.when(at_end)(leap(i).wait_send)
        for t in range(chips - 1):
            for direction in range(2):
                ok, copy = line(direction, t, i)
                pl.when(ok)(copy.wait_send)

    def lend(h):
        return remote(
            coup.at[:, unit_columns(helpers - h)], shard_at(LENT, me),
            x_s.at[0], x_r.at[0], helper0 + h, "slab",
        )

    def lend_all():
        columns = pl.ds(depth_lent, helpers * depth_lent)
        lent_columns = coup.at[:, columns]
        here = full.at[COUP, pl.ds(0, width), columns]
        return remote(lent_columns, here, x_s.at[0], x_r.at[0], helper0, "slab")

    def answer(h):
        return remote(dst, dv.at[h], x_s.at[1], x_r.at[1 + h], 0, "slab")

    def spread(u, owner, to):
        shard = shard_at(LENT + u, owner)
        return remote(shard, shard, x_s.at[2 + u], x_r.at[1 + helpers + u], to)

    def spread_rows(u, count):
        some = points_at(LENT + u, pl.ds(0, count * width))
        return remote(some, some, x_s.at[2 + u], x_r.at[1 + helpers + u], mate)

    relayed = is_first & skip_ends
    middle = (chip > 0) & (chip < chips - 1)
    pair = me + 2 - 4 * lax.rem(chip, 2)
    low = chip < chips // 2
    across = me + 2 * (jnp.where(low, chips // 2, chips // 2 - 1) - chip)
    other_half = me + 2 * (jnp.where(low, chips // 2, 0) - chip)

    def lent_share(u, k):
        same = shard_at(LENT + u, lax.rem(me + 2 * k, n))
        return remote(same, same, p_s.at[LENT + u], p_r.at[LENT + u], mate)

    def spread_unit(u):
        lent_share(u, 0).start()

        @pl.when(relayed)
        def _():
            spread(u, me, across).start()
            spread(u, me, pair).start()

        @pl.when(~relayed)
        def _():
            for k in range(1, chips):
                spread(u, me, lax.rem(me + 2 * k, n)).start()

    def share_unit(u):
        spread_rows(u, chips - 1).wait_recv()
        @pl.when(relayed & middle)
        def _():
            for k in range(chips // 2):
                spread(u, other_half + 2 * k, pair).start()

        for k in range(1, chips):
            lent_share(u, k).start()

    def unit_sent(u):
        all_shares(LENT + u).wait_send()
        pl.when(relayed & middle)(lambda: spread_rows(u, chips).wait_send())
        pl.when(relayed & ~middle)(lambda: spread_rows(u, chips // 2).wait_send())
        pl.when(~relayed)(lambda: spread_rows(u, chips - 1).wait_send())

    def edges_here(count):
        @pl.when(is_sender)
        def _():
            own_edge.wait()
            edge_blocks(count * helping - 1).wait_recv()

        @pl.when(~is_sender)
        def _():
            edge_blocks(count * helping).wait_recv()

        for j in range(count * helping):
            for q in range(fold):
                at = j * width + q * part
                bv[at : at + part, :] = br[j, :, q * rows : (q + 1) * rows]

    def edge_term(u, r):
        edge = bv[u * depth_lent : (u + 1) * depth_lent, :].T
        return dot3(edge, *halves(lent[u, r : r + block, :]))

    def edge_block(d):
        to = lax.rem(me + d, n)
        return remote(bst.at[to], br.at[edge_at], b_s.at[0], b_r.at[0], to)

    own_edge = pltpu.make_async_copy(bst.at[me], br.at[edge_at], b_s.at[1])

    def edge_blocks(count):
        blocks = bst.at[pl.ds(0, count)]
        return remote(blocks, blocks, b_s.at[0], b_r.at[0], mate)

    launch(0, INV)

    @pl.when(is_first)
    def _():
        for h in range(helpers):
            lend(h).start()
        for u in range(KEPT):
            keep_unit(u).wait()
            spread_unit(u)

    pl.when(is_later & ~is_helper)(lambda: launch(0, COUP))

    @pl.when(is_sender)
    def _():
        read_done(BND)
        for j in range(n):
            for q in range(fold):
                bst[j, :, q * rows : (q + 1) * rows] = bnd[
                    q * part : (q + 1) * part, j * rows : (j + 1) * rows
                ]
        own_edge.start()
        for d in range(1, n):
            edge_block(d).start()

    read_done(MERGE)
    read_done(SLOT)
    m_hi, m_lo = halves(mv[...])
    place = (
        lax.broadcasted_iota(jnp.int32, (edges, edges), 0) == slot[...]
    ).astype(jnp.float32).astype(jnp.bfloat16)
    first = (dot_t(m_hi, place).astype(jnp.bfloat16), dot_t(m_lo, place).astype(jnp.bfloat16))

    def flux(which):
        acc = None
        for k in range(DEPTH_CHUNKS):
            if which == 0:
                read_done(LEAF + k)
            read_done(SRC + which * DEPTH_CHUNKS + k)
            cols = slice(k * kd, (k + 1) * kd)
            part = dot_t(sv[which * total // 2 : (which + 1) * total // 2, cols], lv[:, cols])
            acc = part if acc is None else acc + part
        return acc

    offset = 0
    place_of = []
    for level in range(levels):
        half = total >> (level + 1)
        pieces = 2 if level < levels - 1 else 1
        place_of.append((offset, half // pieces, pieces))
        offset += half

    def give(level, y):
        start, size, pieces = place_of[level]
        lsend[start : start + size * pieces, :] = y
        copies = []
        for c in range(pieces):
            at = pl.ds(start + c * size, size)
            copy = remote(
                lsend.at[at, :], lrecv.at[at, :], lev_s.at[0], lev_r.at[level, c], peer(level)
            )
            copies.append(copy)
            if level == 0:
                pl.when(~is_helper)(copy.start)
            else:
                copy.start()
        return copies

    def got(level, c):
        start, size, _ = place_of[level]
        return lrecv[start + c * size : start + (c + 1) * size, :]

    copies = give(0, dot3(flux(0), *first))
    keep = dot3(flux(1), *first)
    read_done(LIFT)
    lift_split[0], lift_split[1] = halves(ltv[...])
    for i in range(2):
        read_done(OWN + i)

    @pl.when(is_helper)
    def _():
        lend(0).wait_recv()
        spread_unit(0)
        for copy in copies:
            copy.start()

    def takes(t):
        take(t, INV)
        pl.when(is_later & ~is_helper)(lambda: take(t, COUP))

        if t > 0:
            pl.when(is_helper)(lambda: take(t - 1, COUP))
            return

        @pl.when(is_helper)
        def _():
            launch(0, COUP)
            share_unit(0)

    def share_kept():
        for u in range(KEPT):
            share_unit(u)

    def keep_first():
        pl.when(~(middle & relayed))(share_kept)
        edges_here(KEPT)
        for u in range(KEPT):
            all_shares(LENT + u).wait_recv()
        for r in range(0, points, block):
            cz[:, r : r + block] = sum(edge_term(u, r) for u in range(KEPT))

    def help_first():
        edges_here(1)
        all_shares(LENT).wait_recv()
        for r in range(0, points, block):
            dst[:, r : r + block] = edge_term(0, r)
        answer(slab - helper0).start()

    taken = 0
    for level in range(levels):
        size = place_of[level][1]
        if taken < chips - 1:
            takes(taken)
            if taken == 0:
                pl.when(relayed & middle)(share_kept)
            taken += 1
        copies[0].wait_recv()
        x = keep[:size] + got(level, 0)
        if level < levels - 1:
            later = give(level + 1, dot3(x, m_hi, m_lo))
            if level == 0:
                pl.when(is_helper)(help_first)
            copies[1].wait_recv()
            keep = dot3(keep[size:] + got(level, 1), m_hi, m_lo)
            if level == levels - 2:
                pl.when(is_first)(keep_first)
            copies = later
    load = dot3(x, lift_split[0], lift_split[1])

    for t in range(taken, chips - 1):
        takes(t)
    pl.when(is_helper)(lambda: take(chips - 2, COUP))

    def prepare(i):
        for r in range(0, points, block):
            hi, lo = halves(full[i, r : r + block, :])
            split[2 * i, r : r + block, :] = hi
            split[2 * i + 1, r : r + block, :] = lo

    def times(x, i):
        if split_ahead:
            return dot3(x, split[2 * i], split[2 * i + 1])
        return jnp.concatenate(
            [dot3(x, *halves(full[i, r : r + block, :])) for r in range(0, points, block)], axis=1
        )

    all_shares(INV).wait_recv()
    if split_ahead:
        prepare(INV)

    @pl.when(is_first)
    def _():
        cz[...] = load - cz[...]
        for h in range(helpers):
            answer(h).wait_recv()
            cz[...] = cz[...] - dv[h]

    @pl.when(is_later)
    def _():
        cz[...] = times(load, INV) if split_ahead else load
        all_shares(COUP).wait_recv()
        if split_ahead:
            prepare(COUP)
            for r in range(0, points, block):
                at = slice(r, r + block)
                joint = product3(
                    split[2 * INV, at, :], split[2 * INV + 1, at, :],
                    split[2 * COUP], split[2 * COUP + 1],
                )
                split[4, at, :], split[5, at, :] = halves(joint)

    chunks = max(1, min(CHAIN_CHUNKS, rows // 16))
    size = rows // chunks

    def hop(c):
        at = pl.ds(c * size, size)
        return remote(
            st.at[at, :], pv.at[at, :], ch_s.at[0], ch_r.at[c],
            lax.rem(slab + 1, n_slab), "slab",
        )

    all_hops = remote(st, pv, ch_s.at[0], ch_r.at[0], lax.rem(slab + 1, n_slab), "slab")
    for c in range(chunks):
        at = slice(c * size, (c + 1) * size)

        @pl.when(is_first)
        def _():
            st[at, :] = times(cz[at, :], INV)

        @pl.when(is_later)
        def _():
            hop(c).wait_recv()
            if split_ahead:
                st[at, :] = cz[at, :] - times(pv[at, :], 2)
            else:
                st[at, :] = times(cz[at, :] - times(pv[at, :], COUP), INV)

        pl.when(slab < n_slab - 1)(hop(c).start)

    turned = st[...].T
    for j in range(n):
        for q in range(fold):
            at = j * width + q * part
            ob[j, :, q * rows : (q + 1) * rows] = turned[at : at + part]
    own = pltpu.make_async_copy(ob.at[me], rb.at[me], o_s.at[1])
    for mask in [m ^ 1 for m in range(n - 1, 1, -1)] + [1]:
        to = flip(mask)
        remote(ob.at[to], rb.at[me], o_s.at[0], o_r.at[0], to).start()
    own.start()

    exchanged = lsend.at[pl.ds(0, offset), :]
    remote(exchanged, exchanged, lev_s.at[0], lev_r.at[0, 0], mate).wait_send()
    all_sent(INV)
    pl.when(is_later)(lambda: all_sent(COUP))

    @pl.when(is_first)
    def _():
        lend_all().wait_send()
        for u in range(KEPT):
            unit_sent(u)


    @pl.when(is_helper)
    def _():
        unit_sent(0)
        answer(0).wait_send()

    pl.when(is_sender)(lambda: edge_blocks(n - 1).wait_send())
    pl.when(slab < n_slab - 1)(all_hops.wait_send)
    own.wait()
    rest = remote(ob.at[pl.ds(0, n - 1)], rb.at[pl.ds(0, n - 1)], o_s.at[0], o_r.at[0], mate)
    rest.wait_recv()
    for j in range(n):
        for q in range(fold):
            out[q * part : (q + 1) * part, j * rows : (j + 1) * rows] = rb[
                j, :, q * rows : (q + 1) * rows
            ]
    rest.wait_send()


def on_device(sources, leaf_ops, edge_slot, merge_ops, lift_ops, coupling, inverse, boundary):
    n, n_slab = lax.axis_size("box"), lax.axis_size("slab")
    total, depth = sources.shape[2:]
    edges = leaf_ops.shape[2]
    points = lift_ops.shape[2]
    rows, width = total // n, points // n
    chips, levels = n // 2, n.bit_length() - 1
    split_ahead = points * points <= 2**20
    f32, bf16 = jnp.float32, jnp.bfloat16
    hbm = pl.BlockSpec(memory_space=pl.ANY)
    dma = lambda *s: pltpu.SemaphoreType.DMA(s)
    vmem = pl.BlockSpec(memory_space=pltpu.VMEM)
    fold = st_fold(rows)
    helpers = min(HELPERS, n_slab - 1)
    units = KEPT + helpers
    result = pl.pallas_call(
        functools.partial(kernel, n, n_slab, split_ahead),
        out_shape=pltpu.VMEM((width, total), f32),
        in_specs=[hbm] * 8,
        out_specs=vmem,
        scratch_shapes=[
            pltpu.VMEM((total, depth), bf16),
            pltpu.VMEM((edges, depth), bf16),
            pltpu.VMEM((edges, edges), f32),
            pltpu.VMEM((points, edges), f32),
            pltpu.VMEM((1, edges), jnp.int32),
            pltpu.VMEM((width, total), f32),
            pltpu.VMEM((2, points, points), f32),
            pltpu.VMEM((KEPT, points, points // units), f32),
            pltpu.VMEM((6, points, points) if split_ahead else (6, 16, 128), bf16),
            pltpu.VMEM((2, points, edges), bf16),
            pltpu.VMEM((total, edges), f32),
            pltpu.VMEM((total, edges), f32),
            pltpu.VMEM((n, width // fold, rows * fold), f32),
            pltpu.VMEM((KEPT * n // units, width // fold, rows * fold), f32),
            pltpu.VMEM((KEPT * points // units, rows), f32),
            pltpu.VMEM((rows, points), f32),
            pltpu.VMEM((helpers, rows, points), f32),
            pltpu.VMEM((rows, points), f32),
            pltpu.VMEM((rows, points), f32),
            pltpu.VMEM((rows, points), f32),
            pltpu.VMEM((n, width // fold, rows * fold), f32),
            pltpu.VMEM((n, width // fold, rows * fold), f32),
            dma(3 * DEPTH_CHUNKS + 6),
            dma(1), dma(levels, 2),
            dma(2, chips + 1), dma(2, chips),
            dma(2 + KEPT), dma(2 + KEPT),
            dma(1), dma(CHAIN_CHUNKS),
            dma(2), dma(1), dma(2), dma(1), dma(2 + 2 * KEPT), dma(1 + helpers + KEPT),
        ],
        compiler_params=pltpu.CompilerParams(collective_id=0, has_side_effects=True),
        name="slab_solve",
    )(
        sources[0, 0], leaf_ops[0, 0], edge_slot[0], merge_ops[0, 0], lift_ops[0, 0],
        coupling[0], inverse[0], boundary.T,
    )
    return result.T[None]


def solution(mesh):
    return jax.shard_map(
        on_device,
        mesh=mesh,
        in_specs=(
            P("slab", "box", None, None),
            P("slab", "box", None, None),
            P("slab", "box", None),
            P("slab", "box", None, None),
            P("slab", "box", None, None),
            P("slab", "box", None),
            P("slab", "box", None),
            P(None, "box"),
        ),
        out_specs=P("slab", None, "box"),
        check_vma=False,
    )
```

```python
import functools

import jax
import jax.numpy as jnp
from jax import lax
from jax.experimental import pallas as pl
from jax.experimental.pallas import tpu as pltpu
from jax.sharding import PartitionSpec as P

MESH = pl.DeviceIdType.MESH
contract_last = (((1,), (1,)), ((), ()))
DEPTH_CHUNKS = 2
CHAIN_CHUNKS = 4
HELPERS = 2
KEPT = 2
OUT_PARTS = 2
COUP, INV, LENT = 0, 1, 2


def dot_t(a, b):
    return lax.dot_general(a, b, contract_last, preferred_element_type=jnp.float32)


def st_fold(rows):
    return max(1, 128 // rows)


def halves(x):
    hi = x.astype(jnp.bfloat16)
    return hi, (x - hi.astype(jnp.float32)).astype(jnp.bfloat16)


def product3(a_hi, a_lo, b_hi, b_lo):
    mm = functools.partial(jnp.dot, preferred_element_type=jnp.float32)
    return mm(a_hi, b_hi) + (mm(a_hi, b_lo) + mm(a_lo, b_hi))


def dot3(x, w_hi, w_lo):
    hi, lo = halves(x)
    if x.shape[0] <= 64:
        both = dot_t(jnp.concatenate([hi, lo], axis=0), w_hi)
        return both[: x.shape[0]] + (dot_t(hi, w_lo) + both[x.shape[0] :])
    return dot_t(hi, w_hi) + (dot_t(hi, w_lo) + dot_t(lo, w_hi))


def kernel(
    n, n_slab, split_ahead,
    src, leaf, slot_in, merge, lift, coup, inv, bnd_in, out,
    sv, lv, mv, ltv, slot, bnd, full, lent, split, lift_split, lsend, lrecv,
    bst, br, bv, dst, dv, pv, st, cz, ob, rb,
    loc, lev_s, lev_r, g_s, g_r, p_s, p_r, ch_s, ch_r, o_s, o_r, b_s, b_r, x_s, x_r,
):
    me, slab = lax.axis_index("box"), lax.axis_index("slab")
    chips = n // 2
    skip_ends = chips == 4
    chip = me // 2
    core = me - 2 * chip
    mate = me + 1 - 2 * core
    rows, points = pv.shape
    width = points // n
    total, edges = lsend.shape
    depth = lv.shape[1]
    kd = depth // DEPTH_CHUNKS
    levels = n.bit_length() - 1
    block = min(points, 256)
    depth_lent = lent.shape[2]
    units = points // depth_lent
    helpers = units - KEPT
    helping = n // units
    helper0 = n_slab - helpers
    is_helper = slab >= helper0
    is_first = slab == 0
    kept = (0, units - 1)
    my_unit = me // helping
    is_sender = (is_first & ((my_unit == kept[0]) | (my_unit == kept[1]))) | (
        is_helper & (my_unit == helpers - slab + helper0)
    )
    edge_at = lax.rem(me, helping) + jnp.where(is_first & (my_unit == kept[1]), helping, 0)
    is_later = slab > 0
    fold = st_fold(rows)
    part = width // fold
    parts, _, out_part, _ = ob.shape
    out_rows = rows // parts
    out_fold = width // out_part

    leaping = is_first | is_helper

    def flip(mask):
        to = me
        for q in range(levels):
            if (mask >> q) & 1:
                to = to + 2**q - 2 ** (q + 1) * lax.rem(me // 2**q, 2)
        return to

    def peer(level):
        mask = 2 ** (levels - 1 - level)
        return me + mask - 2 * mask * lax.rem(me // mask, 2)

    def block_of(position):
        block = 0
        for q in range(levels):
            bit = lax.rem(me // 2**q, 2)
            block = block + 2**q * (bit if (position >> q) & 1 else 1 - bit)
        return block

    def read(k, pairs):
        copies = [pltpu.make_async_copy(a, b, loc.at[k]) for a, b in pairs]
        for c in copies:
            c.start()

    def rows_of(who):
        return pl.ds(pl.multiple_of(who * rows, rows), rows)

    def points_at(i, at):
        return lent.at[i - LENT, at, :] if i >= LENT else full.at[i, at, :]

    def shard_at(i, owner):
        return points_at(i, pl.ds(pl.multiple_of(owner * width, width), width))

    def src_part(which, k):
        return sv.at[pl.ds(which * total // 2, total // 2), pl.ds(k * kd, kd)]

    def leaf_part(k):
        return lv.at[:, pl.ds(k * kd, kd)]

    SLOT, MERGE, LIFT, OWN, BND, SRC = 0, 1, 2, 3, 5, 6
    LEAF = SRC + 2 * DEPTH_CHUNKS
    arrays = {SLOT: slot, MERGE: mv, LIFT: ltv, OWN: shard_at(0, me), OWN + 1: shard_at(1, me), BND: bnd}
    for k in range(DEPTH_CHUNKS):
        arrays[LEAF + k] = leaf_part(k)
        for which in range(2):
            arrays[SRC + which * DEPTH_CHUNKS + k] = src_part(which, k)

    def read_done(k):
        pltpu.make_async_copy(arrays[k], arrays[k], loc.at[k]).wait()

    barrier = pltpu.get_barrier_semaphore()
    for d in range(1, n):
        pl.semaphore_signal(
            barrier, inc=1, device_id={"box": lax.rem(me + d, n)}, device_id_type=MESH
        )
    for d in range(1, n_slab):
        pl.semaphore_signal(
            barrier, inc=1, device_id={"slab": lax.rem(slab + d, n_slab)}, device_id_type=MESH
        )

    pl.when(is_sender)(lambda: read(BND, [(bnd_in, bnd)]))
    read(SLOT, [(slot_in, slot)])
    read(MERGE, [(merge, mv)])
    for which in range(2):
        for k in range(DEPTH_CHUNKS):
            cols = pl.ds(k * kd, kd)
            if which == 0:
                read(LEAF + k, [(leaf.at[:, cols], lv.at[:, cols])])
            read(SRC + which * DEPTH_CHUNKS + k, [
                (src.at[rows_of(block_of(p)), cols], sv.at[pl.ds(p * rows, rows), cols])
                for p in range(which * n // 2, (which + 1) * n // 2)
            ])
    read(LIFT, [(lift, ltv)])
    for i, m in enumerate((coup, inv)):
        read(OWN + i, [(m, shard_at(i, me))])

    def unit_columns(k):
        return pl.ds(k * depth_lent, depth_lent)

    def keep_unit(k):
        return pltpu.make_async_copy(
            coup.at[:, unit_columns(kept[k])], shard_at(LENT + k, me), x_s.at[2 + KEPT + k]
        )

    @pl.when(is_first)
    def _():
        for u in range(KEPT):
            keep_unit(u).start()

    pl.semaphore_wait(barrier, n + n_slab - 2)

    def remote(a, b, s, r, to, axis="box"):
        return pltpu.make_async_remote_copy(
            src_ref=a, dst_ref=b, send_sem=s, recv_sem=r,
            device_id={axis: to}, device_id_type=MESH,
        )

    def line(direction, t, i):
        step = 1 if direction == 0 else -1
        owner = me - 2 * step * t
        ok_chip = chip - step * t
        to_chip = chip + step
        a = (coup, inv)[i] if t == 0 else shard_at(i, owner)
        ok = (ok_chip >= 0) & (ok_chip < chips) & (to_chip >= 0) & (to_chip < chips)
        if skip_ends and t == 1:
            ok = ok & (~leaping | ((ok_chip > 0) & (ok_chip < chips - 1)))
        return ok, remote(
            a, shard_at(i, owner), g_s.at[i, ok_chip + direction], g_r.at[i, ok_chip], me + 2 * step
        )

    def leap(i):
        inward = jnp.where(chip == 0, 2, -2)
        return remote(
            (coup, inv)[i], shard_at(i, me), g_s.at[i, jnp.where(chip == 0, 1, chips - 1)],
            g_r.at[i, chip], me + 2 * inward,
        )

    at_end = leaping & ((chip == 0) | (chip == chips - 1))

    def arrival(direction, t, i):
        step = 1 if direction == 0 else -1
        ref = shard_at(i, me - 2 * step * (t + 1))
        return remote(
            ref, ref, g_s.at[i, chip], g_r.at[i, chip - step * (t + 1)], me - 2 * step
        )

    def came(direction, t):
        owner_chip = chip - (t + 1 if direction == 0 else -t - 1)
        return (owner_chip >= 0) & (owner_chip < chips)

    def share(direction, t, i):
        step = 1 if direction == 0 else -1
        owner = me - 2 * step * (t + 1)
        a = (coup, inv)[i] if t < 0 else shard_at(i, owner)
        return remote(a, shard_at(i, owner), p_s.at[i], p_r.at[i], mate)

    def all_shares(i):
        half = points_at(i, pl.ds(0, points // 2))
        return remote(half, half, p_s.at[i], p_r.at[i], mate)

    def launch(t, i):
        if t == 0:
            share(0, -1, i).start()
        for direction in range(2):
            ok, copy = line(direction, t, i)
            pl.when(ok)(copy.start)

    def take(t, i):
        if t == 0 and skip_ends:
            pl.when(at_end)(leap(i).start)
        for direction in range(2):
            pl.when(came(direction, t))(arrival(direction, t, i).wait_recv)
        if t + 1 < chips - 1:
            launch(t + 1, i)
        for direction in range(2):
            pl.when(came(direction, t))(share(direction, t, i).start)

    def all_here(i):
        all_shares(i).wait_recv()

    def all_sent(i):
        all_shares(i).wait_send()
        if skip_ends:
            pl.when(at_end)(leap(i).wait_send)
        for t in range(chips - 1):
            for direction in range(2):
                ok, copy = line(direction, t, i)
                pl.when(ok)(copy.wait_send)

    def lend(h):
        return remote(
            coup.at[:, unit_columns(helpers - h)], shard_at(LENT, me),
            x_s.at[0], x_r.at[0], helper0 + h, "slab",
        )

    def lend_all():
        columns = pl.ds(depth_lent, helpers * depth_lent)
        lent_columns = coup.at[:, columns]
        here = full.at[COUP, pl.ds(0, width), columns]
        return remote(lent_columns, here, x_s.at[0], x_r.at[0], helper0, "slab")

    def answer(h):
        return remote(dst, dv.at[h], x_s.at[1], x_r.at[1 + h], 0, "slab")

    def spread(u, owner, to):
        shard = shard_at(LENT + u, owner)
        return remote(shard, shard, x_s.at[2 + u], x_r.at[1 + helpers + u], to)

    def spread_rows(u, count):
        some = points_at(LENT + u, pl.ds(0, count * width))
        return remote(some, some, x_s.at[2 + u], x_r.at[1 + helpers + u], mate)

    relayed = is_first & skip_ends
    middle = (chip > 0) & (chip < chips - 1)
    pair = me + 2 - 4 * lax.rem(chip, 2)
    low = chip < chips // 2
    across = me + 2 * (jnp.where(low, chips // 2, chips // 2 - 1) - chip)
    other_half = me + 2 * (jnp.where(low, chips // 2, 0) - chip)

    def lent_share(u, k):
        same = shard_at(LENT + u, lax.rem(me + 2 * k, n))
        return remote(same, same, p_s.at[LENT + u], p_r.at[LENT + u], mate)

    def spread_unit(u):
        lent_share(u, 0).start()

        @pl.when(relayed)
        def _():
            spread(u, me, across).start()
            spread(u, me, pair).start()

        @pl.when(~relayed)
        def _():
            for k in range(1, chips):
                spread(u, me, lax.rem(me + 2 * k, n)).start()

    def share_unit(u):
        spread_rows(u, chips - 1).wait_recv()
        @pl.when(relayed & middle)
        def _():
            for k in range(chips // 2):
                spread(u, other_half + 2 * k, pair).start()

        for k in range(1, chips):
            lent_share(u, k).start()

    def unit_sent(u):
        all_shares(LENT + u).wait_send()
        pl.when(relayed & middle)(lambda: spread_rows(u, chips).wait_send())
        pl.when(relayed & ~middle)(lambda: spread_rows(u, chips // 2).wait_send())
        pl.when(~relayed)(lambda: spread_rows(u, chips - 1).wait_send())

    def edges_here(count):
        @pl.when(is_sender)
        def _():
            own_edge.wait()
            edge_blocks(count * helping - 1).wait_recv()

        @pl.when(~is_sender)
        def _():
            edge_blocks(count * helping).wait_recv()

        for j in range(count * helping):
            for q in range(fold):
                at = j * width + q * part
                bv[at : at + part, :] = br[j, :, q * rows : (q + 1) * rows]

    def edge_term(u, r):
        edge = bv[u * depth_lent : (u + 1) * depth_lent, :].T
        return dot3(edge, *halves(lent[u, r : r + block, :]))

    def edge_block(d):
        to = lax.rem(me + d, n)
        return remote(bst.at[to], br.at[edge_at], b_s.at[0], b_r.at[0], to)

    own_edge = pltpu.make_async_copy(bst.at[me], br.at[edge_at], b_s.at[1])

    def edge_blocks(count):
        blocks = bst.at[pl.ds(0, count)]
        return remote(blocks, blocks, b_s.at[0], b_r.at[0], mate)

    launch(0, INV)

    @pl.when(is_first)
    def _():
        for h in range(helpers):
            lend(h).start()
        for u in range(KEPT):
            keep_unit(u).wait()
            spread_unit(u)

    pl.when(is_later & ~is_helper)(lambda: launch(0, COUP))

    @pl.when(is_sender)
    def _():
        read_done(BND)
        for j in range(n):
            for q in range(fold):
                bst[j, :, q * rows : (q + 1) * rows] = bnd[
                    q * part : (q + 1) * part, j * rows : (j + 1) * rows
                ]
        own_edge.start()
        for d in range(1, n):
            edge_block(d).start()

    read_done(MERGE)
    read_done(SLOT)
    m_hi, m_lo = halves(mv[...])
    place = (
        lax.broadcasted_iota(jnp.int32, (edges, edges), 0) == slot[...]
    ).astype(jnp.float32).astype(jnp.bfloat16)
    first = (dot_t(m_hi, place).astype(jnp.bfloat16), dot_t(m_lo, place).astype(jnp.bfloat16))

    def flux(which):
        acc = None
        for k in range(DEPTH_CHUNKS):
            if which == 0:
                read_done(LEAF + k)
            read_done(SRC + which * DEPTH_CHUNKS + k)
            cols = slice(k * kd, (k + 1) * kd)
            part = dot_t(sv[which * total // 2 : (which + 1) * total // 2, cols], lv[:, cols])
            acc = part if acc is None else acc + part
        return acc

    offset = 0
    place_of = []
    for level in range(levels):
        half = total >> (level + 1)
        pieces = 2 if level < levels - 1 else 1
        place_of.append((offset, half // pieces, pieces))
        offset += half

    def give(level, y):
        start, size, pieces = place_of[level]
        lsend[start : start + size * pieces, :] = y
        copies = []
        for c in range(pieces):
            at = pl.ds(start + c * size, size)
            copy = remote(
                lsend.at[at, :], lrecv.at[at, :], lev_s.at[0], lev_r.at[level, c], peer(level)
            )
            copies.append(copy)
            if level == 0:
                pl.when(~is_helper)(copy.start)
            else:
                copy.start()
        return copies

    def got(level, c):
        start, size, _ = place_of[level]
        return lrecv[start + c * size : start + (c + 1) * size, :]

    copies = give(0, dot3(flux(0), *first))
    keep = dot3(flux(1), *first)
    read_done(LIFT)
    lift_split[0], lift_split[1] = halves(ltv[...])
    for i in range(2):
        read_done(OWN + i)

    @pl.when(is_helper)
    def _():
        lend(0).wait_recv()
        spread_unit(0)
        for copy in copies:
            copy.start()

    def takes(t):
        take(t, INV)
        if t < chips - 2:
            pl.when(is_later & ~is_helper)(lambda: take(t, COUP))

        if t > 0:
            pl.when(is_helper)(lambda: take(t - 1, COUP))
            return

        @pl.when(is_helper)
        def _():
            launch(0, COUP)
            share_unit(0)

    def share_kept():
        for u in range(KEPT):
            share_unit(u)

    def keep_first():
        pl.when(~(middle & relayed))(share_kept)
        edges_here(KEPT)
        for u in range(KEPT):
            all_shares(LENT + u).wait_recv()
        for r in range(0, points, block):
            cz[:, r : r + block] = sum(edge_term(u, r) for u in range(KEPT))

    def help_first():
        edges_here(1)
        all_shares(LENT).wait_recv()
        for r in range(0, points, block):
            dst[:, r : r + block] = edge_term(0, r)
        answer(slab - helper0).start()

    taken = 0
    for level in range(levels):
        size = place_of[level][1]
        if taken < chips - 1:
            takes(taken)
            if taken == 0:
                pl.when(relayed & middle)(share_kept)
            taken += 1
        if level == 0:
            pl.when(is_helper)(help_first)
        copies[0].wait_recv()
        x = keep[:size] + got(level, 0)
        if level < levels - 1:
            later = give(level + 1, dot3(x, m_hi, m_lo))
            copies[1].wait_recv()
            keep = dot3(keep[size:] + got(level, 1), m_hi, m_lo)
            if level == levels - 2:
                pl.when(is_first)(keep_first)
            copies = later
    load = dot3(x, lift_split[0], lift_split[1])

    for t in range(taken, chips - 1):
        takes(t)

    def prepare(i):
        for r in range(0, points, block):
            hi, lo = halves(full[i, r : r + block, :])
            split[2 * i, r : r + block, :] = hi
            split[2 * i + 1, r : r + block, :] = lo

    def times(x, i):
        if split_ahead:
            return dot3(x, split[2 * i], split[2 * i + 1])
        return jnp.concatenate(
            [dot3(x, *halves(full[i, r : r + block, :])) for r in range(0, points, block)], axis=1
        )

    all_shares(INV).wait_recv()
    if split_ahead:
        prepare(INV)

    @pl.when(is_first)
    def _():
        cz[...] = load - cz[...]
        for h in range(helpers):
            answer(h).wait_recv()
            cz[...] = cz[...] - dv[h]

    @pl.when(is_later)
    def _():
        cz[...] = times(load, INV) if split_ahead else load
        take(chips - 2, COUP)
        all_shares(COUP).wait_recv()
        if split_ahead:
            prepare(COUP)
            for r in range(0, points, block):
                at = slice(r, r + block)
                joint = product3(
                    split[2 * INV, at, :], split[2 * INV + 1, at, :],
                    split[2 * COUP], split[2 * COUP + 1],
                )
                split[4, at, :], split[5, at, :] = halves(joint)

    chunks = max(1, min(CHAIN_CHUNKS, rows // 16))
    size = rows // chunks

    def hop(c):
        at = pl.ds(c * size, size)
        return remote(
            st.at[at, :], pv.at[at, :], ch_s.at[0], ch_r.at[c],
            lax.rem(slab + 1, n_slab), "slab",
        )

    def hand_out(p):
        turned = st[p * out_rows : (p + 1) * out_rows, :].T
        for j in range(n):
            for q in range(out_fold):
                at = j * width + q * out_part
                ob[p, j, :, q * out_rows : (q + 1) * out_rows] = turned[at : at + out_part]
        for mask in [m ^ 1 for m in range(n - 1, 1, -1)] + [1]:
            to = flip(mask)
            remote(ob.at[p, to], rb.at[p, me], o_s.at[p], o_r.at[p], to).start()
        own(p).start()

    def own(p):
        return pltpu.make_async_copy(ob.at[p, me], rb.at[p, me], o_s.at[parts + p])

    def out_rest(p):
        some = pl.ds(0, n - 1)
        return remote(ob.at[p, some], rb.at[p, some], o_s.at[p], o_r.at[p], mate)

    all_hops = remote(st, pv, ch_s.at[0], ch_r.at[0], lax.rem(slab + 1, n_slab), "slab")
    for c in range(chunks):
        at = slice(c * size, (c + 1) * size)

        @pl.when(is_first)
        def _():
            st[at, :] = times(cz[at, :], INV)

        @pl.when(is_later)
        def _():
            hop(c).wait_recv()
            if split_ahead:
                st[at, :] = cz[at, :] - times(pv[at, :], 2)
            else:
                st[at, :] = times(cz[at, :] - times(pv[at, :], COUP), INV)

        pl.when(slab < n_slab - 1)(hop(c).start)
        done, odd = divmod((c + 1) * size, out_rows)
        if not odd and done < parts:
            pl.when(slab == n_slab - 1)(functools.partial(hand_out, done - 1))

    for p in range(parts - 1):
        pl.when(slab < n_slab - 1)(functools.partial(hand_out, p))
    hand_out(parts - 1)

    exchanged = lsend.at[pl.ds(0, offset), :]
    remote(exchanged, exchanged, lev_s.at[0], lev_r.at[0, 0], mate).wait_send()
    all_sent(INV)
    pl.when(is_later)(lambda: all_sent(COUP))

    @pl.when(is_first)
    def _():
        lend_all().wait_send()
        for u in range(KEPT):
            unit_sent(u)


    @pl.when(is_helper)
    def _():
        unit_sent(0)
        answer(0).wait_send()

    pl.when(is_sender)(lambda: edge_blocks(n - 1).wait_send())
    pl.when(slab < n_slab - 1)(all_hops.wait_send)
    for p in range(parts):
        own(p).wait()
        out_rest(p).wait_recv()
        for j in range(n):
            for q in range(out_fold):
                at = j * rows + p * out_rows
                out[q * out_part : (q + 1) * out_part, at : at + out_rows] = rb[
                    p, j, :, q * out_rows : (q + 1) * out_rows
                ]
    for p in range(parts):
        out_rest(p).wait_send()


def on_device(sources, leaf_ops, edge_slot, merge_ops, lift_ops, coupling, inverse, boundary):
    n, n_slab = lax.axis_size("box"), lax.axis_size("slab")
    total, depth = sources.shape[2:]
    edges = leaf_ops.shape[2]
    points = lift_ops.shape[2]
    rows, width = total // n, points // n
    chips, levels = n // 2, n.bit_length() - 1
    split_ahead = points * points <= 2**20
    f32, bf16 = jnp.float32, jnp.bfloat16
    hbm = pl.BlockSpec(memory_space=pl.ANY)
    dma = lambda *s: pltpu.SemaphoreType.DMA(s)
    vmem = pl.BlockSpec(memory_space=pltpu.VMEM)
    fold = st_fold(rows)
    parts = OUT_PARTS if rows >= 32 else 1
    out_fold = st_fold(rows // parts)
    helpers = min(HELPERS, n_slab - 1)
    units = KEPT + helpers
    result = pl.pallas_call(
        functools.partial(kernel, n, n_slab, split_ahead),
        out_shape=pltpu.VMEM((width, total), f32),
        in_specs=[hbm] * 8,
        out_specs=vmem,
        scratch_shapes=[
            pltpu.VMEM((total, depth), bf16),
            pltpu.VMEM((edges, depth), bf16),
            pltpu.VMEM((edges, edges), f32),
            pltpu.VMEM((points, edges), f32),
            pltpu.VMEM((1, edges), jnp.int32),
            pltpu.VMEM((width, total), f32),
            pltpu.VMEM((2, points, points), f32),
            pltpu.VMEM((KEPT, points, points // units), f32),
            pltpu.VMEM((6, points, points) if split_ahead else (6, 16, 128), bf16),
            pltpu.VMEM((2, points, edges), bf16),
            pltpu.VMEM((total, edges), f32),
            pltpu.VMEM((total, edges), f32),
            pltpu.VMEM((n, width // fold, rows * fold), f32),
            pltpu.VMEM((KEPT * n // units, width // fold, rows * fold), f32),
            pltpu.VMEM((KEPT * points // units, rows), f32),
            pltpu.VMEM((rows, points), f32),
            pltpu.VMEM((helpers, rows, points), f32),
            pltpu.VMEM((rows, points), f32),
            pltpu.VMEM((rows, points), f32),
            pltpu.VMEM((rows, points), f32),
            pltpu.VMEM((parts, n, width // out_fold, rows // parts * out_fold), f32),
            pltpu.VMEM((parts, n, width // out_fold, rows // parts * out_fold), f32),
            dma(3 * DEPTH_CHUNKS + 6),
            dma(1), dma(levels, 2),
            dma(2, chips + 1), dma(2, chips),
            dma(2 + KEPT), dma(2 + KEPT),
            dma(1), dma(CHAIN_CHUNKS),
            dma(2 * parts), dma(parts), dma(2), dma(1), dma(2 + 2 * KEPT), dma(1 + helpers + KEPT),
        ],
        compiler_params=pltpu.CompilerParams(collective_id=0, has_side_effects=True),
        name="slab_solve",
    )(
        sources[0, 0], leaf_ops[0, 0], edge_slot[0], merge_ops[0, 0], lift_ops[0, 0],
        coupling[0], inverse[0], boundary.T,
    )
    return result.T[None]


def solution(mesh):
    return jax.shard_map(
        on_device,
        mesh=mesh,
        in_specs=(
            P("slab", "box", None, None),
            P("slab", "box", None, None),
            P("slab", "box", None),
            P("slab", "box", None, None),
            P("slab", "box", None, None),
            P("slab", "box", None),
            P("slab", "box", None),
            P(None, "box"),
        ),
        out_specs=P("slab", None, "box"),
        check_vma=False,
    )
```

```python
import functools

import jax
import jax.numpy as jnp
from jax import lax
from jax.experimental import pallas as pl
from jax.experimental.pallas import tpu as pltpu
from jax.sharding import PartitionSpec as P

MESH = pl.DeviceIdType.MESH
contract_last = (((1,), (1,)), ((), ()))
DEPTH_CHUNKS = 2
CHAIN_CHUNKS = 4
HELPERS = 2
KEPT = 2
OUT_PARTS = 2
COUP, INV, LENT = 0, 1, 2


def dot_t(a, b):
    return lax.dot_general(a, b, contract_last, preferred_element_type=jnp.float32)


def st_fold(rows):
    return max(1, 128 // rows)


def halves(x):
    hi = x.astype(jnp.bfloat16)
    return hi, (x - hi.astype(jnp.float32)).astype(jnp.bfloat16)


def product3(a_hi, a_lo, b_hi, b_lo):
    mm = functools.partial(jnp.dot, preferred_element_type=jnp.float32)
    return mm(a_hi, b_hi) + (mm(a_hi, b_lo) + mm(a_lo, b_hi))


def dot3(x, w_hi, w_lo):
    hi, lo = halves(x)
    if x.shape[0] <= 64:
        both = dot_t(jnp.concatenate([hi, lo], axis=0), w_hi)
        return both[: x.shape[0]] + (dot_t(hi, w_lo) + both[x.shape[0] :])
    return dot_t(hi, w_hi) + (dot_t(hi, w_lo) + dot_t(lo, w_hi))


def kernel(
    n, n_slab, split_ahead,
    src, leaf, slot_in, merge, lift, coup, inv, bnd_in, out,
    sv, lv, mv, ltv, slot, bnd, full, lent, split, lift_split, lsend, lrecv,
    bst, br, bv, dst, dv, pv, st, cz, ob, rb,
    loc, lev_s, lev_r, g_s, g_r, p_s, p_r, ch_s, ch_r, o_s, o_r, b_s, b_r, x_s, x_r,
):
    me, slab = lax.axis_index("box"), lax.axis_index("slab")
    chips = n // 2
    skip_ends = chips == 4
    chip = me // 2
    core = me - 2 * chip
    mate = me + 1 - 2 * core
    rows, points = pv.shape
    width = points // n
    total, edges = lsend.shape
    depth = lv.shape[1]
    kd = depth // DEPTH_CHUNKS
    levels = n.bit_length() - 1
    block = min(points, 256)
    depth_lent = lent.shape[2]
    units = points // depth_lent
    helpers = units - KEPT
    helping = n // units
    helper0 = n_slab - helpers
    is_helper = slab >= helper0
    is_first = slab == 0
    kept = (0, units - 1)
    my_unit = me // helping
    is_sender = (is_first & ((my_unit == kept[0]) | (my_unit == kept[1]))) | (
        is_helper & (my_unit == helpers - slab + helper0)
    )
    edge_at = lax.rem(me, helping) + jnp.where(is_first & (my_unit == kept[1]), helping, 0)
    is_later = slab > 0
    fold = st_fold(rows)
    part = width // fold
    parts, _, out_part, _ = ob.shape
    out_rows = rows // parts
    out_fold = width // out_part

    leaping = is_first

    def flip(mask):
        to = me
        for q in range(levels):
            if (mask >> q) & 1:
                to = to + 2**q - 2 ** (q + 1) * lax.rem(me // 2**q, 2)
        return to

    def peer(level):
        mask = 2 ** (levels - 1 - level)
        return me + mask - 2 * mask * lax.rem(me // mask, 2)

    def block_of(position):
        block = 0
        for q in range(levels):
            bit = lax.rem(me // 2**q, 2)
            block = block + 2**q * (bit if (position >> q) & 1 else 1 - bit)
        return block

    def read(k, pairs):
        copies = [pltpu.make_async_copy(a, b, loc.at[k]) for a, b in pairs]
        for c in copies:
            c.start()

    def rows_of(who):
        return pl.ds(pl.multiple_of(who * rows, rows), rows)

    def points_at(i, at):
        return lent.at[i - LENT, at, :] if i >= LENT else full.at[i, at, :]

    def shard_at(i, owner):
        return points_at(i, pl.ds(pl.multiple_of(owner * width, width), width))

    def src_part(which, k):
        return sv.at[pl.ds(which * total // 2, total // 2), pl.ds(k * kd, kd)]

    def leaf_part(k):
        return lv.at[:, pl.ds(k * kd, kd)]

    SLOT, MERGE, LIFT, OWN, BND, SRC = 0, 1, 2, 3, 5, 6
    LEAF = SRC + 2 * DEPTH_CHUNKS
    arrays = {SLOT: slot, MERGE: mv, LIFT: ltv, OWN: shard_at(0, me), OWN + 1: shard_at(1, me), BND: bnd}
    for k in range(DEPTH_CHUNKS):
        arrays[LEAF + k] = leaf_part(k)
        for which in range(2):
            arrays[SRC + which * DEPTH_CHUNKS + k] = src_part(which, k)

    def read_done(k):
        pltpu.make_async_copy(arrays[k], arrays[k], loc.at[k]).wait()

    barrier = pltpu.get_barrier_semaphore()
    for d in range(1, n):
        pl.semaphore_signal(
            barrier, inc=1, device_id={"box": lax.rem(me + d, n)}, device_id_type=MESH
        )
    for d in range(1, n_slab):
        pl.semaphore_signal(
            barrier, inc=1, device_id={"slab": lax.rem(slab + d, n_slab)}, device_id_type=MESH
        )

    pl.when(is_sender)(lambda: read(BND, [(bnd_in, bnd)]))
    read(SLOT, [(slot_in, slot)])
    read(MERGE, [(merge, mv)])
    for which in range(2):
        for k in range(DEPTH_CHUNKS):
            cols = pl.ds(k * kd, kd)
            if which == 0:
                read(LEAF + k, [(leaf.at[:, cols], lv.at[:, cols])])
            read(SRC + which * DEPTH_CHUNKS + k, [
                (src.at[rows_of(block_of(p)), cols], sv.at[pl.ds(p * rows, rows), cols])
                for p in range(which * n // 2, (which + 1) * n // 2)
            ])
    read(LIFT, [(lift, ltv)])
    for i, m in enumerate((coup, inv)):
        read(OWN + i, [(m, shard_at(i, me))])

    def unit_columns(k):
        return pl.ds(k * depth_lent, depth_lent)

    def keep_unit(k):
        return pltpu.make_async_copy(
            coup.at[:, unit_columns(kept[k])], shard_at(LENT + k, me), x_s.at[2 + KEPT + k]
        )

    @pl.when(is_first)
    def _():
        for u in range(KEPT):
            keep_unit(u).start()

    pl.semaphore_wait(barrier, n + n_slab - 2)

    def remote(a, b, s, r, to, axis="box"):
        return pltpu.make_async_remote_copy(
            src_ref=a, dst_ref=b, send_sem=s, recv_sem=r,
            device_id={axis: to}, device_id_type=MESH,
        )

    def line(direction, t, i):
        step = 1 if direction == 0 else -1
        owner = me - 2 * step * t
        ok_chip = chip - step * t
        to_chip = chip + step
        a = (coup, inv)[i] if t == 0 else shard_at(i, owner)
        ok = (ok_chip >= 0) & (ok_chip < chips) & (to_chip >= 0) & (to_chip < chips)
        if skip_ends and t == 1:
            ok = ok & (~leaping | ((ok_chip > 0) & (ok_chip < chips - 1)))
        return ok, remote(
            a, shard_at(i, owner), g_s.at[i, ok_chip + direction], g_r.at[i, ok_chip], me + 2 * step
        )

    def leap(i):
        inward = jnp.where(chip == 0, 2, -2)
        return remote(
            (coup, inv)[i], shard_at(i, me), g_s.at[i, jnp.where(chip == 0, 1, chips - 1)],
            g_r.at[i, chip], me + 2 * inward,
        )

    at_end = leaping & ((chip == 0) | (chip == chips - 1))

    def arrival(direction, t, i):
        step = 1 if direction == 0 else -1
        ref = shard_at(i, me - 2 * step * (t + 1))
        return remote(
            ref, ref, g_s.at[i, chip], g_r.at[i, chip - step * (t + 1)], me - 2 * step
        )

    def came(direction, t):
        owner_chip = chip - (t + 1 if direction == 0 else -t - 1)
        return (owner_chip >= 0) & (owner_chip < chips)

    def share(direction, t, i):
        step = 1 if direction == 0 else -1
        owner = me - 2 * step * (t + 1)
        a = (coup, inv)[i] if t < 0 else shard_at(i, owner)
        return remote(a, shard_at(i, owner), p_s.at[i], p_r.at[i], mate)

    def all_shares(i):
        half = points_at(i, pl.ds(0, points // 2))
        return remote(half, half, p_s.at[i], p_r.at[i], mate)

    def launch(t, i):
        if t == 0:
            share(0, -1, i).start()
        for direction in range(2):
            ok, copy = line(direction, t, i)
            pl.when(ok)(copy.start)

    def take(t, i):
        if t == 0 and skip_ends:
            pl.when(at_end)(leap(i).start)
        for direction in range(2):
            pl.when(came(direction, t))(arrival(direction, t, i).wait_recv)
        if t + 1 < chips - 1:
            launch(t + 1, i)
        for direction in range(2):
            pl.when(came(direction, t))(share(direction, t, i).start)

    def all_here(i):
        all_shares(i).wait_recv()

    def all_sent(i):
        all_shares(i).wait_send()
        if skip_ends:
            pl.when(at_end)(leap(i).wait_send)
        for t in range(chips - 1):
            for direction in range(2):
                ok, copy = line(direction, t, i)
                pl.when(ok)(copy.wait_send)

    def lend(h):
        return remote(
            coup.at[:, unit_columns(helpers - h)], shard_at(LENT, me),
            x_s.at[0], x_r.at[0], helper0 + h, "slab",
        )

    def lend_all():
        columns = pl.ds(depth_lent, helpers * depth_lent)
        lent_columns = coup.at[:, columns]
        here = full.at[COUP, pl.ds(0, width), columns]
        return remote(lent_columns, here, x_s.at[0], x_r.at[0], helper0, "slab")

    def answer(h):
        return remote(dst, dv.at[h], x_s.at[1], x_r.at[1 + h], 0, "slab")

    def spread(u, owner, to):
        shard = shard_at(LENT + u, owner)
        return remote(shard, shard, x_s.at[2 + u], x_r.at[1 + helpers + u], to)

    def spread_rows(u, count):
        some = points_at(LENT + u, pl.ds(0, count * width))
        return remote(some, some, x_s.at[2 + u], x_r.at[1 + helpers + u], mate)

    relayed = is_first & skip_ends
    middle = (chip > 0) & (chip < chips - 1)
    pair = me + 2 - 4 * lax.rem(chip, 2)
    low = chip < chips // 2
    across = me + 2 * (jnp.where(low, chips // 2, chips // 2 - 1) - chip)
    other_half = me + 2 * (jnp.where(low, chips // 2, 0) - chip)

    def lent_share(u, k):
        same = shard_at(LENT + u, lax.rem(me + 2 * k, n))
        return remote(same, same, p_s.at[LENT + u], p_r.at[LENT + u], mate)

    def spread_unit(u):
        lent_share(u, 0).start()

        @pl.when(relayed)
        def _():
            spread(u, me, across).start()
            spread(u, me, pair).start()

        @pl.when(~relayed)
        def _():
            for k in range(1, chips):
                spread(u, me, lax.rem(me + 2 * k, n)).start()

    def share_unit(u):
        spread_rows(u, chips - 1).wait_recv()
        @pl.when(relayed & middle)
        def _():
            for k in range(chips // 2):
                spread(u, other_half + 2 * k, pair).start()

        for k in range(1, chips):
            lent_share(u, k).start()

    def unit_sent(u):
        all_shares(LENT + u).wait_send()
        pl.when(relayed & middle)(lambda: spread_rows(u, chips).wait_send())
        pl.when(relayed & ~middle)(lambda: spread_rows(u, chips // 2).wait_send())
        pl.when(~relayed)(lambda: spread_rows(u, chips - 1).wait_send())

    def edges_here(count):
        @pl.when(is_sender)
        def _():
            own_edge.wait()
            edge_blocks(count * helping - 1).wait_recv()

        @pl.when(~is_sender)
        def _():
            edge_blocks(count * helping).wait_recv()

        for j in range(count * helping):
            for q in range(fold):
                at = j * width + q * part
                bv[at : at + part, :] = br[j, :, q * rows : (q + 1) * rows]

    def edge_term(u, r):
        edge = bv[u * depth_lent : (u + 1) * depth_lent, :].T
        return dot3(edge, *halves(lent[u, r : r + block, :]))

    def edge_block(d):
        to = lax.rem(me + d, n)
        return remote(bst.at[to], br.at[edge_at], b_s.at[0], b_r.at[0], to)

    own_edge = pltpu.make_async_copy(bst.at[me], br.at[edge_at], b_s.at[1])

    def edge_blocks(count):
        blocks = bst.at[pl.ds(0, count)]
        return remote(blocks, blocks, b_s.at[0], b_r.at[0], mate)

    launch(0, INV)

    @pl.when(is_first)
    def _():
        for h in range(helpers):
            lend(h).start()
        for u in range(KEPT):
            keep_unit(u).wait()
            spread_unit(u)

    pl.when(is_later & ~is_helper)(lambda: launch(0, COUP))

    @pl.when(is_sender)
    def _():
        read_done(BND)
        for j in range(n):
            for q in range(fold):
                bst[j, :, q * rows : (q + 1) * rows] = bnd[
                    q * part : (q + 1) * part, j * rows : (j + 1) * rows
                ]
        own_edge.start()
        for d in range(1, n):
            edge_block(d).start()

    read_done(MERGE)
    read_done(SLOT)
    m_hi, m_lo = halves(mv[...])
    place = (
        lax.broadcasted_iota(jnp.int32, (edges, edges), 0) == slot[...]
    ).astype(jnp.float32).astype(jnp.bfloat16)
    first = (dot_t(m_hi, place).astype(jnp.bfloat16), dot_t(m_lo, place).astype(jnp.bfloat16))

    def flux(which):
        acc = None
        for k in range(DEPTH_CHUNKS):
            if which == 0:
                read_done(LEAF + k)
            read_done(SRC + which * DEPTH_CHUNKS + k)
            cols = slice(k * kd, (k + 1) * kd)
            part = dot_t(sv[which * total // 2 : (which + 1) * total // 2, cols], lv[:, cols])
            acc = part if acc is None else acc + part
        return acc

    offset = 0
    place_of = []
    for level in range(levels):
        half = total >> (level + 1)
        pieces = 2 if level < levels - 1 else 1
        place_of.append((offset, half // pieces, pieces))
        offset += half

    def give(level, y):
        start, size, pieces = place_of[level]
        lsend[start : start + size * pieces, :] = y
        copies = []
        for c in range(pieces):
            at = pl.ds(start + c * size, size)
            copy = remote(
                lsend.at[at, :], lrecv.at[at, :], lev_s.at[0], lev_r.at[level, c], peer(level)
            )
            copies.append(copy)
            if level == 0:
                pl.when(~is_helper)(copy.start)
            else:
                copy.start()
        return copies

    def got(level, c):
        start, size, _ = place_of[level]
        return lrecv[start + c * size : start + (c + 1) * size, :]

    copies = give(0, dot3(flux(0), *first))
    keep = dot3(flux(1), *first)
    read_done(LIFT)
    lift_split[0], lift_split[1] = halves(ltv[...])
    for i in range(2):
        read_done(OWN + i)

    @pl.when(is_helper)
    def _():
        lend(0).wait_recv()
        spread_unit(0)
        for copy in copies:
            copy.start()

    def takes(t):
        take(t, INV)
        if t < chips - 2:
            pl.when(is_later & ~is_helper)(lambda: take(t, COUP))

        if t > 0:
            pl.when(is_helper)(lambda: take(t - 1, COUP))
            return

        @pl.when(is_helper)
        def _():
            launch(0, COUP)
            share_unit(0)

    def share_kept():
        for u in range(KEPT):
            share_unit(u)

    def kept_term():
        edges_here(KEPT)
        for u in range(KEPT):
            all_shares(LENT + u).wait_recv()
        for r in range(0, points, block):
            cz[:, r : r + block] = sum(edge_term(u, r) for u in range(KEPT))

    def keep_first():
        share_kept()
        kept_term()

    def help_first():
        edges_here(1)
        all_shares(LENT).wait_recv()
        for r in range(0, points, block):
            dst[:, r : r + block] = edge_term(0, r)
        answer(slab - helper0).start()

    taken = 0
    for level in range(levels):
        size = place_of[level][1]
        if taken < chips - 1:
            takes(taken)
            if taken == 0:
                pl.when(relayed & middle)(share_kept)
            taken += 1
        if level == 0:
            pl.when(is_helper)(help_first)
        if level == 1:
            pl.when(relayed & middle)(kept_term)
        copies[0].wait_recv()
        x = keep[:size] + got(level, 0)
        if level < levels - 1:
            later = give(level + 1, dot3(x, m_hi, m_lo))
            copies[1].wait_recv()
            keep = dot3(keep[size:] + got(level, 1), m_hi, m_lo)
            if level == levels - 2:
                pl.when(is_first & ~(middle & relayed))(keep_first)
            copies = later
    load = dot3(x, lift_split[0], lift_split[1])

    for t in range(taken, chips - 1):
        takes(t)

    def prepare(i):
        for r in range(0, points, block):
            hi, lo = halves(full[i, r : r + block, :])
            split[2 * i, r : r + block, :] = hi
            split[2 * i + 1, r : r + block, :] = lo

    def times(x, i):
        if split_ahead:
            return dot3(x, split[2 * i], split[2 * i + 1])
        return jnp.concatenate(
            [dot3(x, *halves(full[i, r : r + block, :])) for r in range(0, points, block)], axis=1
        )

    all_shares(INV).wait_recv()
    if split_ahead:
        prepare(INV)

    @pl.when(is_first)
    def _():
        cz[...] = load - cz[...]
        for h in range(helpers):
            answer(h).wait_recv()
            cz[...] = cz[...] - dv[h]

    @pl.when(is_later)
    def _():
        cz[...] = times(load, INV) if split_ahead else load
        take(chips - 2, COUP)
        all_shares(COUP).wait_recv()
        if split_ahead:
            prepare(COUP)
            for r in range(0, points, block):
                at = slice(r, r + block)
                joint = product3(
                    split[2 * INV, at, :], split[2 * INV + 1, at, :],
                    split[2 * COUP], split[2 * COUP + 1],
                )
                split[4, at, :], split[5, at, :] = halves(joint)

    chunks = max(1, min(CHAIN_CHUNKS, rows // 16))
    size = rows // chunks

    def hop(c):
        at = pl.ds(c * size, size)
        return remote(
            st.at[at, :], pv.at[at, :], ch_s.at[0], ch_r.at[c],
            lax.rem(slab + 1, n_slab), "slab",
        )

    def hand_out(p):
        turned = st[p * out_rows : (p + 1) * out_rows, :].T
        for j in range(n):
            for q in range(out_fold):
                at = j * width + q * out_part
                ob[p, j, :, q * out_rows : (q + 1) * out_rows] = turned[at : at + out_part]
        for k in range(n - 1):
            to = k + jnp.where(me <= k, 1, 0)
            remote(ob.at[p, to], rb.at[p, me], o_s.at[p], o_r.at[p], to).start()
        own(p).start()

    def own(p):
        return pltpu.make_async_copy(ob.at[p, me], rb.at[p, me], o_s.at[parts + p])

    def out_rest(p):
        some = pl.ds(0, n - 1)
        return remote(ob.at[p, some], rb.at[p, some], o_s.at[p], o_r.at[p], mate)

    all_hops = remote(st, pv, ch_s.at[0], ch_r.at[0], lax.rem(slab + 1, n_slab), "slab")
    for c in range(chunks):
        at = slice(c * size, (c + 1) * size)

        @pl.when(is_first)
        def _():
            st[at, :] = times(cz[at, :], INV)

        @pl.when(is_later)
        def _():
            hop(c).wait_recv()
            if split_ahead:
                st[at, :] = cz[at, :] - times(pv[at, :], 2)
            else:
                st[at, :] = times(cz[at, :] - times(pv[at, :], COUP), INV)

        pl.when(slab < n_slab - 1)(hop(c).start)
        done, odd = divmod((c + 1) * size, out_rows)
        if not odd and done < parts:
            pl.when(slab == n_slab - 1)(functools.partial(hand_out, done - 1))

    for p in range(parts - 1):
        pl.when(slab < n_slab - 1)(functools.partial(hand_out, p))
    hand_out(parts - 1)

    exchanged = lsend.at[pl.ds(0, offset), :]
    remote(exchanged, exchanged, lev_s.at[0], lev_r.at[0, 0], mate).wait_send()
    all_sent(INV)
    pl.when(is_later)(lambda: all_sent(COUP))

    @pl.when(is_first)
    def _():
        lend_all().wait_send()
        for u in range(KEPT):
            unit_sent(u)


    @pl.when(is_helper)
    def _():
        unit_sent(0)
        answer(0).wait_send()

    pl.when(is_sender)(lambda: edge_blocks(n - 1).wait_send())
    pl.when(slab < n_slab - 1)(all_hops.wait_send)
    for p in range(parts):
        own(p).wait()
        out_rest(p).wait_recv()
        for j in range(n):
            for q in range(out_fold):
                at = j * rows + p * out_rows
                out[q * out_part : (q + 1) * out_part, at : at + out_rows] = rb[
                    p, j, :, q * out_rows : (q + 1) * out_rows
                ]
    for p in range(parts):
        out_rest(p).wait_send()


def on_device(sources, leaf_ops, edge_slot, merge_ops, lift_ops, coupling, inverse, boundary):
    n, n_slab = lax.axis_size("box"), lax.axis_size("slab")
    total, depth = sources.shape[2:]
    edges = leaf_ops.shape[2]
    points = lift_ops.shape[2]
    rows, width = total // n, points // n
    chips, levels = n // 2, n.bit_length() - 1
    split_ahead = points * points <= 2**20
    f32, bf16 = jnp.float32, jnp.bfloat16
    hbm = pl.BlockSpec(memory_space=pl.ANY)
    dma = lambda *s: pltpu.SemaphoreType.DMA(s)
    vmem = pl.BlockSpec(memory_space=pltpu.VMEM)
    fold = st_fold(rows)
    parts = OUT_PARTS if rows >= 32 else 1
    out_fold = st_fold(rows // parts)
    helpers = min(HELPERS, n_slab - 1)
    units = KEPT + helpers
    result = pl.pallas_call(
        functools.partial(kernel, n, n_slab, split_ahead),
        out_shape=pltpu.VMEM((width, total), f32),
        in_specs=[hbm] * 8,
        out_specs=vmem,
        scratch_shapes=[
            pltpu.VMEM((total, depth), bf16),
            pltpu.VMEM((edges, depth), bf16),
            pltpu.VMEM((edges, edges), f32),
            pltpu.VMEM((points, edges), f32),
            pltpu.VMEM((1, edges), jnp.int32),
            pltpu.VMEM((width, total), f32),
            pltpu.VMEM((2, points, points), f32),
            pltpu.VMEM((KEPT, points, points // units), f32),
            pltpu.VMEM((6, points, points) if split_ahead else (6, 16, 128), bf16),
            pltpu.VMEM((2, points, edges), bf16),
            pltpu.VMEM((total, edges), f32),
            pltpu.VMEM((total, edges), f32),
            pltpu.VMEM((n, width // fold, rows * fold), f32),
            pltpu.VMEM((KEPT * n // units, width // fold, rows * fold), f32),
            pltpu.VMEM((KEPT * points // units, rows), f32),
            pltpu.VMEM((rows, points), f32),
            pltpu.VMEM((helpers, rows, points), f32),
            pltpu.VMEM((rows, points), f32),
            pltpu.VMEM((rows, points), f32),
            pltpu.VMEM((rows, points), f32),
            pltpu.VMEM((parts, n, width // out_fold, rows // parts * out_fold), f32),
            pltpu.VMEM((parts, n, width // out_fold, rows // parts * out_fold), f32),
            dma(3 * DEPTH_CHUNKS + 6),
            dma(1), dma(levels, 2),
            dma(2, chips + 1), dma(2, chips),
            dma(2 + KEPT), dma(2 + KEPT),
            dma(1), dma(CHAIN_CHUNKS),
            dma(2 * parts), dma(parts), dma(2), dma(1), dma(2 + 2 * KEPT), dma(1 + helpers + KEPT),
        ],
        compiler_params=pltpu.CompilerParams(collective_id=0, has_side_effects=True),
        name="slab_solve",
    )(
        sources[0, 0], leaf_ops[0, 0], edge_slot[0], merge_ops[0, 0], lift_ops[0, 0],
        coupling[0], inverse[0], boundary.T,
    )
    return result.T[None]


def solution(mesh):
    return jax.shard_map(
        on_device,
        mesh=mesh,
        in_specs=(
            P("slab", "box", None, None),
            P("slab", "box", None, None),
            P("slab", "box", None),
            P("slab", "box", None, None),
            P("slab", "box", None, None),
            P("slab", "box", None),
            P("slab", "box", None),
            P(None, "box"),
        ),
        out_specs=P("slab", None, "box"),
        check_vma=False,
    )
```

```python
import functools

import jax
import jax.numpy as jnp
from jax import lax
from jax.experimental import pallas as pl
from jax.experimental.pallas import tpu as pltpu
from jax.sharding import PartitionSpec as P

MESH = pl.DeviceIdType.MESH
contract_last = (((1,), (1,)), ((), ()))
DEPTH_CHUNKS = 1
CHAIN_CHUNKS = 4
HELPERS = 2
KEPT = 2
OUT_PARTS = 2
COUP, INV, LENT = 0, 1, 2


def dot_t(a, b):
    return lax.dot_general(a, b, contract_last, preferred_element_type=jnp.float32)


def st_fold(rows):
    return max(1, 128 // rows)


def halves(x):
    hi = x.astype(jnp.bfloat16)
    return hi, (x - hi.astype(jnp.float32)).astype(jnp.bfloat16)


def product3(a_hi, a_lo, b_hi, b_lo):
    mm = functools.partial(jnp.dot, preferred_element_type=jnp.float32)
    return mm(a_hi, b_hi) + (mm(a_hi, b_lo) + mm(a_lo, b_hi))


def dot3(x, w_hi, w_lo):
    hi, lo = halves(x)
    if x.shape[0] <= 64:
        both = dot_t(jnp.concatenate([hi, lo], axis=0), w_hi)
        return both[: x.shape[0]] + (dot_t(hi, w_lo) + both[x.shape[0] :])
    return dot_t(hi, w_hi) + (dot_t(hi, w_lo) + dot_t(lo, w_hi))


def kernel(
    n, n_slab, split_ahead,
    src, leaf, slot_in, merge, lift, coup, inv, bnd_in, out,
    sv, lv, mv, ltv, slot, bnd, full, lent, split, lift_split, lsend, lrecv,
    bst, br, bv, dst, dv, pv, st, cz, ob, rb,
    loc, lev_s, lev_r, g_s, g_r, p_s, p_r, ch_s, ch_r, o_s, o_r, b_s, b_r, x_s, x_r,
):
    me, slab = lax.axis_index("box"), lax.axis_index("slab")
    chips = n // 2
    skip_ends = chips == 4
    chip = me // 2
    core = me - 2 * chip
    mate = me + 1 - 2 * core
    rows, points = pv.shape
    width = points // n
    total, edges = lsend.shape
    depth = lv.shape[1]
    kd = depth // DEPTH_CHUNKS
    levels = n.bit_length() - 1
    block = min(points, 256)
    depth_lent = lent.shape[2]
    units = points // depth_lent
    helpers = units - KEPT
    helping = n // units
    helper0 = n_slab - helpers
    is_helper = slab >= helper0
    is_first = slab == 0
    kept = (0, units - 1)
    my_unit = me // helping
    is_sender = (is_first & ((my_unit == kept[0]) | (my_unit == kept[1]))) | (
        is_helper & (my_unit == helpers - slab + helper0)
    )
    edge_at = lax.rem(me, helping) + jnp.where(is_first & (my_unit == kept[1]), helping, 0)
    is_later = slab > 0
    fold = st_fold(rows)
    part = width // fold
    parts, _, out_part, _ = ob.shape
    out_rows = rows // parts
    out_fold = width // out_part

    leaping = is_first | is_helper

    def flip(mask):
        to = me
        for q in range(levels):
            if (mask >> q) & 1:
                to = to + 2**q - 2 ** (q + 1) * lax.rem(me // 2**q, 2)
        return to

    def peer(level):
        mask = 2 ** (levels - 1 - level)
        return me + mask - 2 * mask * lax.rem(me // mask, 2)

    def block_of(position):
        block = 0
        for q in range(levels):
            bit = lax.rem(me // 2**q, 2)
            block = block + 2**q * (bit if (position >> q) & 1 else 1 - bit)
        return block

    def read(k, pairs):
        copies = [pltpu.make_async_copy(a, b, loc.at[k]) for a, b in pairs]
        for c in copies:
            c.start()

    def rows_of(who):
        return pl.ds(pl.multiple_of(who * rows, rows), rows)

    def points_at(i, at):
        return lent.at[i - LENT, at, :] if i >= LENT else full.at[i, at, :]

    def shard_at(i, owner):
        return points_at(i, pl.ds(pl.multiple_of(owner * width, width), width))

    def src_part(which, k):
        return sv.at[pl.ds(which * total // 2, total // 2), pl.ds(k * kd, kd)]

    def leaf_part(k):
        return lv.at[:, pl.ds(k * kd, kd)]

    SLOT, MERGE, LIFT, OWN, BND, SRC = 0, 1, 2, 3, 5, 6
    LEAF = SRC + 2 * DEPTH_CHUNKS
    arrays = {SLOT: slot, MERGE: mv, LIFT: ltv, OWN: shard_at(0, me), OWN + 1: shard_at(1, me), BND: bnd}
    for k in range(DEPTH_CHUNKS):
        arrays[LEAF + k] = leaf_part(k)
        for which in range(2):
            arrays[SRC + which * DEPTH_CHUNKS + k] = src_part(which, k)

    def read_done(k):
        pltpu.make_async_copy(arrays[k], arrays[k], loc.at[k]).wait()

    barrier = pltpu.get_barrier_semaphore()
    for d in range(1, n):
        pl.semaphore_signal(
            barrier, inc=1, device_id={"box": lax.rem(me + d, n)}, device_id_type=MESH
        )
    for d in range(1, n_slab):
        pl.semaphore_signal(
            barrier, inc=1, device_id={"slab": lax.rem(slab + d, n_slab)}, device_id_type=MESH
        )

    pl.when(is_sender)(lambda: read(BND, [(bnd_in, bnd)]))
    read(SLOT, [(slot_in, slot)])
    read(MERGE, [(merge, mv)])
    for which in range(2):
        for k in range(DEPTH_CHUNKS):
            cols = pl.ds(k * kd, kd)
            if which == 0:
                read(LEAF + k, [(leaf.at[:, cols], lv.at[:, cols])])
            read(SRC + which * DEPTH_CHUNKS + k, [
                (src.at[rows_of(block_of(p)), cols], sv.at[pl.ds(p * rows, rows), cols])
                for p in range(which * n // 2, (which + 1) * n // 2)
            ])
    read(LIFT, [(lift, ltv)])
    for i, m in enumerate((coup, inv)):
        read(OWN + i, [(m, shard_at(i, me))])

    def unit_columns(k):
        return pl.ds(k * depth_lent, depth_lent)

    def keep_unit(k):
        return pltpu.make_async_copy(
            coup.at[:, unit_columns(kept[k])], shard_at(LENT + k, me), x_s.at[2 + KEPT + k]
        )

    @pl.when(is_first)
    def _():
        for u in range(KEPT):
            keep_unit(u).start()

    pl.semaphore_wait(barrier, n + n_slab - 2)

    def remote(a, b, s, r, to, axis="box"):
        return pltpu.make_async_remote_copy(
            src_ref=a, dst_ref=b, send_sem=s, recv_sem=r,
            device_id={axis: to}, device_id_type=MESH,
        )

    def line(direction, t, i):
        step = 1 if direction == 0 else -1
        owner = me - 2 * step * t
        ok_chip = chip - step * t
        to_chip = chip + step
        a = (coup, inv)[i] if t == 0 else shard_at(i, owner)
        ok = (ok_chip >= 0) & (ok_chip < chips) & (to_chip >= 0) & (to_chip < chips)
        if skip_ends and t == 1:
            ok = ok & (~leaping | ((ok_chip > 0) & (ok_chip < chips - 1)))
        return ok, remote(
            a, shard_at(i, owner), g_s.at[i, ok_chip + direction], g_r.at[i, ok_chip], me + 2 * step
        )

    def leap(i):
        inward = jnp.where(chip == 0, 2, -2)
        return remote(
            (coup, inv)[i], shard_at(i, me), g_s.at[i, jnp.where(chip == 0, 1, chips - 1)],
            g_r.at[i, chip], me + 2 * inward,
        )

    at_end = leaping & ((chip == 0) | (chip == chips - 1))

    def arrival(direction, t, i):
        step = 1 if direction == 0 else -1
        ref = shard_at(i, me - 2 * step * (t + 1))
        return remote(
            ref, ref, g_s.at[i, chip], g_r.at[i, chip - step * (t + 1)], me - 2 * step
        )

    def came(direction, t):
        owner_chip = chip - (t + 1 if direction == 0 else -t - 1)
        return (owner_chip >= 0) & (owner_chip < chips)

    def share(direction, t, i):
        step = 1 if direction == 0 else -1
        owner = me - 2 * step * (t + 1)
        a = (coup, inv)[i] if t < 0 else shard_at(i, owner)
        return remote(a, shard_at(i, owner), p_s.at[i], p_r.at[i], mate)

    def all_shares(i):
        half = points_at(i, pl.ds(0, points // 2))
        return remote(half, half, p_s.at[i], p_r.at[i], mate)

    def launch(t, i):
        if t == 0:
            share(0, -1, i).start()
        for direction in range(2):
            ok, copy = line(direction, t, i)
            pl.when(ok)(copy.start)

    def take(t, i):
        if t == 0 and skip_ends:
            pl.when(at_end)(leap(i).start)
        for direction in range(2):
            pl.when(came(direction, t))(arrival(direction, t, i).wait_recv)
        if t + 1 < chips - 1:
            launch(t + 1, i)
        for direction in range(2):
            pl.when(came(direction, t))(share(direction, t, i).start)

    def all_here(i):
        all_shares(i).wait_recv()

    def all_sent(i):
        all_shares(i).wait_send()
        if skip_ends:
            pl.when(at_end)(leap(i).wait_send)
        for t in range(chips - 1):
            for direction in range(2):
                ok, copy = line(direction, t, i)
                pl.when(ok)(copy.wait_send)

    def lend(h):
        return remote(
            coup.at[:, unit_columns(helpers - h)], shard_at(LENT, me),
            x_s.at[0], x_r.at[0], helper0 + h, "slab",
        )

    def lend_all():
        columns = pl.ds(depth_lent, helpers * depth_lent)
        lent_columns = coup.at[:, columns]
        here = full.at[COUP, pl.ds(0, width), columns]
        return remote(lent_columns, here, x_s.at[0], x_r.at[0], helper0, "slab")

    def answer(h):
        return remote(dst, dv.at[h], x_s.at[1], x_r.at[1 + h], 0, "slab")

    def spread(u, owner, to):
        shard = shard_at(LENT + u, owner)
        return remote(shard, shard, x_s.at[2 + u], x_r.at[1 + helpers + u], to)

    def spread_rows(u, count):
        some = points_at(LENT + u, pl.ds(0, count * width))
        return remote(some, some, x_s.at[2 + u], x_r.at[1 + helpers + u], mate)

    relayed = is_first & skip_ends
    middle = (chip > 0) & (chip < chips - 1)
    pair = me + 2 - 4 * lax.rem(chip, 2)
    low = chip < chips // 2
    across = me + 2 * (jnp.where(low, chips // 2, chips // 2 - 1) - chip)
    other_half = me + 2 * (jnp.where(low, chips // 2, 0) - chip)

    def lent_share(u, k):
        same = shard_at(LENT + u, lax.rem(me + 2 * k, n))
        return remote(same, same, p_s.at[LENT + u], p_r.at[LENT + u], mate)

    def spread_unit(u):
        lent_share(u, 0).start()

        @pl.when(relayed)
        def _():
            spread(u, me, across).start()
            spread(u, me, pair).start()

        @pl.when(~relayed)
        def _():
            for k in range(1, chips):
                spread(u, me, lax.rem(me + 2 * k, n)).start()

    def share_unit(u):
        spread_rows(u, chips - 1).wait_recv()
        @pl.when(relayed & middle)
        def _():
            for k in range(chips // 2):
                spread(u, other_half + 2 * k, pair).start()

        for k in range(1, chips):
            lent_share(u, k).start()

    def unit_sent(u):
        all_shares(LENT + u).wait_send()
        pl.when(relayed & middle)(lambda: spread_rows(u, chips).wait_send())
        pl.when(relayed & ~middle)(lambda: spread_rows(u, chips // 2).wait_send())
        pl.when(~relayed)(lambda: spread_rows(u, chips - 1).wait_send())

    def edges_here(count):
        @pl.when(is_sender)
        def _():
            own_edge.wait()
            edge_blocks(count * helping - 1).wait_recv()

        @pl.when(~is_sender)
        def _():
            edge_blocks(count * helping).wait_recv()

        for j in range(count * helping):
            for q in range(fold):
                at = j * width + q * part
                bv[at : at + part, :] = br[j, :, q * rows : (q + 1) * rows]

    def edge_term(u, r):
        edge = bv[u * depth_lent : (u + 1) * depth_lent, :].T
        return dot3(edge, *halves(lent[u, r : r + block, :]))

    def edge_block(d):
        to = lax.rem(me + d, n)
        return remote(bst.at[to], br.at[edge_at], b_s.at[0], b_r.at[0], to)

    own_edge = pltpu.make_async_copy(bst.at[me], br.at[edge_at], b_s.at[1])

    def edge_blocks(count):
        blocks = bst.at[pl.ds(0, count)]
        return remote(blocks, blocks, b_s.at[0], b_r.at[0], mate)

    launch(0, INV)

    @pl.when(is_first)
    def _():
        for h in range(helpers):
            lend(h).start()
        for u in range(KEPT):
            keep_unit(u).wait()
            spread_unit(u)

    pl.when(is_later & ~is_helper)(lambda: launch(0, COUP))

    @pl.when(is_sender)
    def _():
        read_done(BND)
        for j in range(n):
            for q in range(fold):
                bst[j, :, q * rows : (q + 1) * rows] = bnd[
                    q * part : (q + 1) * part, j * rows : (j + 1) * rows
                ]
        own_edge.start()
        for d in range(1, n):
            edge_block(d).start()

    read_done(MERGE)
    read_done(SLOT)
    m_hi, m_lo = halves(mv[...])
    place = (
        lax.broadcasted_iota(jnp.int32, (edges, edges), 0) == slot[...]
    ).astype(jnp.float32).astype(jnp.bfloat16)
    first = (dot_t(m_hi, place).astype(jnp.bfloat16), dot_t(m_lo, place).astype(jnp.bfloat16))

    def flux(which):
        acc = None
        for k in range(DEPTH_CHUNKS):
            if which == 0:
                read_done(LEAF + k)
            read_done(SRC + which * DEPTH_CHUNKS + k)
            cols = slice(k * kd, (k + 1) * kd)
            part = dot_t(sv[which * total // 2 : (which + 1) * total // 2, cols], lv[:, cols])
            acc = part if acc is None else acc + part
        return acc

    offset = 0
    place_of = []
    for level in range(levels):
        half = total >> (level + 1)
        pieces = 2 if level < levels - 1 else 1
        place_of.append((offset, half // pieces, pieces))
        offset += half

    def give(level, y):
        start, size, pieces = place_of[level]
        lsend[start : start + size * pieces, :] = y
        copies = []
        for c in range(pieces):
            at = pl.ds(start + c * size, size)
            copy = remote(
                lsend.at[at, :], lrecv.at[at, :], lev_s.at[0], lev_r.at[level, c], peer(level)
            )
            copies.append(copy)
            if level == 0:
                pl.when(~is_helper)(copy.start)
            else:
                copy.start()
        return copies

    def got(level, c):
        start, size, _ = place_of[level]
        return lrecv[start + c * size : start + (c + 1) * size, :]

    copies = give(0, dot3(flux(0), *first))
    keep = dot3(flux(1), *first)
    read_done(LIFT)
    lift_split[0], lift_split[1] = halves(ltv[...])
    for i in range(2):
        read_done(OWN + i)

    @pl.when(is_helper)
    def _():
        lend(0).wait_recv()
        spread_unit(0)
        for copy in copies:
            copy.start()

    def takes(t):
        take(t, INV)
        if t < chips - 2:
            pl.when(is_later & ~is_helper)(lambda: take(t, COUP))

        if t > 0:
            pl.when(is_helper)(lambda: take(t - 1, COUP))
            return

        @pl.when(is_helper)
        def _():
            launch(0, COUP)
            share_unit(0)

    def share_kept():
        for u in range(KEPT):
            share_unit(u)

    def keep_first():
        pl.when(~(middle & relayed))(share_kept)
        edges_here(KEPT)
        for u in range(KEPT):
            all_shares(LENT + u).wait_recv()
        for r in range(0, points, block):
            cz[:, r : r + block] = sum(edge_term(u, r) for u in range(KEPT))

    def help_first():
        edges_here(1)
        all_shares(LENT).wait_recv()
        for r in range(0, points, block):
            dst[:, r : r + block] = edge_term(0, r)
        answer(slab - helper0).start()

    taken = 0
    for level in range(levels):
        size = place_of[level][1]
        if taken < chips - 1:
            takes(taken)
            if taken == 0:
                pl.when(relayed & middle)(share_kept)
            taken += 1
        if level == 0:
            pl.when(is_helper)(help_first)
        copies[0].wait_recv()
        x = keep[:size] + got(level, 0)
        if level < levels - 1:
            later = give(level + 1, dot3(x, m_hi, m_lo))
            copies[1].wait_recv()
            keep = dot3(keep[size:] + got(level, 1), m_hi, m_lo)
            if level == levels - 2:
                pl.when(is_first)(keep_first)
            copies = later
    load = dot3(x, lift_split[0], lift_split[1])

    for t in range(taken, chips - 1):
        takes(t)

    def prepare(i):
        for r in range(0, points, block):
            hi, lo = halves(full[i, r : r + block, :])
            split[2 * i, r : r + block, :] = hi
            split[2 * i + 1, r : r + block, :] = lo

    def times(x, i):
        if split_ahead:
            return dot3(x, split[2 * i], split[2 * i + 1])
        return jnp.concatenate(
            [dot3(x, *halves(full[i, r : r + block, :])) for r in range(0, points, block)], axis=1
        )

    all_shares(INV).wait_recv()
    if split_ahead:
        prepare(INV)

    @pl.when(is_first)
    def _():
        cz[...] = load - cz[...]
        for h in range(helpers):
            answer(h).wait_recv()
            cz[...] = cz[...] - dv[h]

    @pl.when(is_later)
    def _():
        cz[...] = times(load, INV) if split_ahead else load
        take(chips - 2, COUP)
        all_shares(COUP).wait_recv()
        if split_ahead:
            prepare(COUP)
            for r in range(0, points, block):
                at = slice(r, r + block)
                joint = product3(
                    split[2 * INV, at, :], split[2 * INV + 1, at, :],
                    split[2 * COUP], split[2 * COUP + 1],
                )
                split[4, at, :], split[5, at, :] = halves(joint)

    chunks = max(1, min(CHAIN_CHUNKS, rows // 16))
    size = rows // chunks

    def hop(c):
        at = pl.ds(c * size, size)
        return remote(
            st.at[at, :], pv.at[at, :], ch_s.at[0], ch_r.at[c],
            lax.rem(slab + 1, n_slab), "slab",
        )

    def hand_out(p):
        turned = st[p * out_rows : (p + 1) * out_rows, :].T
        for j in range(n):
            for q in range(out_fold):
                at = j * width + q * out_part
                ob[p, j, :, q * out_rows : (q + 1) * out_rows] = turned[at : at + out_part]
        for mask in [m ^ 1 for m in range(n - 1, 1, -1)] + [1]:
            to = flip(mask)
            remote(ob.at[p, to], rb.at[p, me], o_s.at[p], o_r.at[p], to).start()
        own(p).start()

    def own(p):
        return pltpu.make_async_copy(ob.at[p, me], rb.at[p, me], o_s.at[parts + p])

    def out_rest(p):
        some = pl.ds(0, n - 1)
        return remote(ob.at[p, some], rb.at[p, some], o_s.at[p], o_r.at[p], mate)

    all_hops = remote(st, pv, ch_s.at[0], ch_r.at[0], lax.rem(slab + 1, n_slab), "slab")
    for c in range(chunks):
        at = slice(c * size, (c + 1) * size)

        @pl.when(is_first)
        def _():
            st[at, :] = times(cz[at, :], INV)

        @pl.when(is_later)
        def _():
            hop(c).wait_recv()
            if split_ahead:
                st[at, :] = cz[at, :] - times(pv[at, :], 2)
            else:
                st[at, :] = times(cz[at, :] - times(pv[at, :], COUP), INV)

        pl.when(slab < n_slab - 1)(hop(c).start)
        done, odd = divmod((c + 1) * size, out_rows)
        if not odd and done < parts:
            pl.when(slab == n_slab - 1)(functools.partial(hand_out, done - 1))

    for p in range(parts - 1):
        pl.when(slab < n_slab - 1)(functools.partial(hand_out, p))
    hand_out(parts - 1)

    exchanged = lsend.at[pl.ds(0, offset), :]
    remote(exchanged, exchanged, lev_s.at[0], lev_r.at[0, 0], mate).wait_send()
    all_sent(INV)
    pl.when(is_later)(lambda: all_sent(COUP))

    @pl.when(is_first)
    def _():
        lend_all().wait_send()
        for u in range(KEPT):
            unit_sent(u)


    @pl.when(is_helper)
    def _():
        unit_sent(0)
        answer(0).wait_send()

    pl.when(is_sender)(lambda: edge_blocks(n - 1).wait_send())
    pl.when(slab < n_slab - 1)(all_hops.wait_send)
    for p in range(parts):
        own(p).wait()
        out_rest(p).wait_recv()
        for j in range(n):
            for q in range(out_fold):
                at = j * rows + p * out_rows
                out[q * out_part : (q + 1) * out_part, at : at + out_rows] = rb[
                    p, j, :, q * out_rows : (q + 1) * out_rows
                ]
    for p in range(parts):
        out_rest(p).wait_send()


def on_device(sources, leaf_ops, edge_slot, merge_ops, lift_ops, coupling, inverse, boundary):
    n, n_slab = lax.axis_size("box"), lax.axis_size("slab")
    total, depth = sources.shape[2:]
    edges = leaf_ops.shape[2]
    points = lift_ops.shape[2]
    rows, width = total // n, points // n
    chips, levels = n // 2, n.bit_length() - 1
    split_ahead = points * points <= 2**20
    f32, bf16 = jnp.float32, jnp.bfloat16
    hbm = pl.BlockSpec(memory_space=pl.ANY)
    dma = lambda *s: pltpu.SemaphoreType.DMA(s)
    vmem = pl.BlockSpec(memory_space=pltpu.VMEM)
    fold = st_fold(rows)
    parts = OUT_PARTS if rows >= 32 else 1
    out_fold = st_fold(rows // parts)
    helpers = min(HELPERS, n_slab - 1)
    units = KEPT + helpers
    result = pl.pallas_call(
        functools.partial(kernel, n, n_slab, split_ahead),
        out_shape=pltpu.VMEM((width, total), f32),
        in_specs=[hbm] * 8,
        out_specs=vmem,
        scratch_shapes=[
            pltpu.VMEM((total, depth), bf16),
            pltpu.VMEM((edges, depth), bf16),
            pltpu.VMEM((edges, edges), f32),
            pltpu.VMEM((points, edges), f32),
            pltpu.VMEM((1, edges), jnp.int32),
            pltpu.VMEM((width, total), f32),
            pltpu.VMEM((2, points, points), f32),
            pltpu.VMEM((KEPT, points, points // units), f32),
            pltpu.VMEM((6, points, points) if split_ahead else (6, 16, 128), bf16),
            pltpu.VMEM((2, points, edges), bf16),
            pltpu.VMEM((total, edges), f32),
            pltpu.VMEM((total, edges), f32),
            pltpu.VMEM((n, width // fold, rows * fold), f32),
            pltpu.VMEM((KEPT * n // units, width // fold, rows * fold), f32),
            pltpu.VMEM((KEPT * points // units, rows), f32),
            pltpu.VMEM((rows, points), f32),
            pltpu.VMEM((helpers, rows, points), f32),
            pltpu.VMEM((rows, points), f32),
            pltpu.VMEM((rows, points), f32),
            pltpu.VMEM((rows, points), f32),
            pltpu.VMEM((parts, n, width // out_fold, rows // parts * out_fold), f32),
            pltpu.VMEM((parts, n, width // out_fold, rows // parts * out_fold), f32),
            dma(3 * DEPTH_CHUNKS + 6),
            dma(1), dma(levels, 2),
            dma(2, chips + 1), dma(2, chips),
            dma(2 + KEPT), dma(2 + KEPT),
            dma(1), dma(CHAIN_CHUNKS),
            dma(2 * parts), dma(parts), dma(2), dma(1), dma(2 + 2 * KEPT), dma(1 + helpers + KEPT),
        ],
        compiler_params=pltpu.CompilerParams(collective_id=0, has_side_effects=True),
        name="slab_solve",
    )(
        sources[0, 0], leaf_ops[0, 0], edge_slot[0], merge_ops[0, 0], lift_ops[0, 0],
        coupling[0], inverse[0], boundary.T,
    )
    return result.T[None]


def solution(mesh):
    return jax.shard_map(
        on_device,
        mesh=mesh,
        in_specs=(
            P("slab", "box", None, None),
            P("slab", "box", None, None),
            P("slab", "box", None),
            P("slab", "box", None, None),
            P("slab", "box", None, None),
            P("slab", "box", None),
            P("slab", "box", None),
            P(None, "box"),
        ),
        out_specs=P("slab", None, "box"),
        check_vma=False,
    )
```

```python
import functools

import jax
import jax.numpy as jnp
from jax import lax
from jax.experimental import pallas as pl
from jax.experimental.pallas import tpu as pltpu
from jax.sharding import PartitionSpec as P

MESH = pl.DeviceIdType.MESH
contract_last = (((1,), (1,)), ((), ()))
DEPTH_CHUNKS = 1
CHAIN_CHUNKS = 4
HELPERS = 2
KEPT = 2
OUT_PARTS = 2
COUP, INV, LENT = 0, 1, 2


def dot_t(a, b):
    return lax.dot_general(a, b, contract_last, preferred_element_type=jnp.float32)


def st_fold(rows):
    return max(1, 128 // rows)


def halves(x):
    hi = x.astype(jnp.bfloat16)
    return hi, (x - hi.astype(jnp.float32)).astype(jnp.bfloat16)


def product3(a_hi, a_lo, b_hi, b_lo):
    mm = functools.partial(jnp.dot, preferred_element_type=jnp.float32)
    return mm(a_hi, b_hi) + (mm(a_hi, b_lo) + mm(a_lo, b_hi))


def dot3(x, w_hi, w_lo):
    hi, lo = halves(x)
    if x.shape[0] <= 64:
        both = dot_t(jnp.concatenate([hi, lo], axis=0), w_hi)
        return both[: x.shape[0]] + (dot_t(hi, w_lo) + both[x.shape[0] :])
    return dot_t(hi, w_hi) + (dot_t(hi, w_lo) + dot_t(lo, w_hi))


def kernel(
    n, n_slab, split_ahead,
    src, leaf, slot_in, merge, lift, coup, inv, bnd_in, out,
    sv, lv, mv, ltv, slot, bnd, full, lent, split, lift_split, lsend, lrecv,
    bst, br, bv, dst, dv, pv, st, cz, ob, rb,
    loc, lev_s, lev_r, g_s, g_r, p_s, p_r, ch_s, ch_r, o_s, o_r, b_s, b_r, x_s, x_r,
):
    me, slab = lax.axis_index("box"), lax.axis_index("slab")
    chips = n // 2
    skip_ends = chips == 4
    chip = me // 2
    core = me - 2 * chip
    mate = me + 1 - 2 * core
    rows, points = pv.shape
    width = points // n
    total, edges = lsend.shape
    depth = lv.shape[1]
    kd = depth // DEPTH_CHUNKS
    levels = n.bit_length() - 1
    block = min(points, 256)
    depth_lent = lent.shape[2]
    units = points // depth_lent
    helpers = units - KEPT
    helping = n // units
    helper0 = n_slab - helpers
    is_helper = slab >= helper0
    is_first = slab == 0
    kept = (0, units - 1)
    my_unit = me // helping
    is_sender = (is_first & ((my_unit == kept[0]) | (my_unit == kept[1]))) | (
        is_helper & (my_unit == helpers - slab + helper0)
    )
    edge_at = lax.rem(me, helping) + jnp.where(is_first & (my_unit == kept[1]), helping, 0)
    is_later = slab > 0
    fold = st_fold(rows)
    part = width // fold
    parts, _, out_part, _ = ob.shape
    out_rows = rows // parts
    out_fold = width // out_part

    leaping = is_first

    def flip(mask):
        to = me
        for q in range(levels):
            if (mask >> q) & 1:
                to = to + 2**q - 2 ** (q + 1) * lax.rem(me // 2**q, 2)
        return to

    def peer(level):
        mask = 2 ** (levels - 1 - level)
        return me + mask - 2 * mask * lax.rem(me // mask, 2)

    def block_of(position):
        block = 0
        for q in range(levels):
            bit = lax.rem(me // 2**q, 2)
            block = block + 2**q * (bit if (position >> q) & 1 else 1 - bit)
        return block

    def read(k, pairs):
        copies = [pltpu.make_async_copy(a, b, loc.at[k]) for a, b in pairs]
        for c in copies:
            c.start()

    def rows_of(who):
        return pl.ds(pl.multiple_of(who * rows, rows), rows)

    def points_at(i, at):
        return lent.at[i - LENT, at, :] if i >= LENT else full.at[i, at, :]

    def shard_at(i, owner):
        return points_at(i, pl.ds(pl.multiple_of(owner * width, width), width))

    def src_part(which, k):
        return sv.at[pl.ds(which * total // 2, total // 2), pl.ds(k * kd, kd)]

    def leaf_part(k):
        return lv.at[:, pl.ds(k * kd, kd)]

    SLOT, MERGE, LIFT, OWN, BND, SRC = 0, 1, 2, 3, 5, 6
    LEAF = SRC + 2 * DEPTH_CHUNKS
    arrays = {SLOT: slot, MERGE: mv, LIFT: ltv, OWN: shard_at(0, me), OWN + 1: shard_at(1, me), BND: bnd}
    for k in range(DEPTH_CHUNKS):
        arrays[LEAF + k] = leaf_part(k)
        for which in range(2):
            arrays[SRC + which * DEPTH_CHUNKS + k] = src_part(which, k)

    def read_done(k):
        pltpu.make_async_copy(arrays[k], arrays[k], loc.at[k]).wait()

    barrier = pltpu.get_barrier_semaphore()
    for d in range(1, n):
        pl.semaphore_signal(
            barrier, inc=1, device_id={"box": lax.rem(me + d, n)}, device_id_type=MESH
        )
    for d in range(1, n_slab):
        pl.semaphore_signal(
            barrier, inc=1, device_id={"slab": lax.rem(slab + d, n_slab)}, device_id_type=MESH
        )

    pl.when(is_sender)(lambda: read(BND, [(bnd_in, bnd)]))
    read(SLOT, [(slot_in, slot)])
    read(MERGE, [(merge, mv)])
    for which in range(2):
        for k in range(DEPTH_CHUNKS):
            cols = pl.ds(k * kd, kd)
            if which == 0:
                read(LEAF + k, [(leaf.at[:, cols], lv.at[:, cols])])
            read(SRC + which * DEPTH_CHUNKS + k, [
                (src.at[rows_of(block_of(p)), cols], sv.at[pl.ds(p * rows, rows), cols])
                for p in range(which * n // 2, (which + 1) * n // 2)
            ])
    read(LIFT, [(lift, ltv)])
    for i, m in enumerate((coup, inv)):
        read(OWN + i, [(m, shard_at(i, me))])

    def unit_columns(k):
        return pl.ds(k * depth_lent, depth_lent)

    def keep_unit(k):
        return pltpu.make_async_copy(
            coup.at[:, unit_columns(kept[k])], shard_at(LENT + k, me), x_s.at[2 + KEPT + k]
        )

    @pl.when(is_first)
    def _():
        for u in range(KEPT):
            keep_unit(u).start()

    pl.semaphore_wait(barrier, n + n_slab - 2)

    def remote(a, b, s, r, to, axis="box"):
        return pltpu.make_async_remote_copy(
            src_ref=a, dst_ref=b, send_sem=s, recv_sem=r,
            device_id={axis: to}, device_id_type=MESH,
        )

    def line(direction, t, i):
        step = 1 if direction == 0 else -1
        owner = me - 2 * step * t
        ok_chip = chip - step * t
        to_chip = chip + step
        a = (coup, inv)[i] if t == 0 else shard_at(i, owner)
        ok = (ok_chip >= 0) & (ok_chip < chips) & (to_chip >= 0) & (to_chip < chips)
        if skip_ends and t == 1:
            ok = ok & (~leaping | ((ok_chip > 0) & (ok_chip < chips - 1)))
        return ok, remote(
            a, shard_at(i, owner), g_s.at[i, ok_chip + direction], g_r.at[i, ok_chip], me + 2 * step
        )

    def leap(i):
        inward = jnp.where(chip == 0, 2, -2)
        return remote(
            (coup, inv)[i], shard_at(i, me), g_s.at[i, jnp.where(chip == 0, 1, chips - 1)],
            g_r.at[i, chip], me + 2 * inward,
        )

    at_end = leaping & ((chip == 0) | (chip == chips - 1))

    def arrival(direction, t, i):
        step = 1 if direction == 0 else -1
        ref = shard_at(i, me - 2 * step * (t + 1))
        return remote(
            ref, ref, g_s.at[i, chip], g_r.at[i, chip - step * (t + 1)], me - 2 * step
        )

    def came(direction, t):
        owner_chip = chip - (t + 1 if direction == 0 else -t - 1)
        return (owner_chip >= 0) & (owner_chip < chips)

    def share(direction, t, i):
        step = 1 if direction == 0 else -1
        owner = me - 2 * step * (t + 1)
        a = (coup, inv)[i] if t < 0 else shard_at(i, owner)
        return remote(a, shard_at(i, owner), p_s.at[i], p_r.at[i], mate)

    def all_shares(i):
        half = points_at(i, pl.ds(0, points // 2))
        return remote(half, half, p_s.at[i], p_r.at[i], mate)

    def launch(t, i):
        if t == 0:
            share(0, -1, i).start()
        for direction in range(2):
            ok, copy = line(direction, t, i)
            pl.when(ok)(copy.start)

    def take(t, i):
        if t == 0 and skip_ends:
            pl.when(at_end)(leap(i).start)
        for direction in range(2):
            pl.when(came(direction, t))(arrival(direction, t, i).wait_recv)
        if t + 1 < chips - 1:
            launch(t + 1, i)
        for direction in range(2):
            pl.when(came(direction, t))(share(direction, t, i).start)

    def all_here(i):
        all_shares(i).wait_recv()

    def all_sent(i):
        all_shares(i).wait_send()
        if skip_ends:
            pl.when(at_end)(leap(i).wait_send)
        for t in range(chips - 1):
            for direction in range(2):
                ok, copy = line(direction, t, i)
                pl.when(ok)(copy.wait_send)

    def lend(h):
        return remote(
            coup.at[:, unit_columns(helpers - h)], shard_at(LENT, me),
            x_s.at[0], x_r.at[0], helper0 + h, "slab",
        )

    def lend_all():
        columns = pl.ds(depth_lent, helpers * depth_lent)
        lent_columns = coup.at[:, columns]
        here = full.at[COUP, pl.ds(0, width), columns]
        return remote(lent_columns, here, x_s.at[0], x_r.at[0], helper0, "slab")

    def answer(h):
        return remote(dst, dv.at[h], x_s.at[1], x_r.at[1 + h], 0, "slab")

    def spread(u, owner, to):
        shard = shard_at(LENT + u, owner)
        return remote(shard, shard, x_s.at[2 + u], x_r.at[1 + helpers + u], to)

    def spread_rows(u, count):
        some = points_at(LENT + u, pl.ds(0, count * width))
        return remote(some, some, x_s.at[2 + u], x_r.at[1 + helpers + u], mate)

    relayed = is_first & skip_ends
    middle = (chip > 0) & (chip < chips - 1)
    pair = me + 2 - 4 * lax.rem(chip, 2)
    low = chip < chips // 2
    across = me + 2 * (jnp.where(low, chips // 2, chips // 2 - 1) - chip)
    other_half = me + 2 * (jnp.where(low, chips // 2, 0) - chip)

    def lent_share(u, k):
        same = shard_at(LENT + u, lax.rem(me + 2 * k, n))
        return remote(same, same, p_s.at[LENT + u], p_r.at[LENT + u], mate)

    def spread_unit(u):
        lent_share(u, 0).start()

        @pl.when(relayed)
        def _():
            spread(u, me, across).start()
            spread(u, me, pair).start()

        @pl.when(~relayed)
        def _():
            for k in range(1, chips):
                spread(u, me, lax.rem(me + 2 * k, n)).start()

    def share_unit(u):
        spread_rows(u, chips - 1).wait_recv()
        @pl.when(relayed & middle)
        def _():
            for k in range(chips // 2):
                spread(u, other_half + 2 * k, pair).start()

        for k in range(1, chips):
            lent_share(u, k).start()

    def unit_sent(u):
        all_shares(LENT + u).wait_send()
        pl.when(relayed & middle)(lambda: spread_rows(u, chips).wait_send())
        pl.when(relayed & ~middle)(lambda: spread_rows(u, chips // 2).wait_send())
        pl.when(~relayed)(lambda: spread_rows(u, chips - 1).wait_send())

    def edges_here(count):
        @pl.when(is_sender)
        def _():
            own_edge.wait()
            edge_blocks(count * helping - 1).wait_recv()

        @pl.when(~is_sender)
        def _():
            edge_blocks(count * helping).wait_recv()

        for j in range(count * helping):
            for q in range(fold):
                at = j * width + q * part
                bv[at : at + part, :] = br[j, :, q * rows : (q + 1) * rows]

    def edge_term(u, r):
        edge = bv[u * depth_lent : (u + 1) * depth_lent, :].T
        return dot3(edge, *halves(lent[u, r : r + block, :]))

    def edge_block(d):
        to = lax.rem(me + d, n)
        return remote(bst.at[to], br.at[edge_at], b_s.at[0], b_r.at[0], to)

    own_edge = pltpu.make_async_copy(bst.at[me], br.at[edge_at], b_s.at[1])

    def edge_blocks(count):
        blocks = bst.at[pl.ds(0, count)]
        return remote(blocks, blocks, b_s.at[0], b_r.at[0], mate)

    launch(0, INV)

    @pl.when(is_first)
    def _():
        for h in range(helpers):
            lend(h).start()
        for u in range(KEPT):
            keep_unit(u).wait()
            spread_unit(u)

    pl.when(is_later & ~is_helper)(lambda: launch(0, COUP))

    @pl.when(is_sender)
    def _():
        read_done(BND)
        for j in range(n):
            for q in range(fold):
                bst[j, :, q * rows : (q + 1) * rows] = bnd[
                    q * part : (q + 1) * part, j * rows : (j + 1) * rows
                ]
        own_edge.start()
        for d in range(1, n):
            edge_block(d).start()

    read_done(MERGE)
    read_done(SLOT)
    m_hi, m_lo = halves(mv[...])
    place = (
        lax.broadcasted_iota(jnp.int32, (edges, edges), 0) == slot[...]
    ).astype(jnp.float32).astype(jnp.bfloat16)
    first = (dot_t(m_hi, place).astype(jnp.bfloat16), dot_t(m_lo, place).astype(jnp.bfloat16))

    def flux(which):
        acc = None
        for k in range(DEPTH_CHUNKS):
            if which == 0:
                read_done(LEAF + k)
            read_done(SRC + which * DEPTH_CHUNKS + k)
            cols = slice(k * kd, (k + 1) * kd)
            part = dot_t(sv[which * total // 2 : (which + 1) * total // 2, cols], lv[:, cols])
            acc = part if acc is None else acc + part
        return acc

    offset = 0
    place_of = []
    for level in range(levels):
        half = total >> (level + 1)
        pieces = 2 if level < levels - 1 else 1
        place_of.append((offset, half // pieces, pieces))
        offset += half

    def give(level, y):
        start, size, pieces = place_of[level]
        lsend[start : start + size * pieces, :] = y
        copies = []
        for c in range(pieces):
            at = pl.ds(start + c * size, size)
            copy = remote(
                lsend.at[at, :], lrecv.at[at, :], lev_s.at[0], lev_r.at[level, c], peer(level)
            )
            copies.append(copy)
            if level == 0:
                pl.when(~is_helper)(copy.start)
            else:
                copy.start()
        return copies

    def got(level, c):
        start, size, _ = place_of[level]
        return lrecv[start + c * size : start + (c + 1) * size, :]

    copies = give(0, dot3(flux(0), *first))
    keep = dot3(flux(1), *first)
    read_done(LIFT)
    lift_split[0], lift_split[1] = halves(ltv[...])
    for i in range(2):
        read_done(OWN + i)

    @pl.when(is_helper)
    def _():
        lend(0).wait_recv()
        spread_unit(0)
        for copy in copies:
            copy.start()

    def takes(t):
        take(t, INV)
        if t < chips - 2:
            pl.when(is_later & ~is_helper)(lambda: take(t, COUP))

        if t > 0:
            pl.when(is_helper)(lambda: take(t - 1, COUP))
            return

        @pl.when(is_helper)
        def _():
            launch(0, COUP)
            share_unit(0)

    def share_kept():
        for u in range(KEPT):
            share_unit(u)

    def kept_term():
        edges_here(KEPT)
        for u in range(KEPT):
            all_shares(LENT + u).wait_recv()
        for r in range(0, points, block):
            cz[:, r : r + block] = sum(edge_term(u, r) for u in range(KEPT))

    def keep_first():
        share_kept()
        kept_term()

    def help_first():
        edges_here(1)
        all_shares(LENT).wait_recv()
        for r in range(0, points, block):
            dst[:, r : r + block] = edge_term(0, r)
        answer(slab - helper0).start()

    taken = 0
    for level in range(levels):
        size = place_of[level][1]
        if taken < chips - 1:
            takes(taken)
            if taken == 0:
                pl.when(relayed & middle)(share_kept)
            taken += 1
        if level == 0:
            pl.when(is_helper)(help_first)
        if level == 1:
            pl.when(relayed & middle)(kept_term)
        copies[0].wait_recv()
        x = keep[:size] + got(level, 0)
        if level < levels - 1:
            later = give(level + 1, dot3(x, m_hi, m_lo))
            copies[1].wait_recv()
            keep = dot3(keep[size:] + got(level, 1), m_hi, m_lo)
            if level == levels - 2:
                pl.when(is_first & ~(middle & relayed))(keep_first)
            copies = later
    load = dot3(x, lift_split[0], lift_split[1])

    for t in range(taken, chips - 1):
        takes(t)

    def prepare(i):
        for r in range(0, points, block):
            hi, lo = halves(full[i, r : r + block, :])
            split[2 * i, r : r + block, :] = hi
            split[2 * i + 1, r : r + block, :] = lo

    def times(x, i):
        if split_ahead:
            return dot3(x, split[2 * i], split[2 * i + 1])
        return jnp.concatenate(
            [dot3(x, *halves(full[i, r : r + block, :])) for r in range(0, points, block)], axis=1
        )

    all_shares(INV).wait_recv()
    if split_ahead:
        prepare(INV)

    @pl.when(is_first)
    def _():
        cz[...] = load - cz[...]
        for h in range(helpers):
            answer(h).wait_recv()
            cz[...] = cz[...] - dv[h]

    @pl.when(is_later)
    def _():
        cz[...] = times(load, INV) if split_ahead else load
        take(chips - 2, COUP)
        all_shares(COUP).wait_recv()
        if split_ahead:
            prepare(COUP)
            for r in range(0, points, block):
                at = slice(r, r + block)
                joint = product3(
                    split[2 * INV, at, :], split[2 * INV + 1, at, :],
                    split[2 * COUP], split[2 * COUP + 1],
                )
                split[4, at, :], split[5, at, :] = halves(joint)

    chunks = max(1, min(CHAIN_CHUNKS, rows // 16))
    size = rows // chunks

    def hop(c):
        at = pl.ds(c * size, size)
        return remote(
            st.at[at, :], pv.at[at, :], ch_s.at[0], ch_r.at[c],
            lax.rem(slab + 1, n_slab), "slab",
        )

    def hand_out(p):
        turned = st[p * out_rows : (p + 1) * out_rows, :].T
        for j in range(n):
            for q in range(out_fold):
                at = j * width + q * out_part
                ob[p, j, :, q * out_rows : (q + 1) * out_rows] = turned[at : at + out_part]
        for k in range(n - 1):
            to = k + jnp.where(me <= k, 1, 0)
            remote(ob.at[p, to], rb.at[p, me], o_s.at[p], o_r.at[p], to).start()
        own(p).start()

    def own(p):
        return pltpu.make_async_copy(ob.at[p, me], rb.at[p, me], o_s.at[parts + p])

    def out_rest(p):
        some = pl.ds(0, n - 1)
        return remote(ob.at[p, some], rb.at[p, some], o_s.at[p], o_r.at[p], mate)

    all_hops = remote(st, pv, ch_s.at[0], ch_r.at[0], lax.rem(slab + 1, n_slab), "slab")
    for c in range(chunks):
        at = slice(c * size, (c + 1) * size)

        @pl.when(is_first)
        def _():
            st[at, :] = times(cz[at, :], INV)

        @pl.when(is_later)
        def _():
            hop(c).wait_recv()
            if split_ahead:
                st[at, :] = cz[at, :] - times(pv[at, :], 2)
            else:
                st[at, :] = times(cz[at, :] - times(pv[at, :], COUP), INV)

        pl.when(slab < n_slab - 1)(hop(c).start)
        done, odd = divmod((c + 1) * size, out_rows)
        if not odd and done < parts:
            pl.when(slab == n_slab - 1)(functools.partial(hand_out, done - 1))

    for p in range(parts - 1):
        pl.when(slab < n_slab - 1)(functools.partial(hand_out, p))
    hand_out(parts - 1)

    exchanged = lsend.at[pl.ds(0, offset), :]
    remote(exchanged, exchanged, lev_s.at[0], lev_r.at[0, 0], mate).wait_send()
    all_sent(INV)
    pl.when(is_later)(lambda: all_sent(COUP))

    @pl.when(is_first)
    def _():
        lend_all().wait_send()
        for u in range(KEPT):
            unit_sent(u)


    @pl.when(is_helper)
    def _():
        unit_sent(0)
        answer(0).wait_send()

    pl.when(is_sender)(lambda: edge_blocks(n - 1).wait_send())
    pl.when(slab < n_slab - 1)(all_hops.wait_send)
    for p in range(parts):
        own(p).wait()
        out_rest(p).wait_recv()
        for j in range(n):
            for q in range(out_fold):
                at = j * rows + p * out_rows
                out[q * out_part : (q + 1) * out_part, at : at + out_rows] = rb[
                    p, j, :, q * out_rows : (q + 1) * out_rows
                ]
    for p in range(parts):
        out_rest(p).wait_send()


def on_device(sources, leaf_ops, edge_slot, merge_ops, lift_ops, coupling, inverse, boundary):
    n, n_slab = lax.axis_size("box"), lax.axis_size("slab")
    total, depth = sources.shape[2:]
    edges = leaf_ops.shape[2]
    points = lift_ops.shape[2]
    rows, width = total // n, points // n
    chips, levels = n // 2, n.bit_length() - 1
    split_ahead = points * points <= 2**20
    f32, bf16 = jnp.float32, jnp.bfloat16
    hbm = pl.BlockSpec(memory_space=pl.ANY)
    dma = lambda *s: pltpu.SemaphoreType.DMA(s)
    vmem = pl.BlockSpec(memory_space=pltpu.VMEM)
    fold = st_fold(rows)
    parts = OUT_PARTS if rows >= 32 else 1
    out_fold = st_fold(rows // parts)
    helpers = min(HELPERS, n_slab - 1)
    units = KEPT + helpers
    result = pl.pallas_call(
        functools.partial(kernel, n, n_slab, split_ahead),
        out_shape=pltpu.VMEM((width, total), f32),
        in_specs=[hbm] * 8,
        out_specs=vmem,
        scratch_shapes=[
            pltpu.VMEM((total, depth), bf16),
            pltpu.VMEM((edges, depth), bf16),
            pltpu.VMEM((edges, edges), f32),
            pltpu.VMEM((points, edges), f32),
            pltpu.VMEM((1, edges), jnp.int32),
            pltpu.VMEM((width, total), f32),
            pltpu.VMEM((2, points, points), f32),
            pltpu.VMEM((KEPT, points, points // units), f32),
            pltpu.VMEM((6, points, points) if split_ahead else (6, 16, 128), bf16),
            pltpu.VMEM((2, points, edges), bf16),
            pltpu.VMEM((total, edges), f32),
            pltpu.VMEM((total, edges), f32),
            pltpu.VMEM((n, width // fold, rows * fold), f32),
            pltpu.VMEM((KEPT * n // units, width // fold, rows * fold), f32),
            pltpu.VMEM((KEPT * points // units, rows), f32),
            pltpu.VMEM((rows, points), f32),
            pltpu.VMEM((helpers, rows, points), f32),
            pltpu.VMEM((rows, points), f32),
            pltpu.VMEM((rows, points), f32),
            pltpu.VMEM((rows, points), f32),
            pltpu.VMEM((parts, n, width // out_fold, rows // parts * out_fold), f32),
            pltpu.VMEM((parts, n, width // out_fold, rows // parts * out_fold), f32),
            dma(3 * DEPTH_CHUNKS + 6),
            dma(1), dma(levels, 2),
            dma(2, chips + 1), dma(2, chips),
            dma(2 + KEPT), dma(2 + KEPT),
            dma(1), dma(CHAIN_CHUNKS),
            dma(2 * parts), dma(parts), dma(2), dma(1), dma(2 + 2 * KEPT), dma(1 + helpers + KEPT),
        ],
        compiler_params=pltpu.CompilerParams(collective_id=0, has_side_effects=True),
        name="slab_solve",
    )(
        sources[0, 0], leaf_ops[0, 0], edge_slot[0], merge_ops[0, 0], lift_ops[0, 0],
        coupling[0], inverse[0], boundary.T,
    )
    return result.T[None]


def solution(mesh):
    return jax.shard_map(
        on_device,
        mesh=mesh,
        in_specs=(
            P("slab", "box", None, None),
            P("slab", "box", None, None),
            P("slab", "box", None),
            P("slab", "box", None, None),
            P("slab", "box", None, None),
            P("slab", "box", None),
            P("slab", "box", None),
            P(None, "box"),
        ),
        out_specs=P("slab", None, "box"),
        check_vma=False,
    )
```
